32 devices in a mesh: chain: 8 (over y, x, core), cross: 4 (over z).
Axes of the slice: x: 2, y: 2, z: 4, core: 2. Of those that a mesh axis runs over, the one named last changes fastest.
Arguments:
- moments: float32 [20, 512, 1024], P(None, 'cross', 'chain'), as said below
- flags: int32 [512, 1024], P('cross', 'chain'), may hold values from 0 to 2
- shifts: int32 [512, 8], P('cross', 'chain'), may hold values from -48 to 48
- fraction: float32 [512], P('cross'), may hold values from 0.05 to 0.95
Outputs:
- remapped: float32 [20, 512, 1024], P(None, 'cross', 'chain')
- mass_coord: float32 [5, 512, 1024], P(None, 'cross', 'chain')
The draws below stay inside these ranges and needn't reach their ends.
Inputs may be any that keep to these rules, and one draw needn't show every extreme that they name: zeroth-order moments are positive.
All inputs are finite; a program needn't handle non-finite values.
Results may differ from the reference program's by a relative error of at most 0.000084.
Values sent between devices are 32-bit elements; how exact they have to be, the bound alone decides.
A program may use at most 128 MiB of HBM per device.

```python
import jax
import jax.numpy as jnp
from jax import lax

VARS = 5
MOMENTS = 4
BLOCK = 128
SHIFT_MAX = 48
NX = 1024
PENCILS = 512
NBLK = 8


def draw_moments(key, part):
    key_base, key_high = jax.random.split(jax.random.fold_in(key, 7))
    rise_x = 1.0 + 2.0 * jnp.arange(NX, dtype=jnp.float32) / NX
    rise_p = 1.0 + 2.0 * jnp.arange(PENCILS, dtype=jnp.float32) / PENCILS
    scale = rise_p[:, None] * rise_x[None, :]
    base = jax.random.uniform(key_base, (VARS, PENCILS, NX), jnp.float32, 0.15, 0.6)
    higher = jax.random.normal(key_high, (VARS, MOMENTS - 1, PENCILS, NX), jnp.float32)
    means = base * scale[None]
    coefficients = jnp.array([0.5, 0.25, 0.12], jnp.float32)[None, :, None, None]
    rest = higher * coefficients * means[:, None]
    whole = jnp.concatenate([means[:, None], rest], axis=1)
    return whole.reshape(VARS * MOMENTS, PENCILS, NX).astype(jnp.float32)


def plant(values, key, low, top_value):
    longest = values.shape.index(max(values.shape))
    spots = []
    for shift in (0, 1):
        where = [jax.random.randint(jax.random.fold_in(key, axis), (), 0, length) for axis, length in enumerate(values.shape)]
        where[longest] = (where[longest] + shift) % values.shape[longest]
        spots.append(tuple(where))
    return values.at[spots[0]].set(low).at[spots[1]].set(top_value)


def block_scale(own_key, dims, shards, least, top_value):
    factor_of = 1.0
    for dim, blocks in shards:
        draws = jax.random.uniform(jax.random.fold_in(jax.random.fold_in(own_key, 6), dim), (blocks,), jnp.float32, least / len(shards), top_value / len(shards))
        factor_of = factor_of * jnp.repeat(jnp.exp(draws), dims[dim] // blocks).reshape((-1,) + (1,) * (len(dims) - 1 - dim))
    return factor_of


def setup_inputs(seed: int = 0) -> dict:
    keys = jax.random.split(jax.random.key(seed), 5)
    return {
        "moments": draw_moments(jax.random.fold_in(keys[4], 71), 0),
        "flags": plant(jax.random.randint(keys[1], (PENCILS, NX), 0, 3), jax.random.fold_in(keys[1], 1), 0, 2).astype(jnp.int32),
        "shifts": plant(jax.random.randint(keys[2], (PENCILS, NBLK), 0 - SHIFT_MAX, SHIFT_MAX + 1), jax.random.fold_in(keys[2], 1), 0 - SHIFT_MAX, SHIFT_MAX).astype(jnp.int32),
        "fraction": jnp.clip(0.05 + 0.9 * jax.random.uniform(keys[3], (PENCILS,), jnp.float32) ** block_scale(keys[3], (PENCILS,), ((0, 4),), -0.2, 0.2), 0.05, 0.95),
    }


gauss_nodes = (-0.8611363115940526, -0.3399810435848563, 0.3399810435848563, 0.8611363115940526)
gauss_weights = (0.3478548451374538, 0.6521451548625461, 0.6521451548625461, 0.3478548451374538)


def legendre_values(point):
    return [jnp.ones_like(point), point, 0.5 * (3.0 * point * point - 1.0), 0.5 * (5.0 * point * point * point - 3.0 * point)]


def interval_matrix(low_end, high_end, offset):
    half = 0.5 * (high_end - low_end)
    middle = 0.5 * (high_end + low_end)
    entries = [[jnp.zeros_like(low_end) for source_order in range(4)] for target_order in range(4)]
    for node, weight in zip(gauss_nodes, gauss_weights):
        point = middle + half * node
        target = legendre_values(point)
        source = legendre_values(point + offset)
        for target_order in range(4):
            for source_order in range(4):
                entries[target_order][source_order] = entries[target_order][source_order] + weight * half * target[target_order] * source[source_order]
    return jnp.stack([jnp.stack([(target_order + 0.5) * entries[target_order][source_order] for source_order in range(4)]) for target_order in range(4)])


def remap_matrices(fraction):
    first = interval_matrix(-1.0 + 0.0 * fraction, 1.0 - 2.0 * fraction, 2.0 * fraction)
    second = interval_matrix(1.0 - 2.0 * fraction, 1.0 + 0.0 * fraction, 2.0 * fraction - 2.0)
    return first, second


def partial_weights(fraction):
    shifted = 2.0 * fraction - 1.0
    square = shifted * shifted
    return jnp.stack([fraction, fraction * fraction - fraction, 0.25 * (square * shifted - shifted), 0.5 * (0.5 * (1.25 * square * square - 1.5 * square) + 0.125)])


def keep_mask(flags):
    order = jnp.arange(4, dtype=jnp.int32)[:, None, None]
    keep = (order == 0) | ((order == 1) & (flags[None] <= 1)) | (flags[None] == 0)
    return keep.astype(jnp.float32)


def reference(moments, flags, shifts, fraction):
    halo_width = SHIFT_MAX + 1
    expanded = moments.reshape(VARS, MOMENTS, PENCILS, NX)
    limited = expanded * keep_mask(flags)[None]
    padded = jnp.pad(limited, ((0, 0), (0, 0), (0, 0), (halo_width, halo_width)))
    cell_shift = jnp.repeat(shifts, BLOCK, axis=1)
    source = (jnp.arange(NX, dtype=jnp.int32)[None, :] + cell_shift + halo_width).astype(jnp.int32)
    source_cells = jnp.take_along_axis(padded, source[None, None], axis=3)
    next_cells = jnp.take_along_axis(padded, (source + 1)[None, None], axis=3)
    first, second = remap_matrices(fraction)
    remapped = jnp.einsum("kmp,vmpc->vkpc", first, source_cells, precision=lax.Precision.HIGHEST)
    remapped = remapped + jnp.einsum("kmp,vmpc->vkpc", second, next_cells, precision=lax.Precision.HIGHEST)
    means = padded[:, 0]
    cum = jnp.cumsum(means, axis=-1) - means
    cum_at = jnp.take_along_axis(cum, source[None], axis=2)
    partial_value = jnp.einsum("vmpc,mp->vpc", source_cells, partial_weights(fraction), precision=lax.Precision.HIGHEST)
    grand_sum = jnp.sum(expanded[:, 0], axis=(1, 2))
    mass_coord = (cum_at + partial_value) / (grand_sum / PENCILS)[:, None, None]
    return remapped.reshape(VARS * MOMENTS, PENCILS, NX), mass_coord
```

```python
import functools

import jax
import numpy as np
import jax.numpy as jnp
from jax import lax
from jax.experimental import pallas as pl
from jax.experimental.pallas import tpu as pltpu
from jax.sharding import PartitionSpec as P

VARS = 5
MOMENTS = 4
BLOCK = 128
SHIFT_MAX = 48
ROWS = VARS * MOMENTS
STRIDE = SHIFT_MAX + 1
CHUNKS = -(-ROWS * STRIDE // BLOCK)
TILE = 8
GROUP = 2 * TILE
EARLY = 2
PAIRS = tuple((k, m) for k in range(1, MOMENTS) for m in range(k, MOMENTS))
COEFS = MOMENTS + 2 * len(PAIRS)
MESH = pl.DeviceIdType.MESH
HIGHEST = lax.Precision.HIGHEST

gauss_nodes = (-0.8611363115940526, -0.3399810435848563, 0.3399810435848563, 0.8611363115940526)
gauss_weights = (0.3478548451374538, 0.6521451548625461, 0.6521451548625461, 0.3478548451374538)


def segments(first, length):
    held = [[] for _ in range(CHUNKS)]
    for row in range(ROWS):
        start = first + STRIDE * row
        chunk, lane = divmod(start, BLOCK)
        held[chunk % CHUNKS].append((lane, row))
        if lane + length > BLOCK:
            held[(chunk + 1) % CHUNKS].append((0, row))
    return [sorted(chunk) for chunk in held]


AFTER_FIRST, AFTER_LENGTH = SHIFT_MAX, SHIFT_MAX + 1
BEFORE_FIRST, BEFORE_LENGTH = 0, SHIFT_MAX
AFTER = segments(AFTER_FIRST, AFTER_LENGTH)
BEFORE = segments(BEFORE_FIRST, BEFORE_LENGTH)


def places(row, first, length):
    chunk, lane = divmod(first + STRIDE * row, BLOCK)
    chunks = [chunk % CHUNKS]
    if lane + length > BLOCK:
        chunks.append((chunk + 1) % CHUNKS)
    return chunks, lane


def legendre_values(point):
    return [
        jnp.ones_like(point),
        point,
        0.5 * (3.0 * point * point - 1.0),
        0.5 * (5.0 * point * point * point - 3.0 * point),
    ]


def interval_integrals(low_end, high_end, offset):
    half = 0.5 * (high_end - low_end)
    middle = 0.5 * (high_end + low_end)
    entries = [jnp.zeros_like(low_end) for _ in PAIRS]
    for node, weight in zip(gauss_nodes, gauss_weights):
        point = middle + half * node
        target = legendre_values(point)
        source = legendre_values(point + offset)
        scaled = [weight * half * value for value in target]
        for index, (k, m) in enumerate(PAIRS):
            entries[index] = entries[index] + scaled[k] * source[m]
    return entries


def partial_weights(fraction):
    shifted = 2.0 * fraction - 1.0
    square = shifted * shifted
    return [
        fraction,
        fraction * fraction - fraction,
        0.25 * (square * shifted - shifted),
        0.5 * (0.5 * (1.25 * square * square - 1.5 * square) + 0.125),
    ]


def corner_relays(mesh):
    ring = np.moveaxis(mesh.devices, mesh.axis_names.index("chain"), 0).reshape(mesh.shape["chain"], -1)[:, 0]
    if any(getattr(device, "coords", None) is None for device in ring):
        return {}, {}
    spots = [tuple(device.coords) for device in ring]
    rightward, leftward = {}, {}
    if len({spot[0] for spot in spots}) == 2 and len({spot[1] for spot in spots}) == 2:
        for index in range(len(spots) - 1):
            low, high = spots[index], spots[index + 1]
            if low[0] != high[0] and low[1] != high[1]:
                for found, source, target, pick in (
                    (rightward, index, index + 1, max), (leftward, index + 1, index, min)
                ):
                    corner = (spots[source][0], spots[target][1])
                    at = [i for i, spot in enumerate(spots) if spot[:2] == corner]
                    if at:
                        found[source] = (pick(at), target)
    return rightward, leftward


def exact_dot(value, ones):
    high = value.astype(jnp.bfloat16)
    rest = value - high.astype(jnp.float32)
    middle = rest.astype(jnp.bfloat16)
    low = (rest - middle.astype(jnp.float32)).astype(jnp.bfloat16)
    return sum(jnp.dot(part, ones, preferred_element_type=jnp.float32) for part in (low, middle, high))


def kernel(
    chain, cross, relays,
    moments_in, flags_in, shifts_in, fraction_in,
    remapped, mass,
    moments, flags, shifts, fraction,
    to_left, to_right, from_left, from_right, relay,
    sums, parts, raw, coef, shift_of, base, beyond, triangle,
    left_send, left_recv, right_send, right_recv, relay_send, relay_recv,
    sum_send, sum_recv, part_send, part_recv, input_sem,
):
    pencils = moments.shape[1]
    groups = pencils // GROUP
    relayed = groups // 2
    me = lax.axis_index("chain")
    plane = lax.axis_index("cross")

    inputs = [
        pltpu.make_async_copy(source, target, input_sem.at[index])
        for index, (source, target) in enumerate(
            ((moments_in, moments), (flags_in, flags), (shifts_in, shifts), (fraction_in, fraction))
        )
    ]
    for copy in inputs:
        copy.start()

    barrier = pltpu.get_barrier_semaphore()
    for step in range(1, chain):
        peer = lax.rem(me + step, chain)
        pl.semaphore_signal(barrier, inc=1, device_id={"chain": peer}, device_id_type=MESH)
    for step in range(1, cross):
        peer = lax.rem(plane + step, cross)
        pl.semaphore_signal(barrier, inc=1, device_id={"cross": peer}, device_id_type=MESH)

    for copy in inputs:
        copy.wait()

    def leftward(group):
        return pltpu.make_async_remote_copy(
            src_ref=to_left.at[group], dst_ref=from_right.at[group],
            send_sem=left_send.at[group], recv_sem=left_recv.at[group],
            device_id={"chain": lax.rem(me + chain - 1, chain)}, device_id_type=MESH,
        )

    def rightward(group):
        return pltpu.make_async_remote_copy(
            src_ref=to_right.at[group], dst_ref=from_left.at[group],
            send_sem=right_send.at[group], recv_sem=right_recv.at[group],
            device_id={"chain": lax.rem(me + 1, chain)}, device_id_type=MESH,
        )

    has_left, has_right = me > 0, me < chain - 1

    sum_copies = [
        pltpu.make_async_remote_copy(
            src_ref=sums.at[me], dst_ref=sums.at[me],
            send_sem=sum_send.at[step], recv_sem=sum_recv.at[step],
            device_id={"chain": lax.rem(me + step, chain)}, device_id_type=MESH,
        )
        for step in range(1, chain)
    ]

    def send_sums():
        row_id = lax.broadcasted_iota(jnp.int32, (8, BLOCK), 0)
        total = jnp.zeros((8, pencils), jnp.float32)
        for var in range(VARS):
            pick = (row_id == var).astype(jnp.float32)
            total = total + lax.dot_general(
                pick, moments[MOMENTS * var], (((1,), (1,)), ((), ())),
                precision=HIGHEST, preferred_element_type=jnp.float32,
            )
        sums[me] = total
        for copy in sum_copies:
            copy.start()

    wide_lane = lax.broadcasted_iota(jnp.int32, (GROUP, BLOCK), 1)

    def pack(group):
        rows = pl.ds(pl.multiple_of(group * GROUP, GROUP), GROUP)
        flag = flags[rows, :]
        keep_linear, keep_full = flag <= 1, flag == 0
        rolled = []
        for row in range(ROWS):
            value = moments[row, rows, :]
            order = row % MOMENTS
            if order > 0:
                value = jnp.where(keep_linear if order == 1 else keep_full, value, 0.0)
                moments[row, rows, :] = value
            rolled.append(pltpu.roll(value, (STRIDE * row + SHIFT_MAX) % BLOCK, 1))
        for chunk in range(CHUNKS):
            for held, target in ((AFTER, to_left), (BEFORE, to_right)):
                value = rolled[held[chunk][0][1]]
                for start, row in held[chunk][1:]:
                    value = jnp.where(wide_lane >= start, rolled[row], value)
                target[group, chunk] = value

    right_relays, left_relays = relays

    def to_relay(group, source, send_sem, through):
        return pltpu.make_async_remote_copy(
            src_ref=source.at[group], dst_ref=relay.at[group],
            send_sem=send_sem.at[group], recv_sem=relay_recv.at[group],
            device_id={"chain": jnp.int32(through)}, device_id_type=MESH,
        )

    def onward(group, landing, recv_sem, target):
        return pltpu.make_async_remote_copy(
            src_ref=relay.at[group], dst_ref=landing.at[group],
            send_sem=relay_send.at[group], recv_sem=recv_sem.at[group],
            device_id={"chain": jnp.int32(target)}, device_id_type=MESH,
        )

    def send(group, direct, wanted, routes, source, send_sem):
        odd = lax.rem(jnp.int32(group), 2) == 1
        for start, (through, _) in routes.items():
            wanted = wanted & ((me != start) | jnp.logical_not(odd))

            @pl.when((me == start) & odd)
            def _():
                to_relay(group, source, send_sem, through).start()

        @pl.when(wanted)
        def _():
            direct(group).start()

    def send_both(group):
        send(group, leftward, has_left, left_relays, to_left, left_send)
        send(group, rightward, has_right, right_relays, to_right, right_send)

    def pack_and_send(group, carry):
        pack(group)
        send_both(group)
        return carry

    pack(0)
    pl.semaphore_wait(barrier, chain - 1 + cross - 1)
    send_both(0)
    lax.fori_loop(1, EARLY, pack_and_send, 0)
    send_sums()
    lax.fori_loop(EARLY, groups, pack_and_send, 0)

    @pl.when(me == 0)
    def _():
        from_left[...] = jnp.zeros_like(from_left)

    @pl.when(me == chain - 1)
    def _():
        from_right[...] = jnp.zeros_like(from_right)

    f = fraction[...]
    shift_row = shifts[...]
    first = interval_integrals(-1.0 + 0.0 * f, 1.0 - 2.0 * f, 2.0 * f)
    second = interval_integrals(1.0 - 2.0 * f, 1.0 + 0.0 * f, 2.0 * f - 2.0)
    raw[...] = jnp.zeros_like(raw)
    columns = partial_weights(f) + first + second + [shift_row.astype(jnp.float32)]
    for index, value in enumerate(columns):
        raw[index : index + 1, :] = value
    turned = jnp.transpose(raw[...])
    for index in range(COEFS):
        coef[index] = jnp.broadcast_to(turned[:, index : index + 1], (pencils, BLOCK))
    shift_of[...] = jnp.broadcast_to(turned[:, COEFS : COEFS + 1], (pencils, BLOCK)).astype(jnp.int32)

    source_cell = lax.broadcasted_iota(jnp.int32, (BLOCK, BLOCK), 0)
    target_cell = lax.broadcasted_iota(jnp.int32, (BLOCK, BLOCK), 1)
    before_cell = jnp.where(source_cell < target_cell, 1.0, 0.0)
    up_to_edge = jnp.where(
        source_cell < BLOCK // 2, before_cell, 1.0 - before_cell
    )
    triangle[...] = up_to_edge.astype(jnp.bfloat16)
    own_triangle = before_cell.astype(jnp.bfloat16)
    for var in range(VARS):
        base[var] = exact_dot(moments[MOMENTS * var], own_triangle)

    part_copies = [
        pltpu.make_async_remote_copy(
            src_ref=parts.at[plane], dst_ref=parts.at[plane],
            send_sem=part_send.at[step], recv_sem=part_recv.at[step],
            device_id={"cross": lax.rem(plane + step, cross)}, device_id_type=MESH,
        )
        for step in range(1, cross)
    ]

    def pass_on(group, at):
        for routes, source, send_sem, landing, recv_sem in (
            (right_relays, to_right, right_send, from_left, right_recv),
            (left_relays, to_left, left_send, from_right, left_recv),
        ):
            for through, target in routes.values():

                @pl.when((me == through) & at)
                def _():
                    to_relay(group, source, send_sem, through).wait_recv()
                    onward(group, landing, recv_sem, target).start()

    def reduce_chain():
        for copy in sum_copies:
            copy.wait_recv()
        before = jnp.zeros((8, pencils), jnp.float32)
        whole = jnp.zeros((8, pencils), jnp.float32)
        for index in range(chain):
            value = sums[index]
            before = before + jnp.where(index < me, value, 0.0)
            whole = whole + value
        parts[plane] = jnp.broadcast_to(jnp.sum(whole, axis=1, keepdims=True), (8, BLOCK))
        for copy in part_copies:
            copy.start()
        raw[0:8, :] = before
        raw[8:16, :] = before + jnp.where(shift_row >= 0, sums[me], 0.0)
        turned = jnp.transpose(raw[...])
        for var in range(VARS):
            base[var] = base[var] + turned[:, var : var + 1]
            beyond[var] = jnp.broadcast_to(turned[:, 8 + var : 9 + var], (pencils, BLOCK))

    reduce_chain()

    lane = lax.broadcasted_iota(jnp.int32, (TILE, BLOCK), 1)

    def remap(group, carry):
        pass_on(2 * group + 1, group < relayed)

        @pl.when(has_right)
        def _():
            leftward(group).wait_recv()

        @pl.when(has_left)
        def _():
            rightward(group).wait_recv()

        halos, places_of = [], []
        for tile in range(GROUP // TILE):
            rows = pl.ds(pl.multiple_of(group * GROUP + tile * TILE, TILE), TILE)
            inner = pl.ds(tile * TILE, TILE)
            shift = shift_of[rows, :]
            ahead = shift >= 0
            places_of.append((rows, shift, ahead))

            def halo_row(row):
                values = []
                for ref, first_lane, length in (
                    (from_right, AFTER_FIRST, AFTER_LENGTH),
                    (from_left, BEFORE_FIRST, BEFORE_LENGTH),
                ):
                    chunks, start = places(row, first_lane, length)
                    value = ref[group, chunks[0], inner, :]
                    if len(chunks) > 1:
                        value = jnp.where(lane >= start, value, ref[group, chunks[1], inner, :])
                    values.append(value)
                value = jnp.where(ahead, values[0], values[1])
                return pltpu.roll(value, (-(STRIDE * row + SHIFT_MAX)) % BLOCK, 1)

            halos.append([halo_row(row) for row in range(ROWS)])

        signed = []
        for (_, _, ahead), halo in zip(places_of, halos):
            for var in range(VARS):
                value = halo[MOMENTS * var]
                signed.append(jnp.where(
                    ahead,
                    jnp.where(lane < AFTER_LENGTH, value, 0.0),
                    jnp.where(lane >= BLOCK - BEFORE_LENGTH, -value, 0.0),
                ))
        crossed = exact_dot(jnp.concatenate(signed, axis=0), triangle[...])

        for tile, ((rows, shift, ahead), halo) in enumerate(zip(places_of, halos)):
            turn = shift & (BLOCK - 1)
            outside = jnp.where(ahead, lane - turn, turn - 1 - lane) < 0
            outside_next = jnp.where(ahead, lane - turn - 1, turn - lane) < 0
            at = (lane + turn) & (BLOCK - 1)
            weight = [coef[m, rows, :] for m in range(MOMENTS)]
            inside, across = {}, {}
            for index, (k, m) in enumerate(PAIRS):
                inside[k, m] = coef[MOMENTS + index, rows, :]
                across[k, m] = coef[MOMENTS + len(PAIRS) + index, rows, :]

            def settle(value):
                return jnp.take_along_axis(value, at, axis=1, mode="promise_in_bounds")

            for var in range(VARS):
                here, after = [], []
                for order in range(MOMENTS):
                    own = moments[MOMENTS * var + order, rows, :]
                    other = halo[MOMENTS * var + order]
                    here.append(jnp.where(outside, other, own))
                    after.append(pltpu.roll(jnp.where(outside_next, other, own), BLOCK - 1, 1))
                filled = weight[0] * here[0]
                filled_after = weight[0] * after[0]
                for m in range(1, MOMENTS):
                    filled = filled + weight[m] * here[m]
                    filled_after = filled_after + weight[m] * after[m]
                rise = after[0] - here[0]
                remapped[MOMENTS * var, rows, :] = settle(here[0] + (filled_after - filled))
                for k in range(1, MOMENTS):
                    value = inside[k, k] * here[k] + across[k, k] * after[k]
                    for m in range(1, MOMENTS):
                        if m == k:
                            continue
                        pair = (min(k, m), max(k, m))
                        term = inside[pair] * here[m] + across[pair] * after[m]
                        value = value - term if k > m and (k + m) % 2 else value + term
                    edge = (2.0 if k % 2 == 0 else -2.0) * (weight[k] * rise)
                    remapped[MOMENTS * var + k, rows, :] = settle((k + 0.5) * (value + edge))
                index = (tile * VARS + var) * TILE
                start = jnp.where(
                    outside, crossed[index : index + TILE] + beyond[var, rows, :], base[var, rows, :]
                )
                mass[var, rows, :] = settle(start + filled)
        return carry

    lax.fori_loop(0, groups, remap, 0)

    for copy in part_copies:
        copy.wait_recv()
    grand = parts[0]
    for index in range(1, cross):
        grand = grand + parts[index]
    mean = grand / float(pencils * cross)
    for var in range(VARS):
        mass[var] = mass[var] / mean[var : var + 1, :]

    for copy in sum_copies + part_copies:
        copy.wait_send()

    for routes, landing, recv_sem in (
        (right_relays, from_left, right_recv), (left_relays, from_right, left_recv)
    ):
        for through, target in routes.values():

            @pl.when(me == through)
            def _():
                for group in range(relayed):
                    onward(2 * group + 1, landing, recv_sem, target).wait_send()

    @pl.when(has_left)
    def _():
        for group in range(groups):
            leftward(group).wait_send()

    @pl.when(has_right)
    def _():
        for group in range(groups):
            rightward(group).wait_send()


def deliver(remapped, mass, remapped_out, mass_out, sem):
    copies = [
        pltpu.make_async_copy(remapped, remapped_out, sem.at[0]),
        pltpu.make_async_copy(mass, mass_out, sem.at[1]),
    ]
    for copy in copies:
        copy.start()
    for copy in copies:
        copy.wait()


def solution(mesh):
    chain, cross = mesh.shape["chain"], mesh.shape["cross"]
    relays = corner_relays(mesh)

    def shards(moments, flags, shifts, fraction):
        row_count, pencils, cells = moments.shape
        assert row_count == ROWS and cells == BLOCK and pencils == BLOCK
        groups = pencils // GROUP
        block = pltpu.VMEM((groups, CHUNKS, GROUP, BLOCK), jnp.float32)
        dma = pltpu.SemaphoreType.DMA
        results = (
            jax.ShapeDtypeStruct(moments.shape, jnp.float32),
            jax.ShapeDtypeStruct((VARS, pencils, cells), jnp.float32),
        )
        in_vmem = pl.BlockSpec(memory_space=pltpu.VMEM)
        in_hbm = pl.BlockSpec(memory_space=pltpu.HBM)
        ready = pl.pallas_call(
            functools.partial(kernel, chain, cross, relays),
            out_shape=results,
            in_specs=[in_hbm] * 4,
            out_specs=(in_vmem,) * 2,
            scratch_shapes=[
                pltpu.VMEM(moments.shape, jnp.float32),
                pltpu.VMEM(flags.shape, jnp.int32),
                pltpu.VMEM((1, pencils), jnp.int32),
                pltpu.VMEM((1, pencils), jnp.float32),
                block, block, block, block, block,
                pltpu.VMEM((chain, 8, pencils), jnp.float32),
                pltpu.VMEM((cross, 8, BLOCK), jnp.float32),
                pltpu.VMEM((BLOCK, pencils), jnp.float32),
                pltpu.VMEM((COEFS, pencils, BLOCK), jnp.float32),
                pltpu.VMEM((pencils, BLOCK), jnp.int32),
                pltpu.VMEM((VARS, pencils, BLOCK), jnp.float32),
                pltpu.VMEM((VARS, pencils, BLOCK), jnp.float32),
                pltpu.VMEM((BLOCK, BLOCK), jnp.bfloat16),
                dma((groups,)), dma((groups,)), dma((groups,)), dma((groups,)),
                dma((groups,)), dma((groups,)),
                dma((chain,)), dma((chain,)), dma((cross,)), dma((cross,)), dma((4,)),
            ],
            compiler_params=pltpu.CompilerParams(
                collective_id=0, has_side_effects=True, vmem_limit_bytes=32 << 20
            ),
        )(*(
            pltpu.with_memory_space_constraint(value, pltpu.HBM)
            for value in (moments, flags, shifts.T, fraction.reshape(1, pencils))
        ))
        return pl.pallas_call(
            deliver,
            out_shape=results,
            in_specs=[in_vmem] * 2,
            out_specs=(in_hbm,) * 2,
            scratch_shapes=[dma((2,))],
            compiler_params=pltpu.CompilerParams(vmem_limit_bytes=8 << 20),
        )(*ready)

    in_specs = (P(None, "cross", "chain"), P("cross", "chain"), P("cross", "chain"), P("cross"))
    out_specs = (P(None, "cross", "chain"), P(None, "cross", "chain"))
    return jax.shard_map(shards, mesh=mesh, in_specs=in_specs, out_specs=out_specs, check_vma=False)
```

```python
import functools

import jax
import numpy as np
import jax.numpy as jnp
from jax import lax
from jax.experimental import pallas as pl
from jax.experimental.pallas import tpu as pltpu
from jax.sharding import PartitionSpec as P

VARS = 5
MOMENTS = 4
BLOCK = 128
SHIFT_MAX = 48
ROWS = VARS * MOMENTS
STRIDE = SHIFT_MAX + 1
CHUNKS = -(-ROWS * STRIDE // BLOCK)
TILE = 8
GROUP = 2 * TILE
EARLY = 2
RELAYED_RIGHT, RELAYED_LEFT = 4, 3
PAIRS = tuple((k, m) for k in range(1, MOMENTS) for m in range(k, MOMENTS))
COEFS = MOMENTS + 2 * len(PAIRS)
MESH = pl.DeviceIdType.MESH
HIGHEST = lax.Precision.HIGHEST

gauss_nodes = (-0.8611363115940526, -0.3399810435848563, 0.3399810435848563, 0.8611363115940526)
gauss_weights = (0.3478548451374538, 0.6521451548625461, 0.6521451548625461, 0.3478548451374538)


def segments(first, length):
    held = [[] for _ in range(CHUNKS)]
    for row in range(ROWS):
        start = first + STRIDE * row
        chunk, lane = divmod(start, BLOCK)
        held[chunk % CHUNKS].append((lane, row))
        if lane + length > BLOCK:
            held[(chunk + 1) % CHUNKS].append((0, row))
    return [sorted(chunk) for chunk in held]


AFTER_FIRST, AFTER_LENGTH = SHIFT_MAX, SHIFT_MAX + 1
BEFORE_FIRST, BEFORE_LENGTH = 0, SHIFT_MAX
AFTER = segments(AFTER_FIRST, AFTER_LENGTH)
BEFORE = segments(BEFORE_FIRST, BEFORE_LENGTH)


def places(row, first, length):
    chunk, lane = divmod(first + STRIDE * row, BLOCK)
    chunks = [chunk % CHUNKS]
    if lane + length > BLOCK:
        chunks.append((chunk + 1) % CHUNKS)
    return chunks, lane


def legendre_values(point):
    return [
        jnp.ones_like(point),
        point,
        0.5 * (3.0 * point * point - 1.0),
        0.5 * (5.0 * point * point * point - 3.0 * point),
    ]


def interval_integrals(low_end, high_end, offset):
    half = 0.5 * (high_end - low_end)
    middle = 0.5 * (high_end + low_end)
    entries = [jnp.zeros_like(low_end) for _ in PAIRS]
    for node, weight in zip(gauss_nodes, gauss_weights):
        point = middle + half * node
        target = legendre_values(point)
        source = legendre_values(point + offset)
        scaled = [weight * half * value for value in target]
        for index, (k, m) in enumerate(PAIRS):
            entries[index] = entries[index] + scaled[k] * source[m]
    return entries


def partial_weights(fraction):
    shifted = 2.0 * fraction - 1.0
    square = shifted * shifted
    return [
        fraction,
        fraction * fraction - fraction,
        0.25 * (square * shifted - shifted),
        0.5 * (0.5 * (1.25 * square * square - 1.5 * square) + 0.125),
    ]


def corner_relays(mesh):
    ring = np.moveaxis(mesh.devices, mesh.axis_names.index("chain"), 0).reshape(mesh.shape["chain"], -1)[:, 0]
    if any(getattr(device, "coords", None) is None for device in ring):
        return {}, {}
    spots = [tuple(device.coords) for device in ring]
    rightward, leftward = {}, {}
    if len({spot[0] for spot in spots}) == 2 and len({spot[1] for spot in spots}) == 2:
        for index in range(len(spots) - 1):
            low, high = spots[index], spots[index + 1]
            if low[0] != high[0] and low[1] != high[1]:
                for found, source, target, pick in (
                    (rightward, index, index + 1, max), (leftward, index + 1, index, min)
                ):
                    corner = (spots[source][0], spots[target][1])
                    at = [i for i, spot in enumerate(spots) if spot[:2] == corner]
                    if at:
                        found[source] = (pick(at), target)
    return rightward, leftward


def exact_dot(value, ones):
    high = value.astype(jnp.bfloat16)
    rest = value - high.astype(jnp.float32)
    middle = rest.astype(jnp.bfloat16)
    low = (rest - middle.astype(jnp.float32)).astype(jnp.bfloat16)
    return sum(jnp.dot(part, ones, preferred_element_type=jnp.float32) for part in (low, middle, high))


def kernel(
    chain, cross, relays,
    moments_in, flags_in, shifts_in, fraction_in,
    remapped, mass,
    moments, flags, shifts, fraction,
    to_left, to_right, from_left, from_right, relay,
    sums, parts, raw, starts, coef, shift_of, base, beyond, triangle,
    left_send, left_recv, right_send, right_recv, relay_send, relay_recv,
    sum_send, sum_recv, part_send, part_recv, ready_sem, open_sem, input_sem,
):
    pencils = moments.shape[1]
    groups = pencils // GROUP
    me = lax.axis_index("chain")
    plane = lax.axis_index("cross")

    inputs = [
        pltpu.make_async_copy(source, target, input_sem.at[index])
        for index, (source, target) in enumerate(
            ((moments_in, moments), (flags_in, flags), (shifts_in, shifts), (fraction_in, fraction))
        )
    ]
    for copy in inputs:
        copy.start()

    barrier = pltpu.get_barrier_semaphore()
    for step in range(1, chain):
        peer = lax.rem(me + step, chain)
        pl.semaphore_signal(barrier, inc=1, device_id={"chain": peer}, device_id_type=MESH)
    leads = me == 0

    @pl.when(leads)
    def _():
        for step in range(1, cross):
            peer = lax.rem(plane + step, cross)
            pl.semaphore_signal(barrier, inc=1, device_id={"cross": peer}, device_id_type=MESH)

    for copy in inputs:
        copy.wait()

    def leftward(group):
        return pltpu.make_async_remote_copy(
            src_ref=to_left.at[group], dst_ref=from_right.at[group],
            send_sem=left_send.at[group], recv_sem=left_recv.at[group],
            device_id={"chain": lax.rem(me + chain - 1, chain)}, device_id_type=MESH,
        )

    def rightward(group):
        return pltpu.make_async_remote_copy(
            src_ref=to_right.at[group], dst_ref=from_left.at[group],
            send_sem=right_send.at[group], recv_sem=right_recv.at[group],
            device_id={"chain": lax.rem(me + 1, chain)}, device_id_type=MESH,
        )

    has_left, has_right = me > 0, me < chain - 1

    sum_copies = [
        pltpu.make_async_remote_copy(
            src_ref=sums.at[me], dst_ref=sums.at[me],
            send_sem=sum_send.at[step], recv_sem=sum_recv.at[step],
            device_id={"chain": lax.rem(me + step, chain)}, device_id_type=MESH,
        )
        for step in range(1, chain)
    ]

    def send_sums():
        row_id = lax.broadcasted_iota(jnp.int32, (8, BLOCK), 0)
        total = jnp.zeros((8, pencils), jnp.float32)
        for var in range(VARS):
            pick = (row_id == var).astype(jnp.float32)
            total = total + lax.dot_general(
                pick, moments[MOMENTS * var], (((1,), (1,)), ((), ())),
                precision=HIGHEST, preferred_element_type=jnp.float32,
            )
        sums[me] = total
        for copy in sum_copies:
            copy.start()

    wide_lane = lax.broadcasted_iota(jnp.int32, (GROUP, BLOCK), 1)

    def pack(group):
        rows = pl.ds(pl.multiple_of(group * GROUP, GROUP), GROUP)
        flag = flags[rows, :]
        keep_linear, keep_full = flag <= 1, flag == 0
        rolled = []
        for row in range(ROWS):
            value = moments[row, rows, :]
            order = row % MOMENTS
            if order > 0:
                value = jnp.where(keep_linear if order == 1 else keep_full, value, 0.0)
                moments[row, rows, :] = value
            rolled.append(pltpu.roll(value, (STRIDE * row + SHIFT_MAX) % BLOCK, 1))
        for chunk in range(CHUNKS):
            for held, target in ((AFTER, to_left), (BEFORE, to_right)):
                value = rolled[held[chunk][0][1]]
                for start, row in held[chunk][1:]:
                    value = jnp.where(wide_lane >= start, rolled[row], value)
                target[group, chunk] = value

    right_relays, left_relays = relays

    def to_relay(group, source, send_sem, through):
        return pltpu.make_async_remote_copy(
            src_ref=source.at[group], dst_ref=relay.at[group],
            send_sem=send_sem.at[group], recv_sem=relay_recv.at[group],
            device_id={"chain": jnp.int32(through)}, device_id_type=MESH,
        )

    def onward(group, landing, recv_sem, target):
        return pltpu.make_async_remote_copy(
            src_ref=relay.at[group], dst_ref=landing.at[group],
            send_sem=relay_send.at[group], recv_sem=recv_sem.at[group],
            device_id={"chain": jnp.int32(target)}, device_id_type=MESH,
        )

    def send(group, direct, wanted, count, routes, source, send_sem):
        group = jnp.int32(group)
        odd = (lax.rem(group, 2) == 1) & (group < 2 * count)
        for start, (through, _) in routes.items():
            wanted = wanted & ((me != start) | jnp.logical_not(odd))

            @pl.when((me == start) & odd)
            def _():
                to_relay(group, source, send_sem, through).start()

        @pl.when(wanted)
        def _():
            direct(group).start()

    def send_both(group):
        send(group, leftward, has_left, RELAYED_LEFT, left_relays, to_left, left_send)
        send(group, rightward, has_right, RELAYED_RIGHT, right_relays, to_right, right_send)

    def pack_and_send(group, carry):
        pack(group)
        send_both(group)
        return carry

    pack(0)
    pl.semaphore_wait(barrier, jnp.where(leads, chain - 1 + cross - 1, chain - 1))
    send_both(0)

    @pl.when(leads)
    def _():
        for step in range(1, cross):
            peer = lax.rem(plane + step, cross)
            pl.semaphore_signal(ready_sem, inc=1, device_id={"cross": peer}, device_id_type=MESH)

    lax.fori_loop(1, EARLY, pack_and_send, 0)
    send_sums()
    lax.fori_loop(EARLY, groups, pack_and_send, 0)

    part_copies = [
        pltpu.make_async_remote_copy(
            src_ref=parts.at[plane], dst_ref=parts.at[plane],
            send_sem=part_send.at[step], recv_sem=part_recv.at[step],
            device_id={"cross": lax.rem(plane + step, cross)}, device_id_type=MESH,
        )
        for step in range(1, cross)
    ]

    def open_planes():
        @pl.when(leads)
        def _():
            pl.semaphore_wait(ready_sem, cross - 1)
            for peer in range(1, chain):
                pl.semaphore_signal(open_sem, inc=1, device_id={"chain": jnp.int32(peer)}, device_id_type=MESH)

    def send_parts():
        @pl.when(jnp.logical_not(leads))
        def _():
            pl.semaphore_wait(open_sem, 1)

        for copy in part_copies:
            copy.start()

    def pass_on(index):
        group = 2 * index + 1
        for count, routes, source, send_sem, landing, recv_sem in (
            (RELAYED_RIGHT, right_relays, to_right, right_send, from_left, right_recv),
            (RELAYED_LEFT, left_relays, to_left, left_send, from_right, left_recv),
        ):
            for through, target in routes.values():
                if index >= count:
                    continue

                @pl.when(me == through)
                def _():
                    to_relay(group, source, send_sem, through).wait_recv()
                    onward(group, landing, recv_sem, target).start()

    shift_row = shifts[...]

    def reduce_chain():
        starts[...] = jnp.zeros_like(starts)
        for copy in sum_copies:
            copy.wait_recv()
        before = jnp.zeros((8, pencils), jnp.float32)
        whole = jnp.zeros((8, pencils), jnp.float32)
        for index in range(chain):
            value = sums[index]
            before = before + jnp.where(index < me, value, 0.0)
            whole = whole + value

        parts[plane] = jnp.broadcast_to(jnp.sum(whole, axis=1, keepdims=True), (8, BLOCK))
        starts[0:8, :] = before
        starts[8:16, :] = before + jnp.where(shift_row >= 0, sums[me], 0.0)

    def spread_starts():
        turned = jnp.transpose(starts[...])
        for var in range(VARS):
            base[var] = base[var] + turned[:, var : var + 1]
            beyond[var] = jnp.broadcast_to(turned[:, 8 + var : 9 + var], (pencils, BLOCK))

    pass_on(0)

    @pl.when(me == 0)
    def _():
        from_left[...] = jnp.zeros_like(from_left)

    @pl.when(me == chain - 1)
    def _():
        from_right[...] = jnp.zeros_like(from_right)

    f = fraction[...]
    first = interval_integrals(-1.0 + 0.0 * f, 1.0 - 2.0 * f, 2.0 * f)
    second = interval_integrals(1.0 - 2.0 * f, 1.0 + 0.0 * f, 2.0 * f - 2.0)
    raw[...] = jnp.zeros_like(raw)
    columns = partial_weights(f) + first + second + [shift_row.astype(jnp.float32)]
    for index, value in enumerate(columns):
        raw[index : index + 1, :] = value
    turned = jnp.transpose(raw[...])
    for index in range(COEFS):
        coef[index] = jnp.broadcast_to(turned[:, index : index + 1], (pencils, BLOCK))
    shift_of[...] = jnp.broadcast_to(turned[:, COEFS : COEFS + 1], (pencils, BLOCK)).astype(jnp.int32)

    pass_on(1)

    source_cell = lax.broadcasted_iota(jnp.int32, (BLOCK, BLOCK), 0)
    target_cell = lax.broadcasted_iota(jnp.int32, (BLOCK, BLOCK), 1)
    before_cell = jnp.where(source_cell < target_cell, 1.0, 0.0)
    up_to_edge = jnp.where(
        source_cell < BLOCK // 2, before_cell, 1.0 - before_cell
    )
    triangle[...] = up_to_edge.astype(jnp.bfloat16)
    own_triangle = before_cell.astype(jnp.bfloat16)
    for var in range(VARS):
        base[var] = exact_dot(moments[MOMENTS * var], own_triangle)

    pass_on(2)
    pass_on(3)
    reduce_chain()
    open_planes()
    spread_starts()
    send_parts()


    lane = lax.broadcasted_iota(jnp.int32, (TILE, BLOCK), 1)

    def remap(group, carry):
        @pl.when(has_right)
        def _():
            leftward(group).wait_recv()

        @pl.when(has_left)
        def _():
            rightward(group).wait_recv()

        halos, places_of = [], []
        for tile in range(GROUP // TILE):
            rows = pl.ds(pl.multiple_of(group * GROUP + tile * TILE, TILE), TILE)
            inner = pl.ds(tile * TILE, TILE)
            shift = shift_of[rows, :]
            ahead = shift >= 0
            places_of.append((rows, shift, ahead))

            def halo_row(row):
                values = []
                for ref, first_lane, length in (
                    (from_right, AFTER_FIRST, AFTER_LENGTH),
                    (from_left, BEFORE_FIRST, BEFORE_LENGTH),
                ):
                    chunks, start = places(row, first_lane, length)
                    value = ref[group, chunks[0], inner, :]
                    if len(chunks) > 1:
                        value = jnp.where(lane >= start, value, ref[group, chunks[1], inner, :])
                    values.append(value)
                value = jnp.where(ahead, values[0], values[1])
                return pltpu.roll(value, (-(STRIDE * row + SHIFT_MAX)) % BLOCK, 1)

            halos.append([halo_row(row) for row in range(ROWS)])

        signed = []
        for (_, _, ahead), halo in zip(places_of, halos):
            for var in range(VARS):
                value = halo[MOMENTS * var]
                signed.append(jnp.where(
                    ahead,
                    jnp.where(lane < AFTER_LENGTH, value, 0.0),
                    jnp.where(lane >= BLOCK - BEFORE_LENGTH, -value, 0.0),
                ))
        crossed = exact_dot(jnp.concatenate(signed, axis=0), triangle[...])

        for tile, ((rows, shift, ahead), halo) in enumerate(zip(places_of, halos)):
            turn = shift & (BLOCK - 1)
            outside = jnp.where(ahead, lane - turn, turn - 1 - lane) < 0
            outside_next = jnp.where(ahead, lane - turn - 1, turn - lane) < 0
            at = (lane + turn) & (BLOCK - 1)
            weight = [coef[m, rows, :] for m in range(MOMENTS)]
            inside, across = {}, {}
            for index, (k, m) in enumerate(PAIRS):
                inside[k, m] = coef[MOMENTS + index, rows, :]
                across[k, m] = coef[MOMENTS + len(PAIRS) + index, rows, :]

            def settle(value):
                return jnp.take_along_axis(value, at, axis=1, mode="promise_in_bounds")

            for var in range(VARS):
                here, after = [], []
                for order in range(MOMENTS):
                    own = moments[MOMENTS * var + order, rows, :]
                    other = halo[MOMENTS * var + order]
                    here.append(jnp.where(outside, other, own))
                    after.append(pltpu.roll(jnp.where(outside_next, other, own), BLOCK - 1, 1))
                filled = weight[0] * here[0]
                filled_after = weight[0] * after[0]
                for m in range(1, MOMENTS):
                    filled = filled + weight[m] * here[m]
                    filled_after = filled_after + weight[m] * after[m]
                rise = after[0] - here[0]
                remapped[MOMENTS * var, rows, :] = settle(here[0] + (filled_after - filled))
                for k in range(1, MOMENTS):
                    value = inside[k, k] * here[k] + across[k, k] * after[k]
                    for m in range(1, MOMENTS):
                        if m == k:
                            continue
                        pair = (min(k, m), max(k, m))
                        term = inside[pair] * here[m] + across[pair] * after[m]
                        value = value - term if k > m and (k + m) % 2 else value + term
                    edge = (2.0 if k % 2 == 0 else -2.0) * (weight[k] * rise)
                    remapped[MOMENTS * var + k, rows, :] = settle((k + 0.5) * (value + edge))
                index = (tile * VARS + var) * TILE
                start = jnp.where(
                    outside, crossed[index : index + TILE] + beyond[var, rows, :], base[var, rows, :]
                )
                mass[var, rows, :] = settle(start + filled)
        return carry

    lax.fori_loop(0, groups, remap, 0)

    for copy in part_copies:
        copy.wait_recv()
    grand = parts[0]
    for index in range(1, cross):
        grand = grand + parts[index]
    mean = grand / float(pencils * cross)
    for var in range(VARS):
        mass[var] = mass[var] / mean[var : var + 1, :]

    for copy in sum_copies + part_copies:
        copy.wait_send()

    for count, routes, landing, recv_sem in (
        (RELAYED_RIGHT, right_relays, from_left, right_recv), (RELAYED_LEFT, left_relays, from_right, left_recv)
    ):
        for through, target in routes.values():

            @pl.when(me == through)
            def _():
                for group in range(count):
                    onward(2 * group + 1, landing, recv_sem, target).wait_send()

    @pl.when(has_left)
    def _():
        for group in range(groups):
            leftward(group).wait_send()

    @pl.when(has_right)
    def _():
        for group in range(groups):
            rightward(group).wait_send()


def deliver(remapped, mass, remapped_out, mass_out, sem):
    copies = [
        pltpu.make_async_copy(remapped, remapped_out, sem.at[0]),
        pltpu.make_async_copy(mass, mass_out, sem.at[1]),
    ]
    for copy in copies:
        copy.start()
    for copy in copies:
        copy.wait()


def solution(mesh):
    chain, cross = mesh.shape["chain"], mesh.shape["cross"]
    relays = corner_relays(mesh)

    def shards(moments, flags, shifts, fraction):
        row_count, pencils, cells = moments.shape
        assert row_count == ROWS and cells == BLOCK and pencils == BLOCK
        groups = pencils // GROUP
        block = pltpu.VMEM((groups, CHUNKS, GROUP, BLOCK), jnp.float32)
        dma = pltpu.SemaphoreType.DMA
        results = (
            jax.ShapeDtypeStruct(moments.shape, jnp.float32),
            jax.ShapeDtypeStruct((VARS, pencils, cells), jnp.float32),
        )
        in_vmem = pl.BlockSpec(memory_space=pltpu.VMEM)
        in_hbm = pl.BlockSpec(memory_space=pltpu.HBM)
        ready = pl.pallas_call(
            functools.partial(kernel, chain, cross, relays),
            out_shape=results,
            in_specs=[in_hbm] * 4,
            out_specs=(in_vmem,) * 2,
            scratch_shapes=[
                pltpu.VMEM(moments.shape, jnp.float32),
                pltpu.VMEM(flags.shape, jnp.int32),
                pltpu.VMEM((1, pencils), jnp.int32),
                pltpu.VMEM((1, pencils), jnp.float32),
                block, block, block, block, block,
                pltpu.VMEM((chain, 8, pencils), jnp.float32),
                pltpu.VMEM((cross, 8, BLOCK), jnp.float32),
                pltpu.VMEM((BLOCK, pencils), jnp.float32),
                pltpu.VMEM((BLOCK, pencils), jnp.float32),
                pltpu.VMEM((COEFS, pencils, BLOCK), jnp.float32),
                pltpu.VMEM((pencils, BLOCK), jnp.int32),
                pltpu.VMEM((VARS, pencils, BLOCK), jnp.float32),
                pltpu.VMEM((VARS, pencils, BLOCK), jnp.float32),
                pltpu.VMEM((BLOCK, BLOCK), jnp.bfloat16),
                dma((groups,)), dma((groups,)), dma((groups,)), dma((groups,)),
                dma((groups,)), dma((groups,)),
                dma((chain,)), dma((chain,)), dma((cross,)), dma((cross,)), pltpu.SemaphoreType.REGULAR, pltpu.SemaphoreType.REGULAR, dma((4,)),
            ],
            compiler_params=pltpu.CompilerParams(
                collective_id=0, has_side_effects=True, vmem_limit_bytes=32 << 20
            ),
        )(*(
            pltpu.with_memory_space_constraint(value, pltpu.HBM)
            for value in (moments, flags, shifts.T, fraction.reshape(1, pencils))
        ))
        return pl.pallas_call(
            deliver,
            out_shape=results,
            in_specs=[in_vmem] * 2,
            out_specs=(in_hbm,) * 2,
            scratch_shapes=[dma((2,))],
            compiler_params=pltpu.CompilerParams(vmem_limit_bytes=8 << 20),
        )(*ready)

    in_specs = (P(None, "cross", "chain"), P("cross", "chain"), P("cross", "chain"), P("cross"))
    out_specs = (P(None, "cross", "chain"), P(None, "cross", "chain"))
    return jax.shard_map(shards, mesh=mesh, in_specs=in_specs, out_specs=out_specs, check_vma=False)
```

```python
import functools

import jax
import numpy as np
import jax.numpy as jnp
from jax import lax
from jax.experimental import pallas as pl
from jax.experimental.pallas import tpu as pltpu
from jax.sharding import PartitionSpec as P

VARS = 5
MOMENTS = 4
BLOCK = 128
SHIFT_MAX = 48
ROWS = VARS * MOMENTS
STRIDE = SHIFT_MAX + 1
CHUNKS = -(-ROWS * STRIDE // BLOCK)
TILE = 8
GROUP = 2 * TILE
RELAYED_RIGHT, RELAYED_LEFT = (1, 3, 5, 6, 7), (1, 3, 5)
PAIRS = tuple((k, m) for k in range(1, MOMENTS) for m in range(k, MOMENTS))
COEFS = MOMENTS + 2 * len(PAIRS)
MESH = pl.DeviceIdType.MESH
HIGHEST = lax.Precision.HIGHEST

gauss_nodes = (-0.8611363115940526, -0.3399810435848563, 0.3399810435848563, 0.8611363115940526)
gauss_weights = (0.3478548451374538, 0.6521451548625461, 0.6521451548625461, 0.3478548451374538)


def segments(first, length):
    held = [[] for _ in range(CHUNKS)]
    for row in range(ROWS):
        start = first + STRIDE * row
        chunk, lane = divmod(start, BLOCK)
        held[chunk % CHUNKS].append((lane, row))
        if lane + length > BLOCK:
            held[(chunk + 1) % CHUNKS].append((0, row))
    return [sorted(chunk) for chunk in held]


AFTER_FIRST, AFTER_LENGTH = SHIFT_MAX, SHIFT_MAX + 1
BEFORE_FIRST, BEFORE_LENGTH = 0, SHIFT_MAX
AFTER = segments(AFTER_FIRST, AFTER_LENGTH)
BEFORE = segments(BEFORE_FIRST, BEFORE_LENGTH)


def places(row, first, length):
    chunk, lane = divmod(first + STRIDE * row, BLOCK)
    chunks = [chunk % CHUNKS]
    if lane + length > BLOCK:
        chunks.append((chunk + 1) % CHUNKS)
    return chunks, lane


def legendre_values(point):
    return [
        jnp.ones_like(point),
        point,
        0.5 * (3.0 * point * point - 1.0),
        0.5 * (5.0 * point * point * point - 3.0 * point),
    ]


def interval_integrals(low_end, high_end, offset):
    half = 0.5 * (high_end - low_end)
    middle = 0.5 * (high_end + low_end)
    entries = [jnp.zeros_like(low_end) for _ in PAIRS]
    for node, weight in zip(gauss_nodes, gauss_weights):
        point = middle + half * node
        target = legendre_values(point)
        source = legendre_values(point + offset)
        scaled = [weight * half * value for value in target]
        for index, (k, m) in enumerate(PAIRS):
            entries[index] = entries[index] + scaled[k] * source[m]
    return entries


def partial_weights(fraction):
    shifted = 2.0 * fraction - 1.0
    square = shifted * shifted
    return [
        fraction,
        fraction * fraction - fraction,
        0.25 * (square * shifted - shifted),
        0.5 * (0.5 * (1.25 * square * square - 1.5 * square) + 0.125),
    ]


def corner_relays(mesh):
    ring = np.moveaxis(mesh.devices, mesh.axis_names.index("chain"), 0).reshape(mesh.shape["chain"], -1)[:, 0]
    if any(getattr(device, "coords", None) is None for device in ring):
        return {}, {}
    spots = [tuple(device.coords) for device in ring]
    rightward, leftward = {}, {}
    if len({spot[0] for spot in spots}) == 2 and len({spot[1] for spot in spots}) == 2:
        for index in range(len(spots) - 1):
            low, high = spots[index], spots[index + 1]
            if low[0] != high[0] and low[1] != high[1]:
                for found, source, target, pick in (
                    (rightward, index, index + 1, max), (leftward, index + 1, index, max)
                ):
                    corner = (spots[source][0], spots[target][1])
                    at = [i for i, spot in enumerate(spots) if spot[:2] == corner]
                    if at:
                        found[source] = (pick(at), target)
    return rightward, leftward


def exact_dot(value, ones):
    high = value.astype(jnp.bfloat16)
    rest = value - high.astype(jnp.float32)
    middle = rest.astype(jnp.bfloat16)
    low = (rest - middle.astype(jnp.float32)).astype(jnp.bfloat16)
    return sum(jnp.dot(part, ones, preferred_element_type=jnp.float32) for part in (low, middle, high))


def kernel(
    chain, cross, relays,
    moments_in, flags_in, shifts_in, fraction_in,
    remapped, mass,
    moments, flags, shifts, fraction,
    to_left, to_right, from_left, from_right, relay,
    sums, parts, raw, starts, coef, shift_of, base, beyond, triangle,
    left_send, left_recv, right_send, right_recv, relay_send, relay_recv,
    sum_send, sum_recv, part_send, part_recv, ready_sem, open_sem, input_sem,
):
    pencils = moments.shape[1]
    groups = pencils // GROUP
    me = lax.axis_index("chain")
    plane = lax.axis_index("cross")

    first_rows, later_rows = pl.ds(0, GROUP), pl.ds(GROUP, pencils - GROUP)
    inputs = [
        pltpu.make_async_copy(source, target, input_sem.at[index])
        for index, (source, target) in enumerate((
            (flags_in, flags),
            (moments_in.at[:, first_rows, :], moments.at[:, first_rows, :]),
            (moments_in.at[:, later_rows, :], moments.at[:, later_rows, :]),
            (shifts_in, shifts),
            (fraction_in, fraction),
        ))
    ]
    urgent, rest = inputs[:2], inputs[2:]
    for copy in urgent:
        copy.start()

    barrier = pltpu.get_barrier_semaphore()
    for step in range(1, chain):
        peer = lax.rem(me + step, chain)
        pl.semaphore_signal(barrier, inc=1, device_id={"chain": peer}, device_id_type=MESH)
    leads = me == 0

    @pl.when(leads)
    def _():
        for step in range(1, cross):
            peer = lax.rem(plane + step, cross)
            pl.semaphore_signal(barrier, inc=1, device_id={"cross": peer}, device_id_type=MESH)

    for copy in rest:
        copy.start()
    for copy in urgent:
        copy.wait()

    def leftward(group):
        return pltpu.make_async_remote_copy(
            src_ref=to_left.at[group], dst_ref=from_right.at[group],
            send_sem=left_send.at[group], recv_sem=left_recv.at[group],
            device_id={"chain": lax.rem(me + chain - 1, chain)}, device_id_type=MESH,
        )

    def rightward(group):
        return pltpu.make_async_remote_copy(
            src_ref=to_right.at[group], dst_ref=from_left.at[group],
            send_sem=right_send.at[group], recv_sem=right_recv.at[group],
            device_id={"chain": lax.rem(me + 1, chain)}, device_id_type=MESH,
        )

    has_left, has_right = me > 0, me < chain - 1

    sum_copies = [
        pltpu.make_async_remote_copy(
            src_ref=sums.at[me], dst_ref=sums.at[me],
            send_sem=sum_send.at[step], recv_sem=sum_recv.at[step],
            device_id={"chain": lax.rem(me + step, chain)}, device_id_type=MESH,
        )
        for step in range(1, chain)
    ]

    source_cell = lax.broadcasted_iota(jnp.int32, (BLOCK, BLOCK), 0)
    target_cell = lax.broadcasted_iota(jnp.int32, (BLOCK, BLOCK), 1)
    before_cell = jnp.where(source_cell < target_cell, 1.0, 0.0)

    def send_sums():
        total = jnp.zeros((pencils, BLOCK), jnp.float32)
        for var in range(VARS):
            pick = jnp.where(target_cell == var, 1.0, 0.0)
            both = jnp.concatenate([before_cell, pick], axis=1).astype(jnp.bfloat16)
            summed = exact_dot(moments[MOMENTS * var], both)
            base[var] = summed[:, :BLOCK]
            total = total + summed[:, BLOCK:]
        sums[me] = jnp.transpose(total)[:8]
        for copy in sum_copies:
            copy.start()

    wide_lane = lax.broadcasted_iota(jnp.int32, (GROUP, BLOCK), 1)

    def pack(group):
        rows = pl.ds(pl.multiple_of(group * GROUP, GROUP), GROUP)
        flag = flags[rows, :]
        keep_linear, keep_full = flag <= 1, flag == 0
        rolled = []
        for row in range(ROWS):
            value = moments[row, rows, :]
            order = row % MOMENTS
            if order > 0:
                value = jnp.where(keep_linear if order == 1 else keep_full, value, 0.0)
                moments[row, rows, :] = value
            rolled.append(pltpu.roll(value, (STRIDE * row + SHIFT_MAX) % BLOCK, 1))
        for chunk in range(CHUNKS):
            for held, target in ((AFTER, to_left), (BEFORE, to_right)):
                value = rolled[held[chunk][0][1]]
                for start, row in held[chunk][1:]:
                    value = jnp.where(wide_lane >= start, rolled[row], value)
                target[group, chunk] = value

    right_relays, left_relays = relays

    def to_relay(group, source, send_sem, through):
        return pltpu.make_async_remote_copy(
            src_ref=source.at[group], dst_ref=relay.at[group],
            send_sem=send_sem.at[group], recv_sem=relay_recv.at[group],
            device_id={"chain": jnp.int32(through)}, device_id_type=MESH,
        )

    def onward(group, landing, recv_sem, target):
        return pltpu.make_async_remote_copy(
            src_ref=relay.at[group], dst_ref=landing.at[group],
            send_sem=relay_send.at[group], recv_sem=recv_sem.at[group],
            device_id={"chain": jnp.int32(target)}, device_id_type=MESH,
        )

    def send(group, direct, wanted, among, routes, source, send_sem):
        group = jnp.int32(group)
        relayed = functools.reduce(jnp.logical_or, [group == index for index in among])
        for start, (through, _) in routes.items():
            wanted = wanted & ((me != start) | jnp.logical_not(relayed))

            @pl.when((me == start) & relayed)
            def _():
                to_relay(group, source, send_sem, through).start()

        @pl.when(wanted)
        def _():
            direct(group).start()

    def send_both(group):
        send(group, leftward, has_left, RELAYED_LEFT, left_relays, to_left, left_send)
        send(group, rightward, has_right, RELAYED_RIGHT, right_relays, to_right, right_send)

    def pack_and_send(group, carry):
        pack(group)
        send_both(group)
        return carry

    pack(0)
    pl.semaphore_wait(barrier, jnp.where(leads, chain - 1 + cross - 1, chain - 1))
    send_both(0)

    @pl.when(leads)
    def _():
        for step in range(1, cross):
            peer = lax.rem(plane + step, cross)
            pl.semaphore_signal(ready_sem, inc=1, device_id={"cross": peer}, device_id_type=MESH)

    for copy in rest:
        copy.wait()
    send_sums()
    lax.fori_loop(1, groups, pack_and_send, 0)

    part_copies = [
        pltpu.make_async_remote_copy(
            src_ref=parts.at[plane], dst_ref=parts.at[plane],
            send_sem=part_send.at[step], recv_sem=part_recv.at[step],
            device_id={"cross": lax.rem(plane + step, cross)}, device_id_type=MESH,
        )
        for step in range(1, cross)
    ]

    def open_planes():
        @pl.when(leads)
        def _():
            pl.semaphore_wait(ready_sem, cross - 1)
            for peer in range(1, chain):
                pl.semaphore_signal(open_sem, inc=1, device_id={"chain": jnp.int32(peer)}, device_id_type=MESH)

    def send_parts():
        @pl.when(jnp.logical_not(leads))
        def _():
            pl.semaphore_wait(open_sem, 1)

        for copy in part_copies:
            copy.start()

    def pass_on(index):
        for among, routes, source, send_sem, landing, recv_sem in (
            (RELAYED_RIGHT, right_relays, to_right, right_send, from_left, right_recv),
            (RELAYED_LEFT, left_relays, to_left, left_send, from_right, left_recv),
        ):
            for through, target in routes.values():
                if index >= len(among):
                    continue
                group = among[index]

                @pl.when(me == through)
                def _():
                    to_relay(group, source, send_sem, through).wait_recv()
                    onward(group, landing, recv_sem, target).start()

    shift_row = shifts[...]

    def reduce_chain():
        starts[...] = jnp.zeros_like(starts)
        for copy in sum_copies:
            copy.wait_recv()
        before = jnp.zeros((8, pencils), jnp.float32)
        whole = jnp.zeros((8, pencils), jnp.float32)
        for index in range(chain):
            value = sums[index]
            before = before + jnp.where(index < me, value, 0.0)
            whole = whole + value

        parts[plane] = jnp.broadcast_to(jnp.sum(whole, axis=1, keepdims=True), (8, BLOCK))
        starts[0:8, :] = before
        starts[8:16, :] = before + jnp.where(shift_row >= 0, sums[me], 0.0)

    def spread_starts():
        turned = jnp.transpose(starts[...])
        for var in range(VARS):
            base[var] = base[var] + turned[:, var : var + 1]
            beyond[var] = jnp.broadcast_to(turned[:, 8 + var : 9 + var], (pencils, BLOCK))

    pass_on(0)

    @pl.when(me == 0)
    def _():
        from_left[...] = jnp.zeros_like(from_left)

    @pl.when(me == chain - 1)
    def _():
        from_right[...] = jnp.zeros_like(from_right)

    f = fraction[...]
    first = interval_integrals(-1.0 + 0.0 * f, 1.0 - 2.0 * f, 2.0 * f)
    second = interval_integrals(1.0 - 2.0 * f, 1.0 + 0.0 * f, 2.0 * f - 2.0)
    raw[...] = jnp.zeros_like(raw)
    columns = partial_weights(f) + first + second + [shift_row.astype(jnp.float32)]
    for index, value in enumerate(columns):
        raw[index : index + 1, :] = value
    turned = jnp.transpose(raw[...])
    for index in range(COEFS):
        coef[index] = jnp.broadcast_to(turned[:, index : index + 1], (pencils, BLOCK))
    shift_of[...] = jnp.broadcast_to(turned[:, COEFS : COEFS + 1], (pencils, BLOCK)).astype(jnp.int32)

    pass_on(1)
    up_to_edge = jnp.where(source_cell < BLOCK // 2, before_cell, 1.0 - before_cell)
    triangle[...] = up_to_edge.astype(jnp.bfloat16)
    pass_on(2)
    pass_on(3)
    pass_on(4)
    reduce_chain()
    open_planes()
    spread_starts()
    send_parts()


    lane = lax.broadcasted_iota(jnp.int32, (TILE, BLOCK), 1)

    def remap(group, carry):
        @pl.when(has_right)
        def _():
            leftward(group).wait_recv()

        @pl.when(has_left)
        def _():
            rightward(group).wait_recv()

        halos, places_of = [], []
        for tile in range(GROUP // TILE):
            rows = pl.ds(pl.multiple_of(group * GROUP + tile * TILE, TILE), TILE)
            inner = pl.ds(tile * TILE, TILE)
            shift = shift_of[rows, :]
            ahead = shift >= 0
            places_of.append((rows, shift, ahead))

            def halo_row(row):
                values = []
                for ref, first_lane, length in (
                    (from_right, AFTER_FIRST, AFTER_LENGTH),
                    (from_left, BEFORE_FIRST, BEFORE_LENGTH),
                ):
                    chunks, start = places(row, first_lane, length)
                    value = ref[group, chunks[0], inner, :]
                    if len(chunks) > 1:
                        value = jnp.where(lane >= start, value, ref[group, chunks[1], inner, :])
                    values.append(value)
                value = jnp.where(ahead, values[0], values[1])
                return pltpu.roll(value, (-(STRIDE * row + SHIFT_MAX)) % BLOCK, 1)

            halos.append([halo_row(row) for row in range(ROWS)])

        signed = []
        for (_, _, ahead), halo in zip(places_of, halos):
            for var in range(VARS):
                value = halo[MOMENTS * var]
                signed.append(jnp.where(
                    ahead,
                    jnp.where(lane < AFTER_LENGTH, value, 0.0),
                    jnp.where(lane >= BLOCK - BEFORE_LENGTH, -value, 0.0),
                ))
        crossed = exact_dot(jnp.concatenate(signed, axis=0), triangle[...])

        for tile, ((rows, shift, ahead), halo) in enumerate(zip(places_of, halos)):
            turn = shift & (BLOCK - 1)
            outside = jnp.where(ahead, lane - turn, turn - 1 - lane) < 0
            outside_next = jnp.where(ahead, lane - turn - 1, turn - lane) < 0
            at = (lane + turn) & (BLOCK - 1)
            weight = [coef[m, rows, :] for m in range(MOMENTS)]
            inside, across = {}, {}
            for index, (k, m) in enumerate(PAIRS):
                inside[k, m] = coef[MOMENTS + index, rows, :]
                across[k, m] = coef[MOMENTS + len(PAIRS) + index, rows, :]

            def settle(value):
                return jnp.take_along_axis(value, at, axis=1, mode="promise_in_bounds")

            for var in range(VARS):
                here, after = [], []
                for order in range(MOMENTS):
                    own = moments[MOMENTS * var + order, rows, :]
                    other = halo[MOMENTS * var + order]
                    here.append(jnp.where(outside, other, own))
                    after.append(pltpu.roll(jnp.where(outside_next, other, own), BLOCK - 1, 1))
                filled = weight[0] * here[0]
                filled_after = weight[0] * after[0]
                for m in range(1, MOMENTS):
                    filled = filled + weight[m] * here[m]
                    filled_after = filled_after + weight[m] * after[m]
                rise = after[0] - here[0]
                remapped[MOMENTS * var, rows, :] = settle(here[0] + (filled_after - filled))
                for k in range(1, MOMENTS):
                    value = inside[k, k] * here[k] + across[k, k] * after[k]
                    for m in range(1, MOMENTS):
                        if m == k:
                            continue
                        pair = (min(k, m), max(k, m))
                        term = inside[pair] * here[m] + across[pair] * after[m]
                        value = value - term if k > m and (k + m) % 2 else value + term
                    edge = (2.0 if k % 2 == 0 else -2.0) * (weight[k] * rise)
                    remapped[MOMENTS * var + k, rows, :] = settle((k + 0.5) * (value + edge))
                index = (tile * VARS + var) * TILE
                start = jnp.where(
                    outside, crossed[index : index + TILE] + beyond[var, rows, :], base[var, rows, :]
                )
                mass[var, rows, :] = settle(start + filled)
        return carry

    lax.fori_loop(0, groups, remap, 0)

    for copy in part_copies:
        copy.wait_recv()
    grand = parts[0]
    for index in range(1, cross):
        grand = grand + parts[index]
    mean = grand / float(pencils * cross)
    for var in range(VARS):
        mass[var] = mass[var] / mean[var : var + 1, :]

    for copy in sum_copies + part_copies:
        copy.wait_send()

    for among, routes, landing, recv_sem in (
        (RELAYED_RIGHT, right_relays, from_left, right_recv), (RELAYED_LEFT, left_relays, from_right, left_recv)
    ):
        for through, target in routes.values():

            @pl.when(me == through)
            def _():
                for group in among:
                    onward(group, landing, recv_sem, target).wait_send()

    @pl.when(has_left)
    def _():
        for group in range(groups):
            leftward(group).wait_send()

    @pl.when(has_right)
    def _():
        for group in range(groups):
            rightward(group).wait_send()


def deliver(remapped, mass, remapped_out, mass_out, sem):
    copies = [
        pltpu.make_async_copy(remapped, remapped_out, sem.at[0]),
        pltpu.make_async_copy(mass, mass_out, sem.at[1]),
    ]
    for copy in copies:
        copy.start()
    for copy in copies:
        copy.wait()


def solution(mesh):
    chain, cross = mesh.shape["chain"], mesh.shape["cross"]
    relays = corner_relays(mesh)

    def shards(moments, flags, shifts, fraction):
        row_count, pencils, cells = moments.shape
        assert row_count == ROWS and cells == BLOCK and pencils == BLOCK
        groups = pencils // GROUP
        block = pltpu.VMEM((groups, CHUNKS, GROUP, BLOCK), jnp.float32)
        dma = pltpu.SemaphoreType.DMA
        results = (
            jax.ShapeDtypeStruct(moments.shape, jnp.float32),
            jax.ShapeDtypeStruct((VARS, pencils, cells), jnp.float32),
        )
        in_vmem = pl.BlockSpec(memory_space=pltpu.VMEM)
        in_hbm = pl.BlockSpec(memory_space=pltpu.HBM)
        ready = pl.pallas_call(
            functools.partial(kernel, chain, cross, relays),
            out_shape=results,
            in_specs=[in_hbm] * 4,
            out_specs=(in_vmem,) * 2,
            scratch_shapes=[
                pltpu.VMEM(moments.shape, jnp.float32),
                pltpu.VMEM(flags.shape, jnp.int32),
                pltpu.VMEM((1, pencils), jnp.int32),
                pltpu.VMEM((1, pencils), jnp.float32),
                block, block, block, block, block,
                pltpu.VMEM((chain, 8, pencils), jnp.float32),
                pltpu.VMEM((cross, 8, BLOCK), jnp.float32),
                pltpu.VMEM((BLOCK, pencils), jnp.float32),
                pltpu.VMEM((BLOCK, pencils), jnp.float32),
                pltpu.VMEM((COEFS, pencils, BLOCK), jnp.float32),
                pltpu.VMEM((pencils, BLOCK), jnp.int32),
                pltpu.VMEM((VARS, pencils, BLOCK), jnp.float32),
                pltpu.VMEM((VARS, pencils, BLOCK), jnp.float32),
                pltpu.VMEM((BLOCK, BLOCK), jnp.bfloat16),
                dma((groups,)), dma((groups,)), dma((groups,)), dma((groups,)),
                dma((groups,)), dma((groups,)),
                dma((chain,)), dma((chain,)), dma((cross,)), dma((cross,)), pltpu.SemaphoreType.REGULAR, pltpu.SemaphoreType.REGULAR, dma((5,)),
            ],
            compiler_params=pltpu.CompilerParams(
                collective_id=0, has_side_effects=True, vmem_limit_bytes=32 << 20
            ),
        )(*(
            pltpu.with_memory_space_constraint(value, pltpu.HBM)
            for value in (moments, flags, shifts.T, fraction.reshape(1, pencils))
        ))
        return pl.pallas_call(
            deliver,
            out_shape=results,
            in_specs=[in_vmem] * 2,
            out_specs=(in_hbm,) * 2,
            scratch_shapes=[dma((2,))],
            compiler_params=pltpu.CompilerParams(vmem_limit_bytes=8 << 20),
        )(*ready)

    in_specs = (P(None, "cross", "chain"), P("cross", "chain"), P("cross", "chain"), P("cross"))
    out_specs = (P(None, "cross", "chain"), P(None, "cross", "chain"))
    return jax.shard_map(shards, mesh=mesh, in_specs=in_specs, out_specs=out_specs, check_vma=False)
```

```python
import functools

import jax
import numpy as np
import jax.numpy as jnp
from jax import lax
from jax.experimental import pallas as pl
from jax.experimental.pallas import tpu as pltpu
from jax.sharding import PartitionSpec as P

VARS = 5
MOMENTS = 4
BLOCK = 128
SHIFT_MAX = 48
ROWS = VARS * MOMENTS
SPAN = ROWS * SHIFT_MAX
FULL, HALF = SPAN // BLOCK, BLOCK // 2
TILE = 8
TILES = 2
GROUP = TILES * TILE
SENT = TILES * FULL + 1
EDGES = -(-ROWS // 8)
EDGE_STEP = TILES * EDGES
RELAYED_RIGHT, RELAYED_LEFT = (1, 3, 5, 7), (1, 3, 5)
PAIRS = tuple((k, m) for k in range(1, MOMENTS) for m in range(k, MOMENTS))
COEFS = MOMENTS + 2 * len(PAIRS)
MESH = pl.DeviceIdType.MESH
HIGHEST = lax.Precision.HIGHEST

gauss_nodes = (-0.8611363115940526, -0.3399810435848563, 0.3399810435848563, 0.8611363115940526)
gauss_weights = (0.3478548451374538, 0.6521451548625461, 0.6521451548625461, 0.3478548451374538)


AFTER_FIRST, AFTER_LENGTH = SHIFT_MAX, SHIFT_MAX + 1
BEFORE_FIRST, BEFORE_LENGTH = 0, SHIFT_MAX


def place(row, first):
    chunk, lane = divmod((first + SHIFT_MAX * row) % SPAN, BLOCK)
    return chunk, lane, lane + SHIFT_MAX > BLOCK


def segments(first):
    held = [[] for _ in range(FULL + 1)]
    for row in range(ROWS):
        chunk, lane, splits = place(row, first)
        held[chunk].append((lane, row))
        if splits:
            held[chunk + 1].append((0, row))
    return [sorted(chunk) for chunk in held]


AFTER, BEFORE = segments(AFTER_FIRST), segments(BEFORE_FIRST)
WRAPPED = ROWS - 1


def turn_of(row):
    return (SHIFT_MAX * (row + 1)) % BLOCK


def edge_lane(row):
    return (turn_of(row) + SHIFT_MAX) % BLOCK


def legendre_values(point):
    return [
        jnp.ones_like(point),
        point,
        0.5 * (3.0 * point * point - 1.0),
        0.5 * (5.0 * point * point * point - 3.0 * point),
    ]


def interval_integrals(low_end, high_end, offset):
    half = 0.5 * (high_end - low_end)
    middle = 0.5 * (high_end + low_end)
    entries = [jnp.zeros_like(low_end) for _ in PAIRS]
    for node, weight in zip(gauss_nodes, gauss_weights):
        point = middle + half * node
        target = legendre_values(point)
        source = legendre_values(point + offset)
        scaled = [weight * half * value for value in target]
        for index, (k, m) in enumerate(PAIRS):
            entries[index] = entries[index] + scaled[k] * source[m]
    return entries


def partial_weights(fraction):
    shifted = 2.0 * fraction - 1.0
    square = shifted * shifted
    return [
        fraction,
        fraction * fraction - fraction,
        0.25 * (square * shifted - shifted),
        0.5 * (0.5 * (1.25 * square * square - 1.5 * square) + 0.125),
    ]


def corner_relays(mesh):
    ring = np.moveaxis(mesh.devices, mesh.axis_names.index("chain"), 0).reshape(mesh.shape["chain"], -1)[:, 0]
    if any(getattr(device, "coords", None) is None for device in ring):
        return {}, {}
    spots = [tuple(device.coords) for device in ring]
    rightward, leftward = {}, {}
    if len({spot[0] for spot in spots}) == 2 and len({spot[1] for spot in spots}) == 2:
        for index in range(len(spots) - 1):
            low, high = spots[index], spots[index + 1]
            if low[0] != high[0] and low[1] != high[1]:
                for found, source, target, pick in (
                    (rightward, index, index + 1, max), (leftward, index + 1, index, max)
                ):
                    corner = (spots[source][0], spots[target][1])
                    at = [i for i, spot in enumerate(spots) if spot[:2] == corner]
                    if at:
                        found[source] = (pick(at), target)
    return rightward, leftward


def exact_dot(value, ones):
    high = value.astype(jnp.bfloat16)
    rest = value - high.astype(jnp.float32)
    middle = rest.astype(jnp.bfloat16)
    low = (rest - middle.astype(jnp.float32)).astype(jnp.bfloat16)
    return sum(jnp.dot(part, ones, preferred_element_type=jnp.float32) for part in (low, middle, high))


def finish_group(group, held, remapped, mass, skipped):
    moments, from_left, from_right, edges, coef, shift_of, base, beyond, triangle = held
    lane = lax.broadcasted_iota(jnp.int32, (TILE, BLOCK), 1)
    halos, places_of = [], []
    for tile in range(GROUP // TILE):
        rows = pl.ds(pl.multiple_of(group * GROUP + tile * TILE, TILE), TILE)
        inner = pl.ds(tile * TILE, TILE)
        shift = shift_of[rows, :]
        ahead = shift >= 0
        put = pl.ds(pl.multiple_of(group * GROUP + tile * TILE - skipped, TILE), TILE)
        places_of.append((rows, put, shift, ahead))

        folded = {}
        for name, ref in (("right", from_right), ("left", from_left)):
            value = ref[group, SENT - 1]
            folded[name] = pltpu.roll(value, HALF, 1) if tile else value

        def fetch(name, ref, row, first):
            chunk, start, splits = place(row, first)
            values = [
                ref[group, TILES * index + tile] if index < FULL else folded[name]
                for index in ((chunk, chunk + 1) if splits else (chunk,))
            ]
            return jnp.where(lane >= start, *values) if splits else values[0]

        def halo_row(row):
            right = fetch("right", from_right, row, AFTER_FIRST)
            left = fetch("left", from_left, row, BEFORE_FIRST)
            edge = edges[group, EDGES * tile + row // 8]
            wrapped = row == WRAPPED
            value = left if wrapped else jnp.where(ahead, right, left)
            value = jnp.where(ahead & (lane == edge_lane(row)), edge, value)
            value = pltpu.roll(value, (BLOCK - turn_of(row)) % BLOCK, 1) if turn_of(row) else value
            return jnp.where(ahead & (lane < SHIFT_MAX), right, value) if wrapped else value

        halos.append([halo_row(row) for row in range(ROWS)])

    signed = []
    for (_, _, _, ahead), halo in zip(places_of, halos):
        for var in range(VARS):
            value = halo[MOMENTS * var]
            signed.append(jnp.where(
                ahead,
                jnp.where(lane < AFTER_LENGTH, value, 0.0),
                jnp.where(lane >= BLOCK - BEFORE_LENGTH, -value, 0.0),
            ))
    crossed = exact_dot(jnp.concatenate(signed, axis=0), triangle[...])

    for tile, ((rows, put, shift, ahead), halo) in enumerate(zip(places_of, halos)):
        turn = shift & (BLOCK - 1)
        outside = jnp.where(ahead, lane - turn, turn - 1 - lane) < 0
        outside_next = jnp.where(ahead, lane - turn - 1, turn - lane) < 0
        at = (lane + turn) & (BLOCK - 1)
        weight = [coef[m, rows, :] for m in range(MOMENTS)]
        inside, across = {}, {}
        for index, (k, m) in enumerate(PAIRS):
            inside[k, m] = coef[MOMENTS + index, rows, :]
            across[k, m] = coef[MOMENTS + len(PAIRS) + index, rows, :]

        def settle(value):
            return jnp.take_along_axis(value, at, axis=1, mode="promise_in_bounds")

        for var in range(VARS):
            here, after = [], []
            for order in range(MOMENTS):
                own = moments[MOMENTS * var + order, rows, :]
                other = halo[MOMENTS * var + order]
                here.append(jnp.where(outside, other, own))
                after.append(pltpu.roll(jnp.where(outside_next, other, own), BLOCK - 1, 1))
            filled = weight[0] * here[0]
            filled_after = weight[0] * after[0]
            for m in range(1, MOMENTS):
                filled = filled + weight[m] * here[m]
                filled_after = filled_after + weight[m] * after[m]
            rise = after[0] - here[0]
            remapped[MOMENTS * var, put, :] = settle(here[0] + (filled_after - filled))
            for k in range(1, MOMENTS):
                value = inside[k, k] * here[k] + across[k, k] * after[k]
                for m in range(1, MOMENTS):
                    if m == k:
                        continue
                    pair = (min(k, m), max(k, m))
                    term = inside[pair] * here[m] + across[pair] * after[m]
                    value = value - term if k > m and (k + m) % 2 else value + term
                edge = (2.0 if k % 2 == 0 else -2.0) * (weight[k] * rise)
                remapped[MOMENTS * var + k, put, :] = settle((k + 0.5) * (value + edge))
            index = (tile * VARS + var) * TILE
            start = jnp.where(
                outside, crossed[index : index + TILE] + beyond[var, rows, :], base[var, rows, :]
            )
            mass[var, put, :] = settle(start + filled)


def kernel(
    chain, cross, relays,
    moments_in, flags_in, shifts_in, fraction_in,
    remapped, mass, moments, from_left, from_right, edges, coef, shift_of, base, beyond, triangle, mean_of,
    flags, shifts, fraction,
    to_left, to_right, relay, own_edges, edges_out, edges_in,
    sums, parts, raw, starts,
    left_send, left_recv, right_send, right_recv, relay_send, relay_recv,
    sum_send, sum_recv, part_send, part_recv, ready_sem, open_sem, edge_sem, input_sem,
):
    pencils = moments.shape[1]
    groups = pencils // GROUP
    me = lax.axis_index("chain")
    plane = lax.axis_index("cross")

    first_rows, later_rows = pl.ds(0, GROUP), pl.ds(GROUP, pencils - GROUP)
    inputs = [
        pltpu.make_async_copy(source, target, input_sem.at[index])
        for index, (source, target) in enumerate((
            (flags_in, flags),
            (moments_in.at[:, first_rows, :], moments.at[:, first_rows, :]),
            (moments_in.at[:, later_rows, :], moments.at[:, later_rows, :]),
            (shifts_in, shifts),
            (fraction_in, fraction),
        ))
    ]
    urgent, rest = inputs[:2], inputs[2:]
    for copy in urgent:
        copy.start()

    barrier = pltpu.get_barrier_semaphore()
    for step in range(1, chain):
        peer = lax.rem(me + step, chain)
        pl.semaphore_signal(barrier, inc=1, device_id={"chain": peer}, device_id_type=MESH)
    leads = me == 0

    @pl.when(leads)
    def _():
        for step in range(1, cross):
            peer = lax.rem(plane + step, cross)
            pl.semaphore_signal(barrier, inc=1, device_id={"cross": peer}, device_id_type=MESH)

    for copy in rest:
        copy.start()
    for copy in urgent:
        copy.wait()

    def leftward(group):
        return pltpu.make_async_remote_copy(
            src_ref=to_left.at[group], dst_ref=from_right.at[group],
            send_sem=left_send.at[group], recv_sem=left_recv.at[group],
            device_id={"chain": lax.rem(me + chain - 1, chain)}, device_id_type=MESH,
        )

    def rightward(group):
        return pltpu.make_async_remote_copy(
            src_ref=to_right.at[group], dst_ref=from_left.at[group],
            send_sem=right_send.at[group], recv_sem=right_recv.at[group],
            device_id={"chain": lax.rem(me + 1, chain)}, device_id_type=MESH,
        )

    has_left, has_right = me > 0, me < chain - 1

    sum_copies = [
        pltpu.make_async_remote_copy(
            src_ref=sums.at[me], dst_ref=sums.at[me],
            send_sem=sum_send.at[step], recv_sem=sum_recv.at[step],
            device_id={"chain": lax.rem(me + step, chain)}, device_id_type=MESH,
        )
        for step in range(1, chain)
    ]

    source_cell = lax.broadcasted_iota(jnp.int32, (BLOCK, BLOCK), 0)
    target_cell = lax.broadcasted_iota(jnp.int32, (BLOCK, BLOCK), 1)
    before_cell = jnp.where(source_cell < target_cell, 1.0, 0.0)

    def send_sums():
        total = jnp.zeros((pencils, BLOCK), jnp.float32)
        for var in range(VARS):
            pick = jnp.where(target_cell == var, 1.0, 0.0)
            both = jnp.concatenate([before_cell, pick], axis=1).astype(jnp.bfloat16)
            summed = exact_dot(moments[MOMENTS * var], both)
            base[var] = summed[:, :BLOCK]
            total = total + summed[:, BLOCK:]
        sums[me] = jnp.transpose(total)[:8]
        for copy in sum_copies:
            copy.start()

    lane = lax.broadcasted_iota(jnp.int32, (TILE, BLOCK), 1)
    spot = lane & 15

    def pack(group):
        halves = {}
        edge = None
        for tile in range(TILES):
            rows = pl.ds(pl.multiple_of(group * GROUP + tile * TILE, TILE), TILE)
            flag = flags[rows, :]
            keep_linear, keep_full = flag <= 1, flag == 0
            rolled = []
            for row in range(ROWS):
                value = moments[row, rows, :]
                order = row % MOMENTS
                if order > 0:
                    value = jnp.where(keep_linear if order == 1 else keep_full, value, 0.0)
                    moments[row, rows, :] = value
                rolled.append(pltpu.roll(value, turn_of(row), 1) if turn_of(row) else value)
            for side, (held, target) in enumerate(((AFTER, to_left), (BEFORE, to_right))):
                for chunk in range(FULL + 1):
                    value = None
                    for start, row in held[chunk]:
                        part = moments[row, rows, :] if row == WRAPPED and side == 0 else rolled[row]
                        value = part if value is None else jnp.where(lane >= start, part, value)
                    if chunk < FULL:
                        target[group, TILES * chunk + tile] = value
                    else:
                        halves[side, tile] = value
            for index in range(EDGES):
                value = None
                for row in range(8 * index, min(8 * index + 8, ROWS)):
                    here = (lane >> 4) == edge_lane(row) // 16
                    value = rolled[row] if value is None else jnp.where(here, rolled[row], value)
                at = EDGES * tile + index
                value = pltpu.roll(value, at, 1) if at else value
                edge = value if edge is None else jnp.where(spot >= at, value, edge)
        for side, target in enumerate((to_left, to_right)):
            target[group, SENT - 1] = jnp.where(
                lane < HALF, halves[side, 0], pltpu.roll(halves[side, 1], HALF, 1)
            )
        own_edges[group] = edge

    edge_copy = pltpu.make_async_remote_copy(
        src_ref=edges_out, dst_ref=edges_in,
        send_sem=edge_sem.at[0], recv_sem=edge_sem.at[1],
        device_id={"chain": lax.rem(me + chain - 1, chain)}, device_id_type=MESH,
    )

    def send_edges():
        for index in range(groups // 2):
            edges_out[index] = jnp.where(
                spot < EDGE_STEP, own_edges[2 * index], pltpu.roll(own_edges[2 * index + 1], EDGE_STEP, 1)
            )

        @pl.when(has_left)
        def _():
            edge_copy.start()

    def receive_edges():
        @pl.when(has_right)
        def _():
            edge_copy.wait_recv()

        for group in range(groups):
            value = edges_in[group // 2]
            for at in range(EDGE_STEP):
                back = EDGE_STEP * (group % 2) + at
                edges[group, at] = pltpu.roll(value, BLOCK - back, 1) if back else value

    right_relays, left_relays = relays

    def to_relay(group, source, send_sem, through):
        return pltpu.make_async_remote_copy(
            src_ref=source.at[group], dst_ref=relay.at[group],
            send_sem=send_sem.at[group], recv_sem=relay_recv.at[group],
            device_id={"chain": jnp.int32(through)}, device_id_type=MESH,
        )

    def onward(group, landing, recv_sem, target):
        return pltpu.make_async_remote_copy(
            src_ref=relay.at[group], dst_ref=landing.at[group],
            send_sem=relay_send.at[group], recv_sem=recv_sem.at[group],
            device_id={"chain": jnp.int32(target)}, device_id_type=MESH,
        )

    def send(group, direct, wanted, among, routes, source, send_sem):
        group = jnp.int32(group)
        relayed = functools.reduce(jnp.logical_or, [group == index for index in among])
        for start, (through, _) in routes.items():
            wanted = wanted & ((me != start) | jnp.logical_not(relayed))

            @pl.when((me == start) & relayed)
            def _():
                to_relay(group, source, send_sem, through).start()

        @pl.when(wanted)
        def _():
            direct(group).start()

    def send_both(group):
        send(group, leftward, has_left, RELAYED_LEFT, left_relays, to_left, left_send)
        send(group, rightward, has_right, RELAYED_RIGHT, right_relays, to_right, right_send)

    def pack_next(group, carry):
        pack(group)
        return carry

    def send_next(group, carry):
        send_both(group)
        return carry

    pack(0)
    pl.semaphore_wait(barrier, jnp.where(leads, chain - 1 + cross - 1, chain - 1))
    send_both(0)

    @pl.when(leads)
    def _():
        for step in range(1, cross):
            peer = lax.rem(plane + step, cross)
            pl.semaphore_signal(ready_sem, inc=1, device_id={"cross": peer}, device_id_type=MESH)

    for copy in rest:
        copy.wait()
    send_sums()
    pack(1)
    send_both(1)
    lax.fori_loop(2, groups, pack_next, 0)
    send_edges()
    lax.fori_loop(2, groups, send_next, 0)

    part_copies = [
        pltpu.make_async_remote_copy(
            src_ref=parts.at[plane], dst_ref=parts.at[plane],
            send_sem=part_send.at[step], recv_sem=part_recv.at[step],
            device_id={"cross": lax.rem(plane + step, cross)}, device_id_type=MESH,
        )
        for step in range(1, cross)
    ]

    def open_planes():
        @pl.when(leads)
        def _():
            pl.semaphore_wait(ready_sem, cross - 1)
            for peer in range(1, chain):
                pl.semaphore_signal(open_sem, inc=1, device_id={"chain": jnp.int32(peer)}, device_id_type=MESH)

    def send_parts():
        @pl.when(jnp.logical_not(leads))
        def _():
            pl.semaphore_wait(open_sem, 1)

        for copy in part_copies:
            copy.start()

    def pass_on(index):
        for among, routes, source, send_sem, landing, recv_sem in (
            (RELAYED_RIGHT, right_relays, to_right, right_send, from_left, right_recv),
            (RELAYED_LEFT, left_relays, to_left, left_send, from_right, left_recv),
        ):
            for through, target in routes.values():
                if index >= len(among):
                    continue
                group = among[index]

                @pl.when(me == through)
                def _():
                    to_relay(group, source, send_sem, through).wait_recv()
                    onward(group, landing, recv_sem, target).start()

    shift_row = shifts[...]

    def reduce_chain():
        starts[...] = jnp.zeros_like(starts)
        for copy in sum_copies:
            copy.wait_recv()
        before = jnp.zeros((8, pencils), jnp.float32)
        whole = jnp.zeros((8, pencils), jnp.float32)
        for index in range(chain):
            value = sums[index]
            before = before + jnp.where(index < me, value, 0.0)
            whole = whole + value

        parts[plane] = jnp.broadcast_to(jnp.sum(whole, axis=1, keepdims=True), (8, BLOCK))
        starts[0:8, :] = before
        starts[8:16, :] = before + jnp.where(shift_row >= 0, sums[me], 0.0)

    def spread_starts():
        turned = jnp.transpose(starts[...])
        for var in range(VARS):
            base[var] = base[var] + turned[:, var : var + 1]
            beyond[var] = jnp.broadcast_to(turned[:, 8 + var : 9 + var], (pencils, BLOCK))

    pass_on(0)

    @pl.when(me == 0)
    def _():
        from_left[...] = jnp.zeros_like(from_left)

    @pl.when(me == chain - 1)
    def _():
        from_right[...] = jnp.zeros_like(from_right)
        edges_in[...] = jnp.zeros_like(edges_in)

    f = fraction[...]
    first = interval_integrals(-1.0 + 0.0 * f, 1.0 - 2.0 * f, 2.0 * f)
    second = interval_integrals(1.0 - 2.0 * f, 1.0 + 0.0 * f, 2.0 * f - 2.0)
    raw[...] = jnp.zeros_like(raw)
    columns = partial_weights(f) + first + second + [shift_row.astype(jnp.float32)]
    for index, value in enumerate(columns):
        raw[index : index + 1, :] = value
    turned = jnp.transpose(raw[...])
    for index in range(COEFS):
        coef[index] = jnp.broadcast_to(turned[:, index : index + 1], (pencils, BLOCK))
    shift_of[...] = jnp.broadcast_to(turned[:, COEFS : COEFS + 1], (pencils, BLOCK)).astype(jnp.int32)

    pass_on(1)
    up_to_edge = jnp.where(source_cell < BLOCK // 2, before_cell, 1.0 - before_cell)
    triangle[...] = up_to_edge.astype(jnp.bfloat16)
    pass_on(2)
    pass_on(3)
    pass_on(4)
    reduce_chain()
    open_planes()
    spread_starts()
    send_parts()
    receive_edges()


    held = moments, from_left, from_right, edges, coef, shift_of, base, beyond, triangle

    def receive(group):
        @pl.when(has_right)
        def _():
            leftward(group).wait_recv()

        @pl.when(has_left)
        def _():
            rightward(group).wait_recv()

    def remap(group, carry):
        receive(group)
        finish_group(group, held, remapped, mass, 0)
        return carry

    lax.fori_loop(0, groups - 1, remap, 0)

    for copy in part_copies:
        copy.wait_recv()
    grand = parts[0]
    for index in range(1, cross):
        grand = grand + parts[index]
    mean = grand / float(pencils * cross)
    mean_of[...] = mean
    done = pl.ds(0, pencils - GROUP)
    for var in range(VARS):
        mass[var, done, :] = mass[var, done, :] / mean[var : var + 1, :]
    receive(groups - 1)

    for copy in sum_copies + part_copies:
        copy.wait_send()

    for among, routes, landing, recv_sem in (
        (RELAYED_RIGHT, right_relays, from_left, right_recv), (RELAYED_LEFT, left_relays, from_right, left_recv)
    ):
        for through, target in routes.values():

            @pl.when(me == through)
            def _():
                for group in among:
                    onward(group, landing, recv_sem, target).wait_send()

    @pl.when(has_left)
    def _():
        edge_copy.wait_send()
        for group in range(groups):
            leftward(group).wait_send()

    @pl.when(has_right)
    def _():
        for group in range(groups):
            rightward(group).wait_send()


def deliver(
    remapped, mass, moments, from_left, from_right, edges, coef, shift_of, base, beyond, triangle, mean_of,
    remapped_out, mass_out,
    last_remapped, last_mass, sem,
):
    done = remapped.shape[1] - GROUP
    early, late = pl.ds(0, done), pl.ds(done, GROUP)
    held = moments, from_left, from_right, edges, coef, shift_of, base, beyond, triangle
    copies = [
        pltpu.make_async_copy(source, target, sem.at[index])
        for index, (source, target) in enumerate((
            (remapped.at[:, early, :], remapped_out.at[:, early, :]),
            (mass.at[:, early, :], mass_out.at[:, early, :]),
            (last_remapped, remapped_out.at[:, late, :]),
            (last_mass, mass_out.at[:, late, :]),
        ))
    ]
    for copy in copies[:2]:
        copy.start()
    finish_group(done // GROUP, held, last_remapped, last_mass, done)
    for var in range(VARS):
        last_mass[var] = last_mass[var] / mean_of[var : var + 1, :]
    for copy in copies[2:]:
        copy.start()
    for copy in copies:
        copy.wait()


def solution(mesh):
    chain, cross = mesh.shape["chain"], mesh.shape["cross"]
    relays = corner_relays(mesh)

    def shards(moments, flags, shifts, fraction):
        row_count, pencils, cells = moments.shape
        assert row_count == ROWS and cells == BLOCK and pencils == BLOCK
        groups = pencils // GROUP
        dma = pltpu.SemaphoreType.DMA
        float_of = functools.partial(jax.ShapeDtypeStruct, dtype=jnp.float32)
        halo = (groups, SENT, TILE, BLOCK)
        block = pltpu.VMEM(halo, jnp.float32)
        results = float_of(moments.shape), float_of((VARS, pencils, cells))
        handed = results + (
            float_of(moments.shape), float_of(halo), float_of(halo), float_of((groups, EDGE_STEP, TILE, BLOCK)),
            float_of((COEFS, pencils, BLOCK)), jax.ShapeDtypeStruct((pencils, BLOCK), jnp.int32),
            float_of((VARS, pencils, BLOCK)), float_of((VARS, pencils, BLOCK)),
            jax.ShapeDtypeStruct((BLOCK, BLOCK), jnp.bfloat16), float_of((8, BLOCK)),
        )
        in_vmem = pl.BlockSpec(memory_space=pltpu.VMEM)
        in_hbm = pl.BlockSpec(memory_space=pltpu.HBM)
        ready = pl.pallas_call(
            functools.partial(kernel, chain, cross, relays),
            out_shape=handed,
            in_specs=[in_hbm] * 4,
            out_specs=(in_vmem,) * len(handed),
            scratch_shapes=[
                pltpu.VMEM(flags.shape, jnp.int32),
                pltpu.VMEM((1, pencils), jnp.int32),
                pltpu.VMEM((1, pencils), jnp.float32),
                block, block, block,
                pltpu.VMEM((groups, TILE, BLOCK), jnp.float32),
                pltpu.VMEM((groups // 2, TILE, BLOCK), jnp.float32),
                pltpu.VMEM((groups // 2, TILE, BLOCK), jnp.float32),
                pltpu.VMEM((chain, 8, pencils), jnp.float32),
                pltpu.VMEM((cross, 8, BLOCK), jnp.float32),
                pltpu.VMEM((BLOCK, pencils), jnp.float32),
                pltpu.VMEM((BLOCK, pencils), jnp.float32),
                dma((groups,)), dma((groups,)), dma((groups,)), dma((groups,)),
                dma((groups,)), dma((groups,)),
                dma((chain,)), dma((chain,)), dma((cross,)), dma((cross,)),
                pltpu.SemaphoreType.REGULAR, pltpu.SemaphoreType.REGULAR, dma((2,)), dma((5,)),
            ],
            compiler_params=pltpu.CompilerParams(
                collective_id=0, has_side_effects=True, vmem_limit_bytes=24 << 20
            ),
        )(*(
            pltpu.with_memory_space_constraint(value, pltpu.HBM)
            for value in (moments, flags, shifts.T, fraction.reshape(1, pencils))
        ))
        return pl.pallas_call(
            deliver,
            out_shape=results,
            in_specs=[in_vmem] * len(handed),
            out_specs=(in_hbm,) * 2,
            scratch_shapes=[
                pltpu.VMEM((ROWS, GROUP, BLOCK), jnp.float32),
                pltpu.VMEM((VARS, GROUP, BLOCK), jnp.float32),
                dma((4,)),
            ],
            compiler_params=pltpu.CompilerParams(vmem_limit_bytes=16 << 20),
        )(*ready)

    in_specs = (P(None, "cross", "chain"), P("cross", "chain"), P("cross", "chain"), P("cross"))
    out_specs = (P(None, "cross", "chain"), P(None, "cross", "chain"))
    return jax.shard_map(shards, mesh=mesh, in_specs=in_specs, out_specs=out_specs, check_vma=False)
```

```python
import functools

import jax
import numpy as np
import jax.numpy as jnp
from jax import lax
from jax.experimental import pallas as pl
from jax.experimental.pallas import tpu as pltpu
from jax.sharding import PartitionSpec as P

VARS = 5
MOMENTS = 4
BLOCK = 128
SHIFT_MAX = 48
ROWS = VARS * MOMENTS
SPAN = ROWS * SHIFT_MAX
FULL, HALF = SPAN // BLOCK, BLOCK // 2
TILE = 8
TILES = 2
GROUP = TILES * TILE
SENT = TILES * FULL + 1
EDGES = -(-ROWS // 8)
EDGE_STEP = TILES * EDGES
LATE = 2
RELAYED_RIGHT, RELAYED_LEFT = (1, 3, 5, 7), (1, 3, 5)
PAIRS = tuple((k, m) for k in range(1, MOMENTS) for m in range(k, MOMENTS))
COEFS = MOMENTS + 2 * len(PAIRS)
MESH = pl.DeviceIdType.MESH
HIGHEST = lax.Precision.HIGHEST

gauss_nodes = (-0.8611363115940526, -0.3399810435848563, 0.3399810435848563, 0.8611363115940526)
gauss_weights = (0.3478548451374538, 0.6521451548625461, 0.6521451548625461, 0.3478548451374538)


AFTER_FIRST, AFTER_LENGTH = SHIFT_MAX, SHIFT_MAX + 1
BEFORE_FIRST, BEFORE_LENGTH = 0, SHIFT_MAX


def place(row, first):
    chunk, lane = divmod((first + SHIFT_MAX * row) % SPAN, BLOCK)
    return chunk, lane, lane + SHIFT_MAX > BLOCK


def segments(first):
    held = [[] for _ in range(FULL + 1)]
    for row in range(ROWS):
        chunk, lane, splits = place(row, first)
        held[chunk].append((lane, row))
        if splits:
            held[chunk + 1].append((0, row))
    return [sorted(chunk) for chunk in held]


AFTER, BEFORE = segments(AFTER_FIRST), segments(BEFORE_FIRST)
WRAPPED = ROWS - 1


def turn_of(row):
    return (SHIFT_MAX * (row + 1)) % BLOCK


def edge_lane(row):
    return (turn_of(row) + SHIFT_MAX) % BLOCK


def legendre_values(point):
    return [
        jnp.ones_like(point),
        point,
        0.5 * (3.0 * point * point - 1.0),
        0.5 * (5.0 * point * point * point - 3.0 * point),
    ]


def interval_integrals(low_end, high_end, offset):
    half = 0.5 * (high_end - low_end)
    middle = 0.5 * (high_end + low_end)
    entries = [jnp.zeros_like(low_end) for _ in PAIRS]
    for node, weight in zip(gauss_nodes, gauss_weights):
        point = middle + half * node
        target = legendre_values(point)
        source = legendre_values(point + offset)
        scaled = [weight * half * value for value in target]
        for index, (k, m) in enumerate(PAIRS):
            entries[index] = entries[index] + scaled[k] * source[m]
    return entries


def partial_weights(fraction):
    shifted = 2.0 * fraction - 1.0
    square = shifted * shifted
    return [
        fraction,
        fraction * fraction - fraction,
        0.25 * (square * shifted - shifted),
        0.5 * (0.5 * (1.25 * square * square - 1.5 * square) + 0.125),
    ]


def corner_relays(mesh):
    ring = np.moveaxis(mesh.devices, mesh.axis_names.index("chain"), 0).reshape(mesh.shape["chain"], -1)[:, 0]
    if any(getattr(device, "coords", None) is None for device in ring):
        return {}, {}
    spots = [tuple(device.coords) for device in ring]
    rightward, leftward = {}, {}
    if len({spot[0] for spot in spots}) == 2 and len({spot[1] for spot in spots}) == 2:
        for index in range(len(spots) - 1):
            low, high = spots[index], spots[index + 1]
            if low[0] != high[0] and low[1] != high[1]:
                for found, source, target, pick in (
                    (rightward, index, index + 1, max), (leftward, index + 1, index, max)
                ):
                    corner = (spots[source][0], spots[target][1])
                    at = [i for i, spot in enumerate(spots) if spot[:2] == corner]
                    if at:
                        found[source] = (pick(at), target)
    return rightward, leftward


def exact_dot(value, ones):
    high = value.astype(jnp.bfloat16)
    rest = value - high.astype(jnp.float32)
    middle = rest.astype(jnp.bfloat16)
    low = (rest - middle.astype(jnp.float32)).astype(jnp.bfloat16)
    return sum(jnp.dot(part, ones, preferred_element_type=jnp.float32) for part in (low, middle, high))


def finish_group(group, held, remapped, mass, skipped):
    moments, from_left, from_right, edges, coef, shift_of, base, beyond, triangle = held
    lane = lax.broadcasted_iota(jnp.int32, (TILE, BLOCK), 1)
    halos, places_of = [], []
    for tile in range(GROUP // TILE):
        rows = pl.ds(pl.multiple_of(group * GROUP + tile * TILE, TILE), TILE)
        inner = pl.ds(tile * TILE, TILE)
        shift = shift_of[rows, :]
        ahead = shift >= 0
        put = pl.ds(pl.multiple_of(group * GROUP + tile * TILE - skipped, TILE), TILE)
        places_of.append((rows, put, shift, ahead))

        folded = {}
        for name, ref in (("right", from_right), ("left", from_left)):
            value = ref[group, SENT - 1]
            folded[name] = pltpu.roll(value, HALF, 1) if tile else value

        def fetch(name, ref, row, first):
            chunk, start, splits = place(row, first)
            values = [
                ref[group, TILES * index + tile] if index < FULL else folded[name]
                for index in ((chunk, chunk + 1) if splits else (chunk,))
            ]
            return jnp.where(lane >= start, *values) if splits else values[0]

        def halo_row(row):
            right = fetch("right", from_right, row, AFTER_FIRST)
            left = fetch("left", from_left, row, BEFORE_FIRST)
            edge = edges[group, EDGES * tile + row // 8]
            wrapped = row == WRAPPED
            value = left if wrapped else jnp.where(ahead, right, left)
            value = jnp.where(ahead & (lane == edge_lane(row)), edge, value)
            value = pltpu.roll(value, (BLOCK - turn_of(row)) % BLOCK, 1) if turn_of(row) else value
            return jnp.where(ahead & (lane < SHIFT_MAX), right, value) if wrapped else value

        halos.append([halo_row(row) for row in range(ROWS)])

    signed = []
    for (_, _, _, ahead), halo in zip(places_of, halos):
        for var in range(VARS):
            value = halo[MOMENTS * var]
            signed.append(jnp.where(
                ahead,
                jnp.where(lane < AFTER_LENGTH, value, 0.0),
                jnp.where(lane >= BLOCK - BEFORE_LENGTH, -value, 0.0),
            ))
    crossed = exact_dot(jnp.concatenate(signed, axis=0), triangle[...])

    for tile, ((rows, put, shift, ahead), halo) in enumerate(zip(places_of, halos)):
        turn = shift & (BLOCK - 1)
        outside = jnp.where(ahead, lane - turn, turn - 1 - lane) < 0
        outside_next = jnp.where(ahead, lane - turn - 1, turn - lane) < 0
        at = (lane + turn) & (BLOCK - 1)
        weight = [coef[m, rows, :] for m in range(MOMENTS)]
        inside, across = {}, {}
        for index, (k, m) in enumerate(PAIRS):
            inside[k, m] = coef[MOMENTS + index, rows, :]
            across[k, m] = coef[MOMENTS + len(PAIRS) + index, rows, :]

        def settle(value):
            return jnp.take_along_axis(value, at, axis=1, mode="promise_in_bounds")

        for var in range(VARS):
            here, after = [], []
            for order in range(MOMENTS):
                own = moments[MOMENTS * var + order, rows, :]
                other = halo[MOMENTS * var + order]
                here.append(jnp.where(outside, other, own))
                after.append(pltpu.roll(jnp.where(outside_next, other, own), BLOCK - 1, 1))
            filled = weight[0] * here[0]
            filled_after = weight[0] * after[0]
            for m in range(1, MOMENTS):
                filled = filled + weight[m] * here[m]
                filled_after = filled_after + weight[m] * after[m]
            rise = after[0] - here[0]
            remapped[MOMENTS * var, put, :] = settle(here[0] + (filled_after - filled))
            for k in range(1, MOMENTS):
                value = inside[k, k] * here[k] + across[k, k] * after[k]
                for m in range(1, MOMENTS):
                    if m == k:
                        continue
                    pair = (min(k, m), max(k, m))
                    term = inside[pair] * here[m] + across[pair] * after[m]
                    value = value - term if k > m and (k + m) % 2 else value + term
                edge = (2.0 if k % 2 == 0 else -2.0) * (weight[k] * rise)
                remapped[MOMENTS * var + k, put, :] = settle((k + 0.5) * (value + edge))
            index = (tile * VARS + var) * TILE
            start = jnp.where(
                outside, crossed[index : index + TILE] + beyond[var, rows, :], base[var, rows, :]
            )
            mass[var, put, :] = settle(start + filled)


def kernel(
    chain, cross, relays,
    moments_in, flags_in, shifts_in, fraction_in,
    remapped, mass, moments, from_left, from_right, edges, coef, shift_of, base, beyond, triangle, mean_of,
    flags, shifts, fraction,
    to_left, to_right, relay, own_edges, edges_out, edges_in,
    sums, parts, raw, starts,
    left_send, left_recv, right_send, right_recv, relay_send, relay_recv,
    sum_send, sum_recv, part_send, part_recv, ready_sem, open_sem, edge_sem, input_sem,
):
    pencils = moments.shape[1]
    groups = pencils // GROUP
    me = lax.axis_index("chain")
    plane = lax.axis_index("cross")

    first_rows, later_rows = pl.ds(0, GROUP), pl.ds(GROUP, pencils - GROUP)
    inputs = [
        pltpu.make_async_copy(source, target, input_sem.at[index])
        for index, (source, target) in enumerate((
            (flags_in, flags),
            (moments_in.at[:, first_rows, :], moments.at[:, first_rows, :]),
            (moments_in.at[:, later_rows, :], moments.at[:, later_rows, :]),
            (shifts_in, shifts),
            (fraction_in, fraction),
        ))
    ]
    urgent, rest = inputs[:2], inputs[2:]
    for copy in urgent:
        copy.start()

    barrier = pltpu.get_barrier_semaphore()
    for step in range(1, chain):
        peer = lax.rem(me + step, chain)
        pl.semaphore_signal(barrier, inc=1, device_id={"chain": peer}, device_id_type=MESH)
    leads = me == 0

    @pl.when(leads)
    def _():
        for step in range(1, cross):
            peer = lax.rem(plane + step, cross)
            pl.semaphore_signal(barrier, inc=1, device_id={"cross": peer}, device_id_type=MESH)

    for copy in rest:
        copy.start()
    for copy in urgent:
        copy.wait()

    def leftward(group):
        return pltpu.make_async_remote_copy(
            src_ref=to_left.at[group], dst_ref=from_right.at[group],
            send_sem=left_send.at[group], recv_sem=left_recv.at[group],
            device_id={"chain": lax.rem(me + chain - 1, chain)}, device_id_type=MESH,
        )

    def rightward(group):
        return pltpu.make_async_remote_copy(
            src_ref=to_right.at[group], dst_ref=from_left.at[group],
            send_sem=right_send.at[group], recv_sem=right_recv.at[group],
            device_id={"chain": lax.rem(me + 1, chain)}, device_id_type=MESH,
        )

    has_left, has_right = me > 0, me < chain - 1

    sum_copies = [
        pltpu.make_async_remote_copy(
            src_ref=sums.at[me], dst_ref=sums.at[me],
            send_sem=sum_send.at[step], recv_sem=sum_recv.at[step],
            device_id={"chain": lax.rem(me + step, chain)}, device_id_type=MESH,
        )
        for step in range(1, chain)
    ]

    source_cell = lax.broadcasted_iota(jnp.int32, (BLOCK, BLOCK), 0)
    target_cell = lax.broadcasted_iota(jnp.int32, (BLOCK, BLOCK), 1)
    before_cell = jnp.where(source_cell < target_cell, 1.0, 0.0)

    def own_sums():
        total = jnp.zeros((pencils, BLOCK), jnp.float32)
        for var in range(VARS):
            pick = jnp.where(target_cell == var, 1.0, 0.0)
            both = jnp.concatenate([before_cell, pick], axis=1).astype(jnp.bfloat16)
            summed = exact_dot(moments[MOMENTS * var], both)
            base[var] = summed[:, :BLOCK]
            total = total + summed[:, BLOCK:]
        sums[me] = jnp.transpose(total)[:8]

    def send_sums():
        for copy in sum_copies:
            copy.start()

    lane = lax.broadcasted_iota(jnp.int32, (TILE, BLOCK), 1)
    spot = lane & 15

    def pack(group):
        halves = {}
        edge = None
        for tile in range(TILES):
            rows = pl.ds(pl.multiple_of(group * GROUP + tile * TILE, TILE), TILE)
            flag = flags[rows, :]
            keep_linear, keep_full = flag <= 1, flag == 0
            rolled = []
            for row in range(ROWS):
                value = moments[row, rows, :]
                order = row % MOMENTS
                if order > 0:
                    value = jnp.where(keep_linear if order == 1 else keep_full, value, 0.0)
                    moments[row, rows, :] = value
                rolled.append(pltpu.roll(value, turn_of(row), 1) if turn_of(row) else value)
            for side, (held, target) in enumerate(((AFTER, to_left), (BEFORE, to_right))):
                for chunk in range(FULL + 1):
                    value = None
                    for start, row in held[chunk]:
                        part = moments[row, rows, :] if row == WRAPPED and side == 0 else rolled[row]
                        value = part if value is None else jnp.where(lane >= start, part, value)
                    if chunk < FULL:
                        target[group, TILES * chunk + tile] = value
                    else:
                        halves[side, tile] = value
            for index in range(EDGES):
                value = None
                for row in range(8 * index, min(8 * index + 8, ROWS)):
                    here = (lane >> 4) == edge_lane(row) // 16
                    value = rolled[row] if value is None else jnp.where(here, rolled[row], value)
                at = EDGES * tile + index
                value = pltpu.roll(value, at, 1) if at else value
                edge = value if edge is None else jnp.where(spot >= at, value, edge)
        for side, target in enumerate((to_left, to_right)):
            target[group, SENT - 1] = jnp.where(
                lane < HALF, halves[side, 0], pltpu.roll(halves[side, 1], HALF, 1)
            )
        own_edges[group] = edge

    edge_copy = pltpu.make_async_remote_copy(
        src_ref=edges_out, dst_ref=edges_in,
        send_sem=edge_sem.at[0], recv_sem=edge_sem.at[1],
        device_id={"chain": lax.rem(me + chain - 1, chain)}, device_id_type=MESH,
    )

    def send_edges():
        for index in range(groups // 2):
            edges_out[index] = jnp.where(
                spot < EDGE_STEP, own_edges[2 * index], pltpu.roll(own_edges[2 * index + 1], EDGE_STEP, 1)
            )

        @pl.when(has_left)
        def _():
            edge_copy.start()

    def receive_edges():
        @pl.when(has_right)
        def _():
            edge_copy.wait_recv()

        for group in range(groups):
            value = edges_in[group // 2]
            for at in range(EDGE_STEP):
                back = EDGE_STEP * (group % 2) + at
                edges[group, at] = pltpu.roll(value, BLOCK - back, 1) if back else value

    right_relays, left_relays = relays

    def to_relay(group, source, send_sem, through):
        return pltpu.make_async_remote_copy(
            src_ref=source.at[group], dst_ref=relay.at[group],
            send_sem=send_sem.at[group], recv_sem=relay_recv.at[group],
            device_id={"chain": jnp.int32(through)}, device_id_type=MESH,
        )

    def onward(group, landing, recv_sem, target):
        return pltpu.make_async_remote_copy(
            src_ref=relay.at[group], dst_ref=landing.at[group],
            send_sem=relay_send.at[group], recv_sem=recv_sem.at[group],
            device_id={"chain": jnp.int32(target)}, device_id_type=MESH,
        )

    def send(group, direct, wanted, among, routes, source, send_sem):
        group = jnp.int32(group)
        relayed = functools.reduce(jnp.logical_or, [group == index for index in among])
        for start, (through, _) in routes.items():
            wanted = wanted & ((me != start) | jnp.logical_not(relayed))

            @pl.when((me == start) & relayed)
            def _():
                to_relay(group, source, send_sem, through).start()

        if direct is rightward:
            for start in routes:
                wanted = wanted & ((me != start) | (group < LATE))

        @pl.when(wanted)
        def _():
            direct(group).start()

    def send_late():
        for start in right_relays:

            @pl.when(me == start)
            def _():
                for group in range(groups):
                    if group >= LATE and group not in RELAYED_RIGHT:
                        rightward(group).start()

    def send_both(group):
        send(group, leftward, has_left, RELAYED_LEFT, left_relays, to_left, left_send)
        send(group, rightward, has_right, RELAYED_RIGHT, right_relays, to_right, right_send)

    def pack_next(group, carry):
        pack(group)
        return carry

    def send_next(group, carry):
        send_both(group)
        return carry

    pack(0)
    soon = lax.rem(me, 2) == 1
    soon = soon | (me == 0)

    @pl.when(soon)
    def _():
        for copy in rest:
            copy.wait()
        own_sums()

    pl.semaphore_wait(barrier, jnp.where(leads, chain - 1 + cross - 1, chain - 1))
    send_both(0)

    @pl.when(leads)
    def _():
        for step in range(1, cross):
            peer = lax.rem(plane + step, cross)
            pl.semaphore_signal(ready_sem, inc=1, device_id={"cross": peer}, device_id_type=MESH)

    @pl.when(jnp.logical_not(soon))
    def _():
        for copy in rest:
            copy.wait()
        own_sums()

    send_sums()
    pack(1)
    send_both(1)
    lax.fori_loop(2, groups, pack_next, 0)
    send_edges()
    lax.fori_loop(2, groups, send_next, 0)

    part_copies = [
        pltpu.make_async_remote_copy(
            src_ref=parts.at[plane], dst_ref=parts.at[plane],
            send_sem=part_send.at[step], recv_sem=part_recv.at[step],
            device_id={"cross": lax.rem(plane + step, cross)}, device_id_type=MESH,
        )
        for step in range(1, cross)
    ]

    def open_planes():
        @pl.when(leads)
        def _():
            pl.semaphore_wait(ready_sem, cross - 1)
            for peer in range(1, chain):
                pl.semaphore_signal(open_sem, inc=1, device_id={"chain": jnp.int32(peer)}, device_id_type=MESH)

    def send_parts():
        @pl.when(jnp.logical_not(leads))
        def _():
            pl.semaphore_wait(open_sem, 1)

        for copy in part_copies:
            copy.start()

    def pass_on(index):
        for among, routes, source, send_sem, landing, recv_sem in (
            (RELAYED_RIGHT, right_relays, to_right, right_send, from_left, right_recv),
            (RELAYED_LEFT, left_relays, to_left, left_send, from_right, left_recv),
        ):
            for through, target in routes.values():
                if index >= len(among):
                    continue
                group = among[index]

                @pl.when(me == through)
                def _():
                    to_relay(group, source, send_sem, through).wait_recv()
                    onward(group, landing, recv_sem, target).start()

    shift_row = shifts[...]

    def reduce_chain():
        starts[...] = jnp.zeros_like(starts)
        for copy in sum_copies:
            copy.wait_recv()
        before = jnp.zeros((8, pencils), jnp.float32)
        whole = jnp.zeros((8, pencils), jnp.float32)
        for index in range(chain):
            value = sums[index]
            before = before + jnp.where(index < me, value, 0.0)
            whole = whole + value

        parts[plane] = jnp.broadcast_to(jnp.sum(whole, axis=1, keepdims=True), (8, BLOCK))
        starts[0:8, :] = before
        starts[8:16, :] = before + jnp.where(shift_row >= 0, sums[me], 0.0)

    def spread_starts():
        turned = jnp.transpose(starts[...])
        for var in range(VARS):
            base[var] = base[var] + turned[:, var : var + 1]
            beyond[var] = jnp.broadcast_to(turned[:, 8 + var : 9 + var], (pencils, BLOCK))

    open_planes()
    pass_on(0)
    pass_on(1)
    reduce_chain()
    send_parts()

    send_late()
    @pl.when(me == 0)
    def _():
        from_left[...] = jnp.zeros_like(from_left)

    @pl.when(me == chain - 1)
    def _():
        from_right[...] = jnp.zeros_like(from_right)
        edges_in[...] = jnp.zeros_like(edges_in)

    f = fraction[...]
    first = interval_integrals(-1.0 + 0.0 * f, 1.0 - 2.0 * f, 2.0 * f)
    second = interval_integrals(1.0 - 2.0 * f, 1.0 + 0.0 * f, 2.0 * f - 2.0)
    raw[...] = jnp.zeros_like(raw)
    columns = partial_weights(f) + first + second + [shift_row.astype(jnp.float32)]
    for index, value in enumerate(columns):
        raw[index : index + 1, :] = value
    turned = jnp.transpose(raw[...])
    for index in range(COEFS):
        coef[index] = jnp.broadcast_to(turned[:, index : index + 1], (pencils, BLOCK))
    shift_of[...] = jnp.broadcast_to(turned[:, COEFS : COEFS + 1], (pencils, BLOCK)).astype(jnp.int32)

    up_to_edge = jnp.where(source_cell < BLOCK // 2, before_cell, 1.0 - before_cell)
    triangle[...] = up_to_edge.astype(jnp.bfloat16)
    pass_on(2)
    pass_on(3)
    pass_on(4)
    spread_starts()
    receive_edges()


    held = moments, from_left, from_right, edges, coef, shift_of, base, beyond, triangle

    def receive(group):
        @pl.when(has_right)
        def _():
            leftward(group).wait_recv()

        @pl.when(has_left)
        def _():
            rightward(group).wait_recv()

    def remap(group, carry):
        receive(group)
        finish_group(group, held, remapped, mass, 0)
        return carry

    lax.fori_loop(0, groups - 1, remap, 0)

    for copy in part_copies:
        copy.wait_recv()
    grand = parts[0]
    for index in range(1, cross):
        grand = grand + parts[index]
    mean = grand / float(pencils * cross)
    mean_of[...] = mean
    done = pl.ds(0, pencils - GROUP)
    for var in range(VARS):
        mass[var, done, :] = mass[var, done, :] / mean[var : var + 1, :]
    receive(groups - 1)

    for copy in sum_copies + part_copies:
        copy.wait_send()

    for among, routes, landing, recv_sem in (
        (RELAYED_RIGHT, right_relays, from_left, right_recv), (RELAYED_LEFT, left_relays, from_right, left_recv)
    ):
        for through, target in routes.values():

            @pl.when(me == through)
            def _():
                for group in among:
                    onward(group, landing, recv_sem, target).wait_send()

    @pl.when(has_left)
    def _():
        edge_copy.wait_send()
        for group in range(groups):
            leftward(group).wait_send()

    @pl.when(has_right)
    def _():
        for group in range(groups):
            rightward(group).wait_send()


def deliver(
    remapped, mass, moments, from_left, from_right, edges, coef, shift_of, base, beyond, triangle, mean_of,
    remapped_out, mass_out,
    last_remapped, last_mass, sem,
):
    done = remapped.shape[1] - GROUP
    early, late = pl.ds(0, done), pl.ds(done, GROUP)
    held = moments, from_left, from_right, edges, coef, shift_of, base, beyond, triangle
    copies = [
        pltpu.make_async_copy(source, target, sem.at[index])
        for index, (source, target) in enumerate((
            (remapped.at[:, early, :], remapped_out.at[:, early, :]),
            (mass.at[:, early, :], mass_out.at[:, early, :]),
            (last_remapped, remapped_out.at[:, late, :]),
            (last_mass, mass_out.at[:, late, :]),
        ))
    ]
    for copy in copies[:2]:
        copy.start()
    finish_group(done // GROUP, held, last_remapped, last_mass, done)
    for var in range(VARS):
        last_mass[var] = last_mass[var] / mean_of[var : var + 1, :]
    for copy in copies[2:]:
        copy.start()
    for copy in copies:
        copy.wait()


def solution(mesh):
    chain, cross = mesh.shape["chain"], mesh.shape["cross"]
    relays = corner_relays(mesh)

    def shards(moments, flags, shifts, fraction):
        row_count, pencils, cells = moments.shape
        assert row_count == ROWS and cells == BLOCK and pencils == BLOCK
        groups = pencils // GROUP
        dma = pltpu.SemaphoreType.DMA
        float_of = functools.partial(jax.ShapeDtypeStruct, dtype=jnp.float32)
        halo = (groups, SENT, TILE, BLOCK)
        block = pltpu.VMEM(halo, jnp.float32)
        results = float_of(moments.shape), float_of((VARS, pencils, cells))
        handed = results + (
            float_of(moments.shape), float_of(halo), float_of(halo), float_of((groups, EDGE_STEP, TILE, BLOCK)),
            float_of((COEFS, pencils, BLOCK)), jax.ShapeDtypeStruct((pencils, BLOCK), jnp.int32),
            float_of((VARS, pencils, BLOCK)), float_of((VARS, pencils, BLOCK)),
            jax.ShapeDtypeStruct((BLOCK, BLOCK), jnp.bfloat16), float_of((8, BLOCK)),
        )
        in_vmem = pl.BlockSpec(memory_space=pltpu.VMEM)
        in_hbm = pl.BlockSpec(memory_space=pltpu.HBM)
        ready = pl.pallas_call(
            functools.partial(kernel, chain, cross, relays),
            out_shape=handed,
            in_specs=[in_hbm] * 4,
            out_specs=(in_vmem,) * len(handed),
            scratch_shapes=[
                pltpu.VMEM(flags.shape, jnp.int32),
                pltpu.VMEM((1, pencils), jnp.int32),
                pltpu.VMEM((1, pencils), jnp.float32),
                block, block, block,
                pltpu.VMEM((groups, TILE, BLOCK), jnp.float32),
                pltpu.VMEM((groups // 2, TILE, BLOCK), jnp.float32),
                pltpu.VMEM((groups // 2, TILE, BLOCK), jnp.float32),
                pltpu.VMEM((chain, 8, pencils), jnp.float32),
                pltpu.VMEM((cross, 8, BLOCK), jnp.float32),
                pltpu.VMEM((BLOCK, pencils), jnp.float32),
                pltpu.VMEM((BLOCK, pencils), jnp.float32),
                dma((groups,)), dma((groups,)), dma((groups,)), dma((groups,)),
                dma((groups,)), dma((groups,)),
                dma((chain,)), dma((chain,)), dma((cross,)), dma((cross,)),
                pltpu.SemaphoreType.REGULAR, pltpu.SemaphoreType.REGULAR, dma((2,)), dma((5,)),
            ],
            compiler_params=pltpu.CompilerParams(
                collective_id=0, has_side_effects=True, vmem_limit_bytes=24 << 20
            ),
        )(*(
            pltpu.with_memory_space_constraint(value, pltpu.HBM)
            for value in (moments, flags, shifts.T, fraction.reshape(1, pencils))
        ))
        return pl.pallas_call(
            deliver,
            out_shape=results,
            in_specs=[in_vmem] * len(handed),
            out_specs=(in_hbm,) * 2,
            scratch_shapes=[
                pltpu.VMEM((ROWS, GROUP, BLOCK), jnp.float32),
                pltpu.VMEM((VARS, GROUP, BLOCK), jnp.float32),
                dma((4,)),
            ],
            compiler_params=pltpu.CompilerParams(vmem_limit_bytes=16 << 20),
        )(*ready)

    in_specs = (P(None, "cross", "chain"), P("cross", "chain"), P("cross", "chain"), P("cross"))
    out_specs = (P(None, "cross", "chain"), P(None, "cross", "chain"))
    return jax.shard_map(shards, mesh=mesh, in_specs=in_specs, out_specs=out_specs, check_vma=False)
```

```python
import functools

import jax
import numpy as np
import jax.numpy as jnp
from jax import lax
from jax.experimental import pallas as pl
from jax.experimental.pallas import tpu as pltpu
from jax.sharding import PartitionSpec as P

VARS = 5
MOMENTS = 4
BLOCK = 128
SHIFT_MAX = 48
ROWS = VARS * MOMENTS
SPAN = ROWS * SHIFT_MAX
FULL, HALF = SPAN // BLOCK, BLOCK // 2
TILE = 8
TILES = 2
GROUP = TILES * TILE
SENT = TILES * FULL + 1
EDGES = -(-ROWS // 8)
EDGE_STEP = TILES * EDGES
LATE = 2
EARLY = 2
ORDER_RIGHT, ORDER_LEFT = (0, 1, 3, 2, 4, 5, 6), (0, 2, 4, 6, 1, 3, 5)
RELAYED_RIGHT, RELAYED_LEFT = (1, 3, 5, 7), (1, 3, 5)
PAIRS = tuple((k, m) for k in range(1, MOMENTS) for m in range(k, MOMENTS))
COEFS = MOMENTS + 2 * len(PAIRS)
MESH = pl.DeviceIdType.MESH
HIGHEST = lax.Precision.HIGHEST

gauss_nodes = (-0.8611363115940526, -0.3399810435848563, 0.3399810435848563, 0.8611363115940526)
gauss_weights = (0.3478548451374538, 0.6521451548625461, 0.6521451548625461, 0.3478548451374538)


AFTER_FIRST, AFTER_LENGTH = SHIFT_MAX, SHIFT_MAX + 1
BEFORE_FIRST, BEFORE_LENGTH = 0, SHIFT_MAX


def place(row, first):
    chunk, lane = divmod((first + SHIFT_MAX * row) % SPAN, BLOCK)
    return chunk, lane, lane + SHIFT_MAX > BLOCK


def segments(first):
    held = [[] for _ in range(FULL + 1)]
    for row in range(ROWS):
        chunk, lane, splits = place(row, first)
        held[chunk].append((lane, row))
        if splits:
            held[chunk + 1].append((0, row))
    return [sorted(chunk) for chunk in held]


AFTER, BEFORE = segments(AFTER_FIRST), segments(BEFORE_FIRST)
WRAPPED = ROWS - 1


def turn_of(row):
    return (SHIFT_MAX * (row + 1)) % BLOCK


def edge_lane(row):
    return (turn_of(row) + SHIFT_MAX) % BLOCK


def legendre_values(point):
    return [
        jnp.ones_like(point),
        point,
        0.5 * (3.0 * point * point - 1.0),
        0.5 * (5.0 * point * point * point - 3.0 * point),
    ]


def interval_integrals(low_end, high_end, offset):
    half = 0.5 * (high_end - low_end)
    middle = 0.5 * (high_end + low_end)
    entries = [jnp.zeros_like(low_end) for _ in PAIRS]
    for node, weight in zip(gauss_nodes, gauss_weights):
        point = middle + half * node
        target = legendre_values(point)
        source = legendre_values(point + offset)
        scaled = [weight * half * value for value in target]
        for index, (k, m) in enumerate(PAIRS):
            entries[index] = entries[index] + scaled[k] * source[m]
    return entries


def partial_weights(fraction):
    shifted = 2.0 * fraction - 1.0
    square = shifted * shifted
    return [
        fraction,
        fraction * fraction - fraction,
        0.25 * (square * shifted - shifted),
        0.5 * (0.5 * (1.25 * square * square - 1.5 * square) + 0.125),
    ]


def corner_relays(mesh):
    ring = np.moveaxis(mesh.devices, mesh.axis_names.index("chain"), 0).reshape(mesh.shape["chain"], -1)[:, 0]
    if any(getattr(device, "coords", None) is None for device in ring):
        return {}, {}
    spots = [tuple(device.coords) for device in ring]
    rightward, leftward = {}, {}
    if len({spot[0] for spot in spots}) == 2 and len({spot[1] for spot in spots}) == 2:
        for index in range(len(spots) - 1):
            low, high = spots[index], spots[index + 1]
            if low[0] != high[0] and low[1] != high[1]:
                for found, source, target, pick in (
                    (rightward, index, index + 1, max), (leftward, index + 1, index, max)
                ):
                    corner = (spots[source][0], spots[target][1])
                    at = [i for i, spot in enumerate(spots) if spot[:2] == corner]
                    if at:
                        found[source] = (pick(at), target)
    return rightward, leftward


def exact_dot(value, ones):
    high = value.astype(jnp.bfloat16)
    rest = value - high.astype(jnp.float32)
    middle = rest.astype(jnp.bfloat16)
    low = (rest - middle.astype(jnp.float32)).astype(jnp.bfloat16)
    return sum(jnp.dot(part, ones, preferred_element_type=jnp.float32) for part in (low, middle, high))


def finish_group(group, held, remapped, mass, skipped):
    moments, from_left, from_right, edges, coef, shift_of, base, beyond, triangle = held
    lane = lax.broadcasted_iota(jnp.int32, (TILE, BLOCK), 1)
    halos, places_of = [], []
    for tile in range(GROUP // TILE):
        rows = pl.ds(pl.multiple_of(group * GROUP + tile * TILE, TILE), TILE)
        inner = pl.ds(tile * TILE, TILE)
        shift = shift_of[rows, :]
        ahead = shift >= 0
        put = pl.ds(pl.multiple_of(group * GROUP + tile * TILE - skipped, TILE), TILE)
        places_of.append((rows, put, shift, ahead))

        folded = {}
        for name, ref in (("right", from_right), ("left", from_left)):
            value = ref[group, SENT - 1]
            folded[name] = pltpu.roll(value, HALF, 1) if tile else value

        def fetch(name, ref, row, first):
            chunk, start, splits = place(row, first)
            values = [
                ref[group, TILES * index + tile] if index < FULL else folded[name]
                for index in ((chunk, chunk + 1) if splits else (chunk,))
            ]
            return jnp.where(lane >= start, *values) if splits else values[0]

        def halo_row(row):
            right = fetch("right", from_right, row, AFTER_FIRST)
            left = fetch("left", from_left, row, BEFORE_FIRST)
            edge = edges[group, EDGES * tile + row // 8]
            wrapped = row == WRAPPED
            value = left if wrapped else jnp.where(ahead, right, left)
            value = jnp.where(ahead & (lane == edge_lane(row)), edge, value)
            value = pltpu.roll(value, (BLOCK - turn_of(row)) % BLOCK, 1) if turn_of(row) else value
            return jnp.where(ahead & (lane < SHIFT_MAX), right, value) if wrapped else value

        halos.append([halo_row(row) for row in range(ROWS)])

    signed = []
    for (_, _, _, ahead), halo in zip(places_of, halos):
        for var in range(VARS):
            value = halo[MOMENTS * var]
            signed.append(jnp.where(
                ahead,
                jnp.where(lane < AFTER_LENGTH, value, 0.0),
                jnp.where(lane >= BLOCK - BEFORE_LENGTH, -value, 0.0),
            ))
    crossed = exact_dot(jnp.concatenate(signed, axis=0), triangle[...])

    for tile, ((rows, put, shift, ahead), halo) in enumerate(zip(places_of, halos)):
        turn = shift & (BLOCK - 1)
        outside = jnp.where(ahead, lane - turn, turn - 1 - lane) < 0
        outside_next = jnp.where(ahead, lane - turn - 1, turn - lane) < 0
        at = (lane + turn) & (BLOCK - 1)
        weight = [coef[m, rows, :] for m in range(MOMENTS)]
        inside, across = {}, {}
        for index, (k, m) in enumerate(PAIRS):
            inside[k, m] = coef[MOMENTS + index, rows, :]
            across[k, m] = coef[MOMENTS + len(PAIRS) + index, rows, :]

        def settle(value):
            return jnp.take_along_axis(value, at, axis=1, mode="promise_in_bounds")

        for var in range(VARS):
            here, after = [], []
            for order in range(MOMENTS):
                own = moments[MOMENTS * var + order, rows, :]
                other = halo[MOMENTS * var + order]
                here.append(jnp.where(outside, other, own))
                after.append(pltpu.roll(jnp.where(outside_next, other, own), BLOCK - 1, 1))
            filled = weight[0] * here[0]
            filled_after = weight[0] * after[0]
            for m in range(1, MOMENTS):
                filled = filled + weight[m] * here[m]
                filled_after = filled_after + weight[m] * after[m]
            rise = after[0] - here[0]
            remapped[MOMENTS * var, put, :] = settle(here[0] + (filled_after - filled))
            for k in range(1, MOMENTS):
                value = inside[k, k] * here[k] + across[k, k] * after[k]
                for m in range(1, MOMENTS):
                    if m == k:
                        continue
                    pair = (min(k, m), max(k, m))
                    term = inside[pair] * here[m] + across[pair] * after[m]
                    value = value - term if k > m and (k + m) % 2 else value + term
                edge = (2.0 if k % 2 == 0 else -2.0) * (weight[k] * rise)
                remapped[MOMENTS * var + k, put, :] = settle((k + 0.5) * (value + edge))
            index = (tile * VARS + var) * TILE
            start = jnp.where(
                outside, crossed[index : index + TILE] + beyond[var, rows, :], base[var, rows, :]
            )
            mass[var, put, :] = settle(start + filled)


def kernel(
    chain, cross, relays,
    moments_in, flags_in, shifts_in, fraction_in,
    remapped, mass, moments, from_left, from_right, edges, coef, shift_of, base, beyond, triangle, mean_of,
    flags, shifts, fraction,
    to_left, to_right, relay, own_edges, edges_out, edges_in,
    sums, parts, raw, starts,
    left_send, left_recv, right_send, right_recv, relay_send, relay_recv,
    sum_send, sum_recv, part_send, part_recv, ready_sem, open_sem, edge_sem, input_sem,
):
    pencils = moments.shape[1]
    groups = pencils // GROUP
    me = lax.axis_index("chain")
    plane = lax.axis_index("cross")

    first_rows, later_rows = pl.ds(0, GROUP), pl.ds(GROUP, pencils - GROUP)
    inputs = [
        pltpu.make_async_copy(source, target, input_sem.at[index])
        for index, (source, target) in enumerate((
            (flags_in, flags),
            (moments_in.at[:, first_rows, :], moments.at[:, first_rows, :]),
            (moments_in.at[:, later_rows, :], moments.at[:, later_rows, :]),
            (shifts_in, shifts),
            (fraction_in, fraction),
        ))
    ]
    urgent, rest = inputs[:2], inputs[2:]
    for copy in urgent:
        copy.start()

    barrier = pltpu.get_barrier_semaphore()
    for step in range(1, chain):
        peer = lax.rem(me + step, chain)
        pl.semaphore_signal(barrier, inc=1, device_id={"chain": peer}, device_id_type=MESH)
    leads = me == 0

    @pl.when(leads)
    def _():
        for step in range(1, cross):
            peer = lax.rem(plane + step, cross)
            pl.semaphore_signal(barrier, inc=1, device_id={"cross": peer}, device_id_type=MESH)

    for copy in rest:
        copy.start()
    for copy in urgent:
        copy.wait()

    def leftward(group):
        return pltpu.make_async_remote_copy(
            src_ref=to_left.at[group], dst_ref=from_right.at[group],
            send_sem=left_send.at[group], recv_sem=left_recv.at[group],
            device_id={"chain": lax.rem(me + chain - 1, chain)}, device_id_type=MESH,
        )

    def rightward(group):
        return pltpu.make_async_remote_copy(
            src_ref=to_right.at[group], dst_ref=from_left.at[group],
            send_sem=right_send.at[group], recv_sem=right_recv.at[group],
            device_id={"chain": lax.rem(me + 1, chain)}, device_id_type=MESH,
        )

    has_left, has_right = me > 0, me < chain - 1

    def sum_copy(step, rows):
        return pltpu.make_async_remote_copy(
            src_ref=sums.at[me, pl.ds(0, rows)], dst_ref=sums.at[me, pl.ds(0, rows)],
            send_sem=sum_send.at[step], recv_sem=sum_recv.at[step],
            device_id={"chain": lax.rem(me + step, chain)}, device_id_type=MESH,
        )

    def each_sum(act, to_right):
        for step in range(1, chain):
            full = to_right(step)

            @pl.when(full)
            def _():
                act(sum_copy(step, VARS + 1))

            @pl.when(jnp.logical_not(full))
            def _():
                act(sum_copy(step, 1))

    sends_full = lambda step: me + step < chain
    comes_full = lambda step: me - step >= 0

    source_cell = lax.broadcasted_iota(jnp.int32, (BLOCK, BLOCK), 0)
    target_cell = lax.broadcasted_iota(jnp.int32, (BLOCK, BLOCK), 1)
    before_cell = jnp.where(source_cell < target_cell, 1.0, 0.0)

    def own_sums():
        total = jnp.zeros((pencils, BLOCK), jnp.float32)
        for var in range(VARS):
            pick = jnp.where(target_cell == var, 1.0, 0.0)
            both = jnp.concatenate([before_cell, pick], axis=1).astype(jnp.bfloat16)
            summed = exact_dot(moments[MOMENTS * var], both)
            base[var] = summed[:, :BLOCK]
            total = total + summed[:, BLOCK:]
        sums[me, 0:1] = jnp.sum(total, axis=0, keepdims=True)
        sums[me, 1 : VARS + 1] = jnp.transpose(total)[:VARS]

    def send_sums():
        each_sum(lambda copy: copy.start(), sends_full)

    lane = lax.broadcasted_iota(jnp.int32, (TILE, BLOCK), 1)
    spot = lane & 15

    def pack(group):
        halves = {}
        edge = None
        for tile in range(TILES):
            rows = pl.ds(group * GROUP + tile * TILE, TILE)
            flag = flags[rows, :]
            keep_linear, keep_full = flag <= 1, flag == 0
            rolled = []
            for row in range(ROWS):
                value = moments[row, rows, :]
                order = row % MOMENTS
                if order > 0:
                    value = jnp.where(keep_linear if order == 1 else keep_full, value, 0.0)
                    moments[row, rows, :] = value
                rolled.append(pltpu.roll(value, turn_of(row), 1) if turn_of(row) else value)
            for side, (held, target) in enumerate(((AFTER, to_left), (BEFORE, to_right))):
                for chunk in range(FULL + 1):
                    value = None
                    for start, row in held[chunk]:
                        part = moments[row, rows, :] if row == WRAPPED and side == 0 else rolled[row]
                        value = part if value is None else jnp.where(lane >= start, part, value)
                    if chunk < FULL:
                        target[group, TILES * chunk + tile] = value
                    else:
                        halves[side, tile] = value
            for index in range(EDGES):
                value = None
                for row in range(8 * index, min(8 * index + 8, ROWS)):
                    here = (lane >> 4) == edge_lane(row) // 16
                    value = rolled[row] if value is None else jnp.where(here, rolled[row], value)
                at = EDGES * tile + index
                value = pltpu.roll(value, at, 1) if at else value
                edge = value if edge is None else jnp.where(spot >= at, value, edge)
        for side, target in enumerate((to_left, to_right)):
            target[group, SENT - 1] = jnp.where(
                lane < HALF, halves[side, 0], pltpu.roll(halves[side, 1], HALF, 1)
            )
        own_edges[group] = edge

    edge_copy = pltpu.make_async_remote_copy(
        src_ref=edges_out, dst_ref=edges_in,
        send_sem=edge_sem.at[0], recv_sem=edge_sem.at[1],
        device_id={"chain": lax.rem(me + chain - 1, chain)}, device_id_type=MESH,
    )

    def send_edges():
        for index in range(groups // 2):
            edges_out[index] = jnp.where(
                spot < EDGE_STEP, own_edges[2 * index], pltpu.roll(own_edges[2 * index + 1], EDGE_STEP, 1)
            )

        @pl.when(has_left)
        def _():
            edge_copy.start()

    def receive_edges():
        @pl.when(has_right)
        def _():
            edge_copy.wait_recv()

        for group in range(groups):
            value = edges_in[group // 2]
            for at in range(EDGE_STEP):
                back = EDGE_STEP * (group % 2) + at
                edges[group, at] = pltpu.roll(value, BLOCK - back, 1) if back else value

    right_relays, left_relays = relays

    def to_relay(group, source, send_sem, through):
        return pltpu.make_async_remote_copy(
            src_ref=source.at[group], dst_ref=relay.at[group],
            send_sem=send_sem.at[group], recv_sem=relay_recv.at[group],
            device_id={"chain": jnp.int32(through)}, device_id_type=MESH,
        )

    def onward(group, landing, recv_sem, target):
        return pltpu.make_async_remote_copy(
            src_ref=relay.at[group], dst_ref=landing.at[group],
            send_sem=relay_send.at[group], recv_sem=recv_sem.at[group],
            device_id={"chain": jnp.int32(target)}, device_id_type=MESH,
        )

    def send(group, direct, wanted, among, routes, source, send_sem):
        group = jnp.int32(group)
        relayed = functools.reduce(jnp.logical_or, [group == index for index in among])
        for start, (through, _) in routes.items():
            wanted = wanted & ((me != start) | jnp.logical_not(relayed))

            @pl.when((me == start) & relayed)
            def _():
                to_relay(group, source, send_sem, through).start()

        if direct is rightward:
            for start in routes:
                wanted = wanted & ((me != start) | (group < LATE))

        @pl.when(wanted)
        def _():
            direct(group).start()

    def send_late():
        for start in right_relays:

            @pl.when(me == start)
            def _():
                for group in range(groups):
                    if group >= LATE and group not in RELAYED_RIGHT:
                        rightward(group).start()

    def send_both(group):
        send(group, leftward, has_left, RELAYED_LEFT, left_relays, to_left, left_send)
        send(group, rightward, has_right, RELAYED_RIGHT, right_relays, to_right, right_send)

    def pack_next(group, carry):
        pack(group)
        return carry

    def send_next(group, carry):
        send_both(group)
        return carry

    pack(0)
    soon = lax.rem(me, 2) == 1
    soon = soon | (me == 0)

    @pl.when(soon)
    def _():
        for copy in rest:
            copy.wait()
        own_sums()

    pl.semaphore_wait(barrier, jnp.where(leads, chain - 1 + cross - 1, chain - 1))
    send_both(0)

    @pl.when(leads)
    def _():
        for step in range(1, cross):
            peer = lax.rem(plane + step, cross)
            pl.semaphore_signal(ready_sem, inc=1, device_id={"cross": peer}, device_id_type=MESH)

    @pl.when(jnp.logical_not(soon))
    def _():
        for copy in rest:
            copy.wait()
        own_sums()

    send_sums()
    for group in range(1, EARLY):
        pack(group)
        send_both(group)
    for group in range(EARLY, groups):
        pack(group)
    send_edges()
    for group in range(EARLY, groups):
        send_both(group)

    part_copies = [
        pltpu.make_async_remote_copy(
            src_ref=parts.at[plane], dst_ref=parts.at[plane],
            send_sem=part_send.at[step], recv_sem=part_recv.at[step],
            device_id={"cross": lax.rem(plane + step, cross)}, device_id_type=MESH,
        )
        for step in range(1, cross)
    ]

    def open_planes():
        @pl.when(leads)
        def _():
            pl.semaphore_wait(ready_sem, cross - 1)
            for peer in range(1, chain):
                pl.semaphore_signal(open_sem, inc=1, device_id={"chain": jnp.int32(peer)}, device_id_type=MESH)

    def send_parts():
        @pl.when(jnp.logical_not(leads))
        def _():
            pl.semaphore_wait(open_sem, 1)

        for copy in part_copies:
            copy.start()

    def pass_on(index):
        for among, routes, source, send_sem, landing, recv_sem in (
            (RELAYED_RIGHT, right_relays, to_right, right_send, from_left, right_recv),
            (RELAYED_LEFT, left_relays, to_left, left_send, from_right, left_recv),
        ):
            for through, target in routes.values():
                if index >= len(among):
                    continue
                group = among[index]

                @pl.when(me == through)
                def _():
                    to_relay(group, source, send_sem, through).wait_recv()
                    onward(group, landing, recv_sem, target).start()

    shift_row = shifts[...]

    def reduce_chain():
        starts[...] = jnp.zeros_like(starts)
        each_sum(lambda copy: copy.wait_recv(), comes_full)
        before = jnp.zeros((8, pencils), jnp.float32)
        whole = jnp.zeros((1, BLOCK), jnp.float32)
        for index in range(chain):
            before = before + jnp.where(index < me, sums[index], 0.0)
            whole = whole + sums[index, 0:1]
        parts[plane] = whole
        starts[0:8, :] = before
        starts[8:16, :] = before + jnp.where(shift_row >= 0, sums[me], 0.0)

    def spread_starts():
        turned = jnp.transpose(starts[...])
        for var in range(VARS):
            base[var] = base[var] + turned[:, 1 + var : 2 + var]
            beyond[var] = jnp.broadcast_to(turned[:, 9 + var : 10 + var], (pencils, BLOCK))

    open_planes()
    pass_on(0)
    pass_on(1)
    reduce_chain()
    send_parts()

    send_late()
    @pl.when(me == 0)
    def _():
        from_left[...] = jnp.zeros_like(from_left)

    @pl.when(me == chain - 1)
    def _():
        from_right[...] = jnp.zeros_like(from_right)
        edges_in[...] = jnp.zeros_like(edges_in)

    f = fraction[...]
    first = interval_integrals(-1.0 + 0.0 * f, 1.0 - 2.0 * f, 2.0 * f)
    second = interval_integrals(1.0 - 2.0 * f, 1.0 + 0.0 * f, 2.0 * f - 2.0)
    raw[...] = jnp.zeros_like(raw)
    columns = partial_weights(f) + first + second + [shift_row.astype(jnp.float32)]
    for index, value in enumerate(columns):
        raw[index : index + 1, :] = value
    turned = jnp.transpose(raw[...])
    for index in range(COEFS):
        coef[index] = jnp.broadcast_to(turned[:, index : index + 1], (pencils, BLOCK))
    shift_of[...] = jnp.broadcast_to(turned[:, COEFS : COEFS + 1], (pencils, BLOCK)).astype(jnp.int32)

    up_to_edge = jnp.where(source_cell < BLOCK // 2, before_cell, 1.0 - before_cell)
    triangle[...] = up_to_edge.astype(jnp.bfloat16)
    pass_on(2)
    pass_on(3)
    pass_on(4)
    spread_starts()
    receive_edges()


    held = moments, from_left, from_right, edges, coef, shift_of, base, beyond, triangle

    def receive(group):
        @pl.when(has_right)
        def _():
            leftward(group).wait_recv()

        @pl.when(has_left)
        def _():
            rightward(group).wait_recv()

    def turn_to(step):
        group = jnp.int32(step)
        for order, routes in ((ORDER_RIGHT, right_relays), (ORDER_LEFT, left_relays)):
            for _, target in routes.values():
                for index, other in enumerate(order):
                    group = jnp.where((me == target) & (step == index), other, group)
        return group

    def remap(step, carry):
        group = turn_to(step)
        receive(group)
        finish_group(group, held, remapped, mass, 0)
        return carry

    lax.fori_loop(0, groups - 1, remap, 0)

    for copy in part_copies:
        copy.wait_recv()
    grand = parts[0]
    for index in range(1, cross):
        grand = grand + parts[index]
    mean = grand / float(pencils * cross)
    for var in range(VARS):
        mean_of[var : var + 1, :] = jnp.broadcast_to(mean[:, var : var + 1], (1, BLOCK))
    done = pl.ds(0, pencils - GROUP)
    for var in range(VARS):
        mass[var, done, :] = mass[var, done, :] / mean_of[var : var + 1, :]

    each_sum(lambda copy: copy.wait_send(), sends_full)
    for copy in part_copies:
        copy.wait_send()

    for among, routes, landing, recv_sem in (
        (RELAYED_RIGHT, right_relays, from_left, right_recv), (RELAYED_LEFT, left_relays, from_right, left_recv)
    ):
        for through, target in routes.values():

            @pl.when(me == through)
            def _():
                for group in among:
                    onward(group, landing, recv_sem, target).wait_send()

    @pl.when(has_left)
    def _():
        edge_copy.wait_send()
        for group in range(groups):
            leftward(group).wait_send()

    @pl.when(has_right)
    def _():
        for group in range(groups):
            rightward(group).wait_send()

    receive(groups - 1)


def deliver(
    remapped, mass, moments, from_left, from_right, edges, coef, shift_of, base, beyond, triangle, mean_of,
    remapped_out, mass_out,
    last_remapped, last_mass, sem,
):
    done = remapped.shape[1] - GROUP
    early, late = pl.ds(0, done), pl.ds(done, GROUP)
    held = moments, from_left, from_right, edges, coef, shift_of, base, beyond, triangle
    copies = [
        pltpu.make_async_copy(source, target, sem.at[index])
        for index, (source, target) in enumerate((
            (remapped.at[:, early, :], remapped_out.at[:, early, :]),
            (mass.at[:, early, :], mass_out.at[:, early, :]),
            (last_remapped, remapped_out.at[:, late, :]),
            (last_mass, mass_out.at[:, late, :]),
        ))
    ]
    for copy in copies[:2]:
        copy.start()
    finish_group(done // GROUP, held, last_remapped, last_mass, done)
    for var in range(VARS):
        last_mass[var] = last_mass[var] / mean_of[var : var + 1, :]
    for copy in copies[2:]:
        copy.start()
    for copy in copies:
        copy.wait()


def solution(mesh):
    chain, cross = mesh.shape["chain"], mesh.shape["cross"]
    relays = corner_relays(mesh)

    def shards(moments, flags, shifts, fraction):
        row_count, pencils, cells = moments.shape
        assert row_count == ROWS and cells == BLOCK and pencils == BLOCK
        groups = pencils // GROUP
        dma = pltpu.SemaphoreType.DMA
        float_of = functools.partial(jax.ShapeDtypeStruct, dtype=jnp.float32)
        halo = (groups, SENT, TILE, BLOCK)
        block = pltpu.VMEM(halo, jnp.float32)
        results = float_of(moments.shape), float_of((VARS, pencils, cells))
        handed = results + (
            float_of(moments.shape), float_of(halo), float_of(halo), float_of((groups, EDGE_STEP, TILE, BLOCK)),
            float_of((COEFS, pencils, BLOCK)), jax.ShapeDtypeStruct((pencils, BLOCK), jnp.int32),
            float_of((VARS, pencils, BLOCK)), float_of((VARS, pencils, BLOCK)),
            jax.ShapeDtypeStruct((BLOCK, BLOCK), jnp.bfloat16), float_of((8, BLOCK)),
        )
        in_vmem = pl.BlockSpec(memory_space=pltpu.VMEM)
        in_hbm = pl.BlockSpec(memory_space=pltpu.HBM)
        ready = pl.pallas_call(
            functools.partial(kernel, chain, cross, relays),
            out_shape=handed,
            in_specs=[in_hbm] * 4,
            out_specs=(in_vmem,) * len(handed),
            scratch_shapes=[
                pltpu.VMEM(flags.shape, jnp.int32),
                pltpu.VMEM((1, pencils), jnp.int32),
                pltpu.VMEM((1, pencils), jnp.float32),
                block, block, block,
                pltpu.VMEM((groups, TILE, BLOCK), jnp.float32),
                pltpu.VMEM((groups // 2, TILE, BLOCK), jnp.float32),
                pltpu.VMEM((groups // 2, TILE, BLOCK), jnp.float32),
                pltpu.VMEM((chain, 8, pencils), jnp.float32),
                pltpu.VMEM((cross, 1, BLOCK), jnp.float32),
                pltpu.VMEM((BLOCK, pencils), jnp.float32),
                pltpu.VMEM((BLOCK, pencils), jnp.float32),
                dma((groups,)), dma((groups,)), dma((groups,)), dma((groups,)),
                dma((groups,)), dma((groups,)),
                dma((chain,)), dma((chain,)), dma((cross,)), dma((cross,)),
                pltpu.SemaphoreType.REGULAR, pltpu.SemaphoreType.REGULAR, dma((2,)), dma((5,)),
            ],
            compiler_params=pltpu.CompilerParams(
                collective_id=0, has_side_effects=True, vmem_limit_bytes=24 << 20
            ),
        )(*(
            pltpu.with_memory_space_constraint(value, pltpu.HBM)
            for value in (moments, flags, shifts.T, fraction.reshape(1, pencils))
        ))
        return pl.pallas_call(
            deliver,
            out_shape=results,
            in_specs=[in_vmem] * len(handed),
            out_specs=(in_hbm,) * 2,
            scratch_shapes=[
                pltpu.VMEM((ROWS, GROUP, BLOCK), jnp.float32),
                pltpu.VMEM((VARS, GROUP, BLOCK), jnp.float32),
                dma((4,)),
            ],
            compiler_params=pltpu.CompilerParams(vmem_limit_bytes=16 << 20),
        )(*ready)

    in_specs = (P(None, "cross", "chain"), P("cross", "chain"), P("cross", "chain"), P("cross"))
    out_specs = (P(None, "cross", "chain"), P(None, "cross", "chain"))
    return jax.shard_map(shards, mesh=mesh, in_specs=in_specs, out_specs=out_specs, check_vma=False)
```

```python
import functools

import jax
import numpy as np
import jax.numpy as jnp
from jax import lax
from jax.experimental import pallas as pl
from jax.experimental.pallas import tpu as pltpu
from jax.sharding import PartitionSpec as P

VARS = 5
MOMENTS = 4
BLOCK = 128
SHIFT_MAX = 48
ROWS = VARS * MOMENTS
SPAN = ROWS * SHIFT_MAX
FULL, HALF = SPAN // BLOCK, BLOCK // 2
TILE = 8
TILES = 2
GROUP = TILES * TILE
SENT = TILES * FULL + 1
EDGES = -(-ROWS // 8)
EDGE_STEP = TILES * EDGES
LATE = 2
EARLY = 2
ORDER_RIGHT, ORDER_LEFT = (0, 1, 3, 2, 4, 5, 6), (0, 2, 4, 6, 1, 3, 5)
RELAYED_RIGHT, RELAYED_LEFT = (1, 3, 5, 7), (1, 3, 5)
PAIRS = tuple((k, m) for k in range(1, MOMENTS) for m in range(k, MOMENTS))
COEFS = MOMENTS + 2 * len(PAIRS)
MESH = pl.DeviceIdType.MESH
HIGHEST = lax.Precision.HIGHEST

gauss_nodes = (-0.8611363115940526, -0.3399810435848563, 0.3399810435848563, 0.8611363115940526)
gauss_weights = (0.3478548451374538, 0.6521451548625461, 0.6521451548625461, 0.3478548451374538)


AFTER_FIRST, AFTER_LENGTH = SHIFT_MAX, SHIFT_MAX + 1
BEFORE_FIRST, BEFORE_LENGTH = 0, SHIFT_MAX


def place(row, first):
    chunk, lane = divmod((first + SHIFT_MAX * row) % SPAN, BLOCK)
    return chunk, lane, lane + SHIFT_MAX > BLOCK


def segments(first):
    held = [[] for _ in range(FULL + 1)]
    for row in range(ROWS):
        chunk, lane, splits = place(row, first)
        held[chunk].append((lane, row))
        if splits:
            held[chunk + 1].append((0, row))
    return [sorted(chunk) for chunk in held]


AFTER, BEFORE = segments(AFTER_FIRST), segments(BEFORE_FIRST)
WRAPPED = ROWS - 1


def turn_of(row):
    return (SHIFT_MAX * (row + 1)) % BLOCK


def edge_lane(row):
    return (turn_of(row) + SHIFT_MAX) % BLOCK


def legendre_values(point):
    return [
        jnp.ones_like(point),
        point,
        0.5 * (3.0 * point * point - 1.0),
        0.5 * (5.0 * point * point * point - 3.0 * point),
    ]


def interval_integrals(low_end, high_end, offset):
    half = 0.5 * (high_end - low_end)
    middle = 0.5 * (high_end + low_end)
    entries = [jnp.zeros_like(low_end) for _ in PAIRS]
    for node, weight in zip(gauss_nodes, gauss_weights):
        point = middle + half * node
        target = legendre_values(point)
        source = legendre_values(point + offset)
        scaled = [weight * half * value for value in target]
        for index, (k, m) in enumerate(PAIRS):
            entries[index] = entries[index] + scaled[k] * source[m]
    return entries


def partial_weights(fraction):
    shifted = 2.0 * fraction - 1.0
    square = shifted * shifted
    return [
        fraction,
        fraction * fraction - fraction,
        0.25 * (square * shifted - shifted),
        0.5 * (0.5 * (1.25 * square * square - 1.5 * square) + 0.125),
    ]


def corner_relays(mesh):
    ring = np.moveaxis(mesh.devices, mesh.axis_names.index("chain"), 0).reshape(mesh.shape["chain"], -1)[:, 0]
    if any(getattr(device, "coords", None) is None for device in ring):
        return {}, {}
    spots = [tuple(device.coords) for device in ring]
    rightward, leftward = {}, {}
    if len({spot[0] for spot in spots}) == 2 and len({spot[1] for spot in spots}) == 2:
        for index in range(len(spots) - 1):
            low, high = spots[index], spots[index + 1]
            if low[0] != high[0] and low[1] != high[1]:
                for found, source, target, pick in (
                    (rightward, index, index + 1, max), (leftward, index + 1, index, max)
                ):
                    corner = (spots[source][0], spots[target][1])
                    at = [i for i, spot in enumerate(spots) if spot[:2] == corner]
                    if at:
                        found[source] = (pick(at), target)
    return rightward, leftward


def exact_dot(value, ones):
    high = value.astype(jnp.bfloat16)
    rest = value - high.astype(jnp.float32)
    middle = rest.astype(jnp.bfloat16)
    low = (rest - middle.astype(jnp.float32)).astype(jnp.bfloat16)
    return sum(jnp.dot(part, ones, preferred_element_type=jnp.float32) for part in (low, middle, high))


def finish_group(group, held, remapped, mass, skipped):
    moments, from_left, from_right, edges, coef, shift_of, base, beyond, triangle = held
    lane = lax.broadcasted_iota(jnp.int32, (TILE, BLOCK), 1)
    halos, places_of = [], []
    for tile in range(GROUP // TILE):
        rows = pl.ds(pl.multiple_of(group * GROUP + tile * TILE, TILE), TILE)
        inner = pl.ds(tile * TILE, TILE)
        shift = shift_of[rows, :]
        ahead = shift >= 0
        put = pl.ds(pl.multiple_of(group * GROUP + tile * TILE - skipped, TILE), TILE)
        places_of.append((rows, put, shift, ahead))

        folded = {}
        for name, ref in (("right", from_right), ("left", from_left)):
            value = ref[group, SENT - 1]
            folded[name] = pltpu.roll(value, HALF, 1) if tile else value

        def fetch(name, ref, row, first):
            chunk, start, splits = place(row, first)
            values = [
                ref[group, TILES * index + tile] if index < FULL else folded[name]
                for index in ((chunk, chunk + 1) if splits else (chunk,))
            ]
            return jnp.where(lane >= start, *values) if splits else values[0]

        def halo_row(row):
            right = fetch("right", from_right, row, AFTER_FIRST)
            left = fetch("left", from_left, row, BEFORE_FIRST)
            edge = edges[group, EDGES * tile + row // 8]
            wrapped = row == WRAPPED
            value = left if wrapped else jnp.where(ahead, right, left)
            value = jnp.where(ahead & (lane == edge_lane(row)), edge, value)
            value = pltpu.roll(value, (BLOCK - turn_of(row)) % BLOCK, 1) if turn_of(row) else value
            return jnp.where(ahead & (lane < SHIFT_MAX), right, value) if wrapped else value

        halos.append([halo_row(row) for row in range(ROWS)])

    signed = []
    for (_, _, _, ahead), halo in zip(places_of, halos):
        for var in range(VARS):
            value = halo[MOMENTS * var]
            signed.append(jnp.where(
                ahead,
                jnp.where(lane < AFTER_LENGTH, value, 0.0),
                jnp.where(lane >= BLOCK - BEFORE_LENGTH, -value, 0.0),
            ))
    crossed = exact_dot(jnp.concatenate(signed, axis=0), triangle[...])

    for tile, ((rows, put, shift, ahead), halo) in enumerate(zip(places_of, halos)):
        turn = shift & (BLOCK - 1)
        outside = jnp.where(ahead, lane - turn, turn - 1 - lane) < 0
        outside_next = jnp.where(ahead, lane - turn - 1, turn - lane) < 0
        at = (lane + turn) & (BLOCK - 1)
        weight = [coef[m, rows, :] for m in range(MOMENTS)]
        inside, across = {}, {}
        for index, (k, m) in enumerate(PAIRS):
            inside[k, m] = coef[MOMENTS + index, rows, :]
            across[k, m] = coef[MOMENTS + len(PAIRS) + index, rows, :]

        def settle(value):
            return jnp.take_along_axis(value, at, axis=1, mode="promise_in_bounds")

        for var in range(VARS):
            here, after = [], []
            for order in range(MOMENTS):
                own = moments[MOMENTS * var + order, rows, :]
                other = halo[MOMENTS * var + order]
                here.append(jnp.where(outside, other, own))
                after.append(pltpu.roll(jnp.where(outside_next, other, own), BLOCK - 1, 1))
            filled = weight[0] * here[0]
            filled_after = weight[0] * after[0]
            for m in range(1, MOMENTS):
                filled = filled + weight[m] * here[m]
                filled_after = filled_after + weight[m] * after[m]
            rise = after[0] - here[0]
            remapped[MOMENTS * var, put, :] = settle(here[0] + (filled_after - filled))
            for k in range(1, MOMENTS):
                value = inside[k, k] * here[k] + across[k, k] * after[k]
                for m in range(1, MOMENTS):
                    if m == k:
                        continue
                    pair = (min(k, m), max(k, m))
                    term = inside[pair] * here[m] + across[pair] * after[m]
                    value = value - term if k > m and (k + m) % 2 else value + term
                edge = (2.0 if k % 2 == 0 else -2.0) * (weight[k] * rise)
                remapped[MOMENTS * var + k, put, :] = settle((k + 0.5) * (value + edge))
            index = (tile * VARS + var) * TILE
            start = jnp.where(
                outside, crossed[index : index + TILE] + beyond[var, rows, :], base[var, rows, :]
            )
            mass[var, put, :] = settle(start + filled)


def kernel(
    chain, cross, relays,
    moments_in, flags_in, shifts_in, fraction_in,
    remapped, mass, moments, from_left, from_right, edges, coef, shift_of, base, beyond, triangle, mean_of,
    flags, shifts, fraction,
    to_left, to_right, relay, own_edges, edges_out, edges_in,
    sums, parts, raw, starts,
    left_send, left_recv, right_send, right_recv, relay_send, relay_recv,
    sum_sem, part_sem, ready_sem, open_sem, edge_sem, input_sem,
):
    pencils = moments.shape[1]
    groups = pencils // GROUP
    me = lax.axis_index("chain")
    plane = lax.axis_index("cross")

    first_rows, later_rows = pl.ds(0, GROUP), pl.ds(GROUP, pencils - GROUP)
    inputs = [
        pltpu.make_async_copy(source, target, input_sem.at[index])
        for index, (source, target) in enumerate((
            (flags_in, flags),
            (moments_in.at[:, first_rows, :], moments.at[:, first_rows, :]),
            (moments_in.at[:, later_rows, :], moments.at[:, later_rows, :]),
            (shifts_in, shifts),
            (fraction_in, fraction),
        ))
    ]
    urgent, rest = inputs[:2], inputs[2:]
    for copy in urgent:
        copy.start()

    barrier = pltpu.get_barrier_semaphore()
    for step in range(1, chain):
        peer = lax.rem(me + step, chain)
        pl.semaphore_signal(barrier, inc=1, device_id={"chain": peer}, device_id_type=MESH)
    leads = me == 0

    @pl.when(leads)
    def _():
        for step in range(1, cross):
            peer = lax.rem(plane + step, cross)
            pl.semaphore_signal(barrier, inc=1, device_id={"cross": peer}, device_id_type=MESH)

    for copy in rest:
        copy.start()
    for copy in urgent:
        copy.wait()

    def leftward(group):
        return pltpu.make_async_remote_copy(
            src_ref=to_left.at[group], dst_ref=from_right.at[group],
            send_sem=left_send.at[0], recv_sem=left_recv.at[group],
            device_id={"chain": lax.rem(me + chain - 1, chain)}, device_id_type=MESH,
        )

    def rightward(group):
        return pltpu.make_async_remote_copy(
            src_ref=to_right.at[group], dst_ref=from_left.at[group],
            send_sem=right_send.at[0], recv_sem=right_recv.at[group],
            device_id={"chain": lax.rem(me + 1, chain)}, device_id_type=MESH,
        )

    has_left, has_right = me > 0, me < chain - 1

    sum_copies = [
        pltpu.make_async_remote_copy(
            src_ref=sums.at[me], dst_ref=sums.at[me],
            send_sem=sum_sem.at[0], recv_sem=sum_sem.at[1],
            device_id={"chain": lax.rem(me + step, chain)}, device_id_type=MESH,
        )
        for step in range(1, chain)
    ]
    others = pl.ds(0, chain - 1)
    all_sums = pltpu.make_async_remote_copy(
        src_ref=sums.at[others], dst_ref=sums.at[others],
        send_sem=sum_sem.at[0], recv_sem=sum_sem.at[1],
        device_id={"chain": lax.rem(me + 1, chain)}, device_id_type=MESH,
    )

    source_cell = lax.broadcasted_iota(jnp.int32, (BLOCK, BLOCK), 0)
    target_cell = lax.broadcasted_iota(jnp.int32, (BLOCK, BLOCK), 1)
    before_cell = jnp.where(source_cell < target_cell, 1.0, 0.0)

    def own_sums():
        total = jnp.zeros((pencils, BLOCK), jnp.float32)
        for var in range(VARS):
            pick = jnp.where(target_cell == var, 1.0, 0.0)
            both = jnp.concatenate([before_cell, pick], axis=1).astype(jnp.bfloat16)
            summed = exact_dot(moments[MOMENTS * var], both)
            base[var] = summed[:, :BLOCK]
            total = total + summed[:, BLOCK:]
        sums[me] = jnp.where(
            lax.broadcasted_iota(jnp.int32, (8, BLOCK), 0) == VARS,
            jnp.sum(total, axis=0, keepdims=True), jnp.transpose(total)[:8],
        )

    def send_sums():
        for copy in sum_copies:
            copy.start()

    lane = lax.broadcasted_iota(jnp.int32, (TILE, BLOCK), 1)
    spot = lane & 15

    def pack(group):
        halves = {}
        edge = None
        for tile in range(TILES):
            rows = pl.ds(group * GROUP + tile * TILE, TILE)
            flag = flags[rows, :]
            keep_linear, keep_full = flag <= 1, flag == 0
            rolled = []
            for row in range(ROWS):
                value = moments[row, rows, :]
                order = row % MOMENTS
                if order > 0:
                    value = jnp.where(keep_linear if order == 1 else keep_full, value, 0.0)
                    moments[row, rows, :] = value
                rolled.append(pltpu.roll(value, turn_of(row), 1) if turn_of(row) else value)
            for side, (held, target) in enumerate(((AFTER, to_left), (BEFORE, to_right))):
                for chunk in range(FULL + 1):
                    value = None
                    for start, row in held[chunk]:
                        part = moments[row, rows, :] if row == WRAPPED and side == 0 else rolled[row]
                        value = part if value is None else jnp.where(lane >= start, part, value)
                    if chunk < FULL:
                        target[group, TILES * chunk + tile] = value
                    else:
                        halves[side, tile] = value
            for index in range(EDGES):
                value = None
                for row in range(8 * index, min(8 * index + 8, ROWS)):
                    here = (lane >> 4) == edge_lane(row) // 16
                    value = rolled[row] if value is None else jnp.where(here, rolled[row], value)
                at = EDGES * tile + index
                value = pltpu.roll(value, at, 1) if at else value
                edge = value if edge is None else jnp.where(spot >= at, value, edge)
        for side, target in enumerate((to_left, to_right)):
            target[group, SENT - 1] = jnp.where(
                lane < HALF, halves[side, 0], pltpu.roll(halves[side, 1], HALF, 1)
            )
        own_edges[group] = edge

    edge_copy = pltpu.make_async_remote_copy(
        src_ref=edges_out, dst_ref=edges_in,
        send_sem=edge_sem.at[0], recv_sem=edge_sem.at[1],
        device_id={"chain": lax.rem(me + chain - 1, chain)}, device_id_type=MESH,
    )

    def send_edges():
        for index in range(groups // 2):
            edges_out[index] = jnp.where(
                spot < EDGE_STEP, own_edges[2 * index], pltpu.roll(own_edges[2 * index + 1], EDGE_STEP, 1)
            )

        @pl.when(has_left)
        def _():
            edge_copy.start()

    def receive_edges():
        @pl.when(has_right)
        def _():
            edge_copy.wait_recv()

        for group in range(groups):
            value = edges_in[group // 2]
            for at in range(EDGE_STEP):
                back = EDGE_STEP * (group % 2) + at
                edges[group, at] = pltpu.roll(value, BLOCK - back, 1) if back else value

    right_relays, left_relays = relays

    def to_relay(group, source, send_sem, through):
        return pltpu.make_async_remote_copy(
            src_ref=source.at[group], dst_ref=relay.at[group],
            send_sem=send_sem.at[0], recv_sem=relay_recv.at[group // 2],
            device_id={"chain": jnp.int32(through)}, device_id_type=MESH,
        )

    def onward(group, landing, recv_sem, target):
        return pltpu.make_async_remote_copy(
            src_ref=relay.at[group], dst_ref=landing.at[group],
            send_sem=relay_send.at[0], recv_sem=recv_sem.at[group],
            device_id={"chain": jnp.int32(target)}, device_id_type=MESH,
        )

    def send(group, direct, wanted, among, routes, source, send_sem):
        group = jnp.int32(group)
        relayed = functools.reduce(jnp.logical_or, [group == index for index in among])
        for start, (through, _) in routes.items():
            wanted = wanted & ((me != start) | jnp.logical_not(relayed))

            @pl.when((me == start) & relayed)
            def _():
                to_relay(group, source, send_sem, through).start()

        if direct is rightward:
            for start in routes:
                wanted = wanted & ((me != start) | (group < LATE))

        @pl.when(wanted)
        def _():
            direct(group).start()

    def send_late():
        for start in right_relays:

            @pl.when(me == start)
            def _():
                for group in range(groups):
                    if group >= LATE and group not in RELAYED_RIGHT:
                        rightward(group).start()

    def send_both(group):
        send(group, leftward, has_left, RELAYED_LEFT, left_relays, to_left, left_send)
        send(group, rightward, has_right, RELAYED_RIGHT, right_relays, to_right, right_send)

    def pack_next(group, carry):
        pack(group)
        return carry

    def send_next(group, carry):
        send_both(group)
        return carry

    pack(0)
    soon = lax.rem(me, 2) == 1
    soon = soon | (me == 0)

    @pl.when(soon)
    def _():
        for copy in rest:
            copy.wait()
        own_sums()

    pl.semaphore_wait(barrier, jnp.where(leads, chain - 1 + cross - 1, chain - 1))
    send_both(0)

    @pl.when(leads)
    def _():
        for step in range(1, cross):
            peer = lax.rem(plane + step, cross)
            pl.semaphore_signal(ready_sem, inc=1, device_id={"cross": peer}, device_id_type=MESH)

    @pl.when(jnp.logical_not(soon))
    def _():
        for copy in rest:
            copy.wait()
        own_sums()

    send_sums()
    for group in range(1, EARLY):
        pack(group)
        send_both(group)
    for group in range(EARLY, groups):
        pack(group)
    send_edges()
    for group in range(EARLY, groups):
        send_both(group)

    part_copies = [
        pltpu.make_async_remote_copy(
            src_ref=parts.at[plane], dst_ref=parts.at[plane],
            send_sem=part_sem.at[0], recv_sem=part_sem.at[1],
            device_id={"cross": lax.rem(plane + step, cross)}, device_id_type=MESH,
        )
        for step in range(1, cross)
    ]

    elsewhere = pl.ds(0, cross - 1)
    all_parts = pltpu.make_async_remote_copy(
        src_ref=parts.at[elsewhere], dst_ref=parts.at[elsewhere],
        send_sem=part_sem.at[0], recv_sem=part_sem.at[1],
        device_id={"cross": lax.rem(plane + 1, cross)}, device_id_type=MESH,
    )

    def open_planes():
        @pl.when(leads)
        def _():
            pl.semaphore_wait(ready_sem, cross - 1)
            for peer in range(1, chain):
                pl.semaphore_signal(open_sem, inc=1, device_id={"chain": jnp.int32(peer)}, device_id_type=MESH)

    def send_parts():
        @pl.when(jnp.logical_not(leads))
        def _():
            pl.semaphore_wait(open_sem, 1)

        for copy in part_copies:
            copy.start()

    def pass_on(index, sides=(0, 1)):
        for side, (among, routes, source, send_sem, landing, recv_sem) in enumerate((
            (RELAYED_RIGHT, right_relays, to_right, right_send, from_left, right_recv),
            (RELAYED_LEFT, left_relays, to_left, left_send, from_right, left_recv),
        )):
            if side not in sides:
                continue
            for through, target in routes.values():
                if index >= len(among):
                    continue
                group = among[index]

                @pl.when(me == through)
                def _():
                    to_relay(group, source, send_sem, through).wait_recv()
                    onward(group, landing, recv_sem, target).start()

    shift_row = shifts[...]

    def reduce_chain():
        starts[...] = jnp.zeros_like(starts)
        all_sums.wait_recv()
        before = jnp.zeros((8, pencils), jnp.float32)
        whole = jnp.zeros((1, BLOCK), jnp.float32)
        for index in range(chain):
            before = before + jnp.where(index < me, sums[index], 0.0)
            whole = whole + sums[index, VARS : VARS + 1]
        parts[plane] = whole
        starts[0:8, :] = before
        starts[8:16, :] = before + jnp.where(shift_row >= 0, sums[me], 0.0)

    def spread_starts():
        turned = jnp.transpose(starts[...])
        for var in range(VARS):
            base[var] = base[var] + turned[:, var : var + 1]
            beyond[var] = jnp.broadcast_to(turned[:, 8 + var : 9 + var], (pencils, BLOCK))

    open_planes()
    pass_on(0)
    pass_on(1)
    reduce_chain()
    for index in range(2, len(RELAYED_RIGHT)):
        pass_on(index, (0,))
    send_parts()
    send_late()

    @pl.when(me == 0)
    def _():
        from_left[...] = jnp.zeros_like(from_left)

    @pl.when(me == chain - 1)
    def _():
        from_right[...] = jnp.zeros_like(from_right)
        edges_in[...] = jnp.zeros_like(edges_in)

    f = fraction[...]
    first = interval_integrals(-1.0 + 0.0 * f, 1.0 - 2.0 * f, 2.0 * f)
    second = interval_integrals(1.0 - 2.0 * f, 1.0 + 0.0 * f, 2.0 * f - 2.0)
    raw[...] = jnp.zeros_like(raw)
    columns = partial_weights(f) + first + second + [shift_row.astype(jnp.float32)]
    for index, value in enumerate(columns):
        raw[index : index + 1, :] = value
    turned = jnp.transpose(raw[...])
    for index in range(COEFS):
        coef[index] = jnp.broadcast_to(turned[:, index : index + 1], (pencils, BLOCK))
    shift_of[...] = jnp.broadcast_to(turned[:, COEFS : COEFS + 1], (pencils, BLOCK)).astype(jnp.int32)

    up_to_edge = jnp.where(source_cell < BLOCK // 2, before_cell, 1.0 - before_cell)
    triangle[...] = up_to_edge.astype(jnp.bfloat16)
    for index in range(2, len(RELAYED_LEFT)):
        pass_on(index, (1,))
    spread_starts()
    receive_edges()


    held = moments, from_left, from_right, edges, coef, shift_of, base, beyond, triangle

    def receive(group):
        @pl.when(has_right)
        def _():
            leftward(group).wait_recv()

        @pl.when(has_left)
        def _():
            rightward(group).wait_recv()

    def turn_to(step):
        group = jnp.int32(step)
        for order, routes in ((ORDER_RIGHT, right_relays), (ORDER_LEFT, left_relays)):
            for _, target in routes.values():
                for index, other in enumerate(order):
                    group = jnp.where((me == target) & (step == index), other, group)
        return group

    def remap(step, carry):
        group = turn_to(step)
        receive(group)
        finish_group(group, held, remapped, mass, 0)
        return carry

    lax.fori_loop(0, groups - 1, remap, 0)

    all_parts.wait_recv()
    grand = parts[0]
    for index in range(1, cross):
        grand = grand + parts[index]
    mean = grand / float(pencils * cross)
    for var in range(VARS):
        mean_of[var : var + 1, :] = jnp.broadcast_to(mean[:, var : var + 1], (1, BLOCK))
    done = pl.ds(0, pencils - GROUP)
    for var in range(VARS):
        mass[var, done, :] = mass[var, done, :] / mean_of[var : var + 1, :]

    all_sums.wait_send()
    all_parts.wait_send()

    for among, routes, landing, recv_sem in (
        (RELAYED_RIGHT, right_relays, from_left, right_recv), (RELAYED_LEFT, left_relays, from_right, left_recv)
    ):
        for through, target in routes.values():

            @pl.when(me == through)
            def _():
                passed = pl.ds(0, len(among))
                pltpu.make_async_remote_copy(
                    src_ref=relay.at[passed], dst_ref=landing.at[passed],
                    send_sem=relay_send.at[0], recv_sem=recv_sem.at[0],
                    device_id={"chain": jnp.int32(target)}, device_id_type=MESH,
                ).wait_send()

    @pl.when(has_left)
    def _():
        edge_copy.wait_send()
        pltpu.make_async_remote_copy(
            src_ref=to_left, dst_ref=from_right,
            send_sem=left_send.at[0], recv_sem=left_recv.at[0],
            device_id={"chain": lax.rem(me + chain - 1, chain)}, device_id_type=MESH,
        ).wait_send()

    @pl.when(has_right)
    def _():
        pltpu.make_async_remote_copy(
            src_ref=to_right, dst_ref=from_left,
            send_sem=right_send.at[0], recv_sem=right_recv.at[0],
            device_id={"chain": lax.rem(me + 1, chain)}, device_id_type=MESH,
        ).wait_send()

    receive(groups - 1)


def deliver(
    remapped, mass, moments, from_left, from_right, edges, coef, shift_of, base, beyond, triangle, mean_of,
    remapped_out, mass_out,
    last_remapped, last_mass, sem,
):
    done = remapped.shape[1] - GROUP
    early, late = pl.ds(0, done), pl.ds(done, GROUP)
    held = moments, from_left, from_right, edges, coef, shift_of, base, beyond, triangle
    copies = [
        pltpu.make_async_copy(source, target, sem.at[index])
        for index, (source, target) in enumerate((
            (remapped.at[:, early, :], remapped_out.at[:, early, :]),
            (mass.at[:, early, :], mass_out.at[:, early, :]),
            (last_remapped, remapped_out.at[:, late, :]),
            (last_mass, mass_out.at[:, late, :]),
        ))
    ]
    for copy in copies[:2]:
        copy.start()
    finish_group(done // GROUP, held, last_remapped, last_mass, done)
    for var in range(VARS):
        last_mass[var] = last_mass[var] / mean_of[var : var + 1, :]
    for copy in copies[2:]:
        copy.start()
    for copy in copies:
        copy.wait()


def solution(mesh):
    chain, cross = mesh.shape["chain"], mesh.shape["cross"]
    relays = corner_relays(mesh)

    def shards(moments, flags, shifts, fraction):
        row_count, pencils, cells = moments.shape
        assert row_count == ROWS and cells == BLOCK and pencils == BLOCK
        groups = pencils // GROUP
        dma = pltpu.SemaphoreType.DMA
        float_of = functools.partial(jax.ShapeDtypeStruct, dtype=jnp.float32)
        halo = (groups, SENT, TILE, BLOCK)
        block = pltpu.VMEM(halo, jnp.float32)
        results = float_of(moments.shape), float_of((VARS, pencils, cells))
        handed = results + (
            float_of(moments.shape), float_of(halo), float_of(halo), float_of((groups, EDGE_STEP, TILE, BLOCK)),
            float_of((COEFS, pencils, BLOCK)), jax.ShapeDtypeStruct((pencils, BLOCK), jnp.int32),
            float_of((VARS, pencils, BLOCK)), float_of((VARS, pencils, BLOCK)),
            jax.ShapeDtypeStruct((BLOCK, BLOCK), jnp.bfloat16), float_of((8, BLOCK)),
        )
        in_vmem = pl.BlockSpec(memory_space=pltpu.VMEM)
        in_hbm = pl.BlockSpec(memory_space=pltpu.HBM)
        ready = pl.pallas_call(
            functools.partial(kernel, chain, cross, relays),
            out_shape=handed,
            in_specs=[in_hbm] * 4,
            out_specs=(in_vmem,) * len(handed),
            scratch_shapes=[
                pltpu.VMEM(flags.shape, jnp.int32),
                pltpu.VMEM((1, pencils), jnp.int32),
                pltpu.VMEM((1, pencils), jnp.float32),
                block, block, block,
                pltpu.VMEM((groups, TILE, BLOCK), jnp.float32),
                pltpu.VMEM((groups // 2, TILE, BLOCK), jnp.float32),
                pltpu.VMEM((groups // 2, TILE, BLOCK), jnp.float32),
                pltpu.VMEM((chain, 8, pencils), jnp.float32),
                pltpu.VMEM((cross, 1, BLOCK), jnp.float32),
                pltpu.VMEM((BLOCK, pencils), jnp.float32),
                pltpu.VMEM((BLOCK, pencils), jnp.float32),
                dma((1,)), dma((groups,)), dma((1,)), dma((groups,)),
                dma((1,)), dma((groups // 2,)), dma((2,)), dma((2,)),
                pltpu.SemaphoreType.REGULAR, pltpu.SemaphoreType.REGULAR, dma((2,)), dma((5,)),
            ],
            compiler_params=pltpu.CompilerParams(
                collective_id=0, has_side_effects=True, vmem_limit_bytes=24 << 20
            ),
        )(*(
            pltpu.with_memory_space_constraint(value, pltpu.HBM)
            for value in (moments, flags, shifts.T, fraction.reshape(1, pencils))
        ))
        return pl.pallas_call(
            deliver,
            out_shape=results,
            in_specs=[in_vmem] * len(handed),
            out_specs=(in_hbm,) * 2,
            scratch_shapes=[
                pltpu.VMEM((ROWS, GROUP, BLOCK), jnp.float32),
                pltpu.VMEM((VARS, GROUP, BLOCK), jnp.float32),
                dma((4,)),
            ],
            compiler_params=pltpu.CompilerParams(vmem_limit_bytes=16 << 20),
        )(*ready)

    in_specs = (P(None, "cross", "chain"), P("cross", "chain"), P("cross", "chain"), P("cross"))
    out_specs = (P(None, "cross", "chain"), P(None, "cross", "chain"))
    return jax.shard_map(shards, mesh=mesh, in_specs=in_specs, out_specs=out_specs, check_vma=False)
```

```python
import functools

import jax
import numpy as np
import jax.numpy as jnp
from jax import lax
from jax.experimental import pallas as pl
from jax.experimental.pallas import tpu as pltpu
from jax.sharding import PartitionSpec as P

VARS = 5
MOMENTS = 4
BLOCK = 128
SHIFT_MAX = 48
ROWS = VARS * MOMENTS
SPAN = ROWS * SHIFT_MAX
FULL, HALF = SPAN // BLOCK, BLOCK // 2
TILE = 8
TILES = 2
GROUP = TILES * TILE
SENT = TILES * FULL + 1
EDGES = -(-ROWS // 8)
EDGE_STEP = TILES * EDGES
LATE = 2
ORDER_RIGHT, ORDER_LEFT = (0, 1, 3, 5, 6, 2, 4), (0, 2, 4, 6, 1, 3, 5)
RELAYED_RIGHT, RELAYED_LEFT = (1, 3, 5, 6), (1, 3, 5)
PAIRS = tuple((k, m) for k in range(1, MOMENTS) for m in range(k, MOMENTS))
COEFS = MOMENTS + 2 * len(PAIRS)
MESH = pl.DeviceIdType.MESH
HIGHEST = lax.Precision.HIGHEST

gauss_nodes = (-0.8611363115940526, -0.3399810435848563, 0.3399810435848563, 0.8611363115940526)
gauss_weights = (0.3478548451374538, 0.6521451548625461, 0.6521451548625461, 0.3478548451374538)


AFTER_FIRST, AFTER_LENGTH = SHIFT_MAX, SHIFT_MAX + 1
BEFORE_FIRST, BEFORE_LENGTH = 0, SHIFT_MAX


def place(row, first):
    chunk, lane = divmod((first + SHIFT_MAX * row) % SPAN, BLOCK)
    return chunk, lane, lane + SHIFT_MAX > BLOCK


def segments(first):
    held = [[] for _ in range(FULL + 1)]
    for row in range(ROWS):
        chunk, lane, splits = place(row, first)
        held[chunk].append((lane, row))
        if splits:
            held[chunk + 1].append((0, row))
    return [sorted(chunk) for chunk in held]


AFTER, BEFORE = segments(AFTER_FIRST), segments(BEFORE_FIRST)
WRAPPED = ROWS - 1


def turn_of(row):
    return (SHIFT_MAX * (row + 1)) % BLOCK


def edge_lane(row):
    return (turn_of(row) + SHIFT_MAX) % BLOCK


def legendre_values(point):
    return [
        jnp.ones_like(point),
        point,
        0.5 * (3.0 * point * point - 1.0),
        0.5 * (5.0 * point * point * point - 3.0 * point),
    ]


def interval_integrals(low_end, high_end, offset):
    half = 0.5 * (high_end - low_end)
    middle = 0.5 * (high_end + low_end)
    entries = [jnp.zeros_like(low_end) for _ in PAIRS]
    for node, weight in zip(gauss_nodes, gauss_weights):
        point = middle + half * node
        target = legendre_values(point)
        source = legendre_values(point + offset)
        scaled = [weight * half * value for value in target]
        for index, (k, m) in enumerate(PAIRS):
            entries[index] = entries[index] + scaled[k] * source[m]
    return entries


def partial_weights(fraction):
    shifted = 2.0 * fraction - 1.0
    square = shifted * shifted
    return [
        fraction,
        fraction * fraction - fraction,
        0.25 * (square * shifted - shifted),
        0.5 * (0.5 * (1.25 * square * square - 1.5 * square) + 0.125),
    ]


def corner_relays(mesh):
    ring = np.moveaxis(mesh.devices, mesh.axis_names.index("chain"), 0).reshape(mesh.shape["chain"], -1)[:, 0]
    if any(getattr(device, "coords", None) is None for device in ring):
        return {}, {}
    spots = [tuple(device.coords) for device in ring]
    rightward, leftward = {}, {}
    if len({spot[0] for spot in spots}) == 2 and len({spot[1] for spot in spots}) == 2:
        for index in range(len(spots) - 1):
            low, high = spots[index], spots[index + 1]
            if low[0] != high[0] and low[1] != high[1]:
                for found, source, target, pick in (
                    (rightward, index, index + 1, max), (leftward, index + 1, index, max)
                ):
                    corner = (spots[source][0], spots[target][1])
                    at = [i for i, spot in enumerate(spots) if spot[:2] == corner]
                    if at:
                        found[source] = (pick(at), target)
    return rightward, leftward


def exact_dot(value, ones):
    high = value.astype(jnp.bfloat16)
    rest = value - high.astype(jnp.float32)
    middle = rest.astype(jnp.bfloat16)
    low = (rest - middle.astype(jnp.float32)).astype(jnp.bfloat16)
    return sum(jnp.dot(part, ones, preferred_element_type=jnp.float32) for part in (low, middle, high))


def finish_group(group, held, remapped, mass, skipped):
    moments, from_left, from_right, edges, coef, shift_of, base, beyond, triangle = held
    lane = lax.broadcasted_iota(jnp.int32, (TILE, BLOCK), 1)
    halos, places_of = [], []
    for tile in range(GROUP // TILE):
        rows = pl.ds(pl.multiple_of(group * GROUP + tile * TILE, TILE), TILE)
        inner = pl.ds(tile * TILE, TILE)
        shift = shift_of[rows, :]
        ahead = shift >= 0
        put = pl.ds(pl.multiple_of(group * GROUP + tile * TILE - skipped, TILE), TILE)
        places_of.append((rows, put, shift, ahead))

        folded = {}
        for name, ref in (("right", from_right), ("left", from_left)):
            value = ref[group, SENT - 1]
            folded[name] = pltpu.roll(value, HALF, 1) if tile else value

        def fetch(name, ref, row, first):
            chunk, start, splits = place(row, first)
            values = [
                ref[group, TILES * index + tile] if index < FULL else folded[name]
                for index in ((chunk, chunk + 1) if splits else (chunk,))
            ]
            return jnp.where(lane >= start, *values) if splits else values[0]

        def halo_row(row):
            right = fetch("right", from_right, row, AFTER_FIRST)
            left = fetch("left", from_left, row, BEFORE_FIRST)
            edge = edges[group, EDGES * tile + row // 8]
            wrapped = row == WRAPPED
            value = left if wrapped else jnp.where(ahead, right, left)
            value = jnp.where(ahead & (lane == edge_lane(row)), edge, value)
            value = pltpu.roll(value, (BLOCK - turn_of(row)) % BLOCK, 1) if turn_of(row) else value
            return jnp.where(ahead & (lane < SHIFT_MAX), right, value) if wrapped else value

        halos.append([halo_row(row) for row in range(ROWS)])

    signed = []
    for (_, _, _, ahead), halo in zip(places_of, halos):
        for var in range(VARS):
            value = halo[MOMENTS * var]
            signed.append(jnp.where(
                ahead,
                jnp.where(lane < AFTER_LENGTH, value, 0.0),
                jnp.where(lane >= BLOCK - BEFORE_LENGTH, -value, 0.0),
            ))
    crossed = exact_dot(jnp.concatenate(signed, axis=0), triangle[...])

    for tile, ((rows, put, shift, ahead), halo) in enumerate(zip(places_of, halos)):
        turn = shift & (BLOCK - 1)
        outside = jnp.where(ahead, lane - turn, turn - 1 - lane) < 0
        outside_next = jnp.where(ahead, lane - turn - 1, turn - lane) < 0
        at = (lane + turn) & (BLOCK - 1)
        weight = [coef[m, rows, :] for m in range(MOMENTS)]
        inside, across = {}, {}
        for index, (k, m) in enumerate(PAIRS):
            inside[k, m] = coef[MOMENTS + index, rows, :]
            across[k, m] = coef[MOMENTS + len(PAIRS) + index, rows, :]

        def settle(value):
            return jnp.take_along_axis(value, at, axis=1, mode="promise_in_bounds")

        for var in range(VARS):
            here, after = [], []
            for order in range(MOMENTS):
                own = moments[MOMENTS * var + order, rows, :]
                other = halo[MOMENTS * var + order]
                here.append(jnp.where(outside, other, own))
                after.append(pltpu.roll(jnp.where(outside_next, other, own), BLOCK - 1, 1))
            filled = weight[0] * here[0]
            filled_after = weight[0] * after[0]
            for m in range(1, MOMENTS):
                filled = filled + weight[m] * here[m]
                filled_after = filled_after + weight[m] * after[m]
            rise = after[0] - here[0]
            remapped[MOMENTS * var, put, :] = settle(here[0] + (filled_after - filled))
            for k in range(1, MOMENTS):
                value = inside[k, k] * here[k] + across[k, k] * after[k]
                for m in range(1, MOMENTS):
                    if m == k:
                        continue
                    pair = (min(k, m), max(k, m))
                    term = inside[pair] * here[m] + across[pair] * after[m]
                    value = value - term if k > m and (k + m) % 2 else value + term
                edge = (2.0 if k % 2 == 0 else -2.0) * (weight[k] * rise)
                remapped[MOMENTS * var + k, put, :] = settle((k + 0.5) * (value + edge))
            index = (tile * VARS + var) * TILE
            start = jnp.where(
                outside, crossed[index : index + TILE] + beyond[var, rows, :], base[var, rows, :]
            )
            mass[var, put, :] = settle(start + filled)


def kernel(
    chain, cross, relays,
    moments_in, flags_in, shifts_in, fraction_in,
    remapped, mass, moments, from_left, from_right, edges, coef, shift_of, base, beyond, triangle, mean_of,
    flags, shifts, fraction,
    to_left, to_right, relay, own_edges, edges_out, edges_in,
    sums, parts, raw, starts,
    left_send, left_recv, right_send, right_recv, relay_send, relay_recv,
    sum_sem, part_sem, ready_sem, open_sem, edge_sem, input_sem,
):
    pencils = moments.shape[1]
    groups = pencils // GROUP
    me = lax.axis_index("chain")
    plane = lax.axis_index("cross")

    first_rows, later_rows = pl.ds(0, GROUP), pl.ds(GROUP, pencils - GROUP)
    inputs = [
        pltpu.make_async_copy(source, target, input_sem.at[index])
        for index, (source, target) in enumerate((
            (flags_in, flags),
            (moments_in.at[:, first_rows, :], moments.at[:, first_rows, :]),
            (moments_in.at[:, later_rows, :], moments.at[:, later_rows, :]),
            (shifts_in, shifts),
            (fraction_in, fraction),
        ))
    ]
    urgent, rest = inputs[:2], inputs[2:]
    for copy in urgent:
        copy.start()

    barrier = pltpu.get_barrier_semaphore()
    for step in range(1, chain):
        peer = lax.rem(me + step, chain)
        pl.semaphore_signal(barrier, inc=1, device_id={"chain": peer}, device_id_type=MESH)
    leads = me == 0

    @pl.when(leads)
    def _():
        for step in range(1, cross):
            peer = lax.rem(plane + step, cross)
            pl.semaphore_signal(barrier, inc=1, device_id={"cross": peer}, device_id_type=MESH)

    for copy in rest:
        copy.start()
    for copy in urgent:
        copy.wait()

    def leftward(group):
        return pltpu.make_async_remote_copy(
            src_ref=to_left.at[group], dst_ref=from_right.at[group],
            send_sem=left_send.at[0], recv_sem=left_recv.at[group],
            device_id={"chain": lax.rem(me + chain - 1, chain)}, device_id_type=MESH,
        )

    def rightward(group):
        return pltpu.make_async_remote_copy(
            src_ref=to_right.at[group], dst_ref=from_left.at[group],
            send_sem=right_send.at[0], recv_sem=right_recv.at[group],
            device_id={"chain": lax.rem(me + 1, chain)}, device_id_type=MESH,
        )

    has_left, has_right = me > 0, me < chain - 1

    sum_copies = [
        pltpu.make_async_remote_copy(
            src_ref=sums.at[me], dst_ref=sums.at[me],
            send_sem=sum_sem.at[0], recv_sem=sum_sem.at[1],
            device_id={"chain": lax.rem(me + step, chain)}, device_id_type=MESH,
        )
        for step in range(1, chain)
    ]
    others = pl.ds(0, chain - 1)
    all_sums = pltpu.make_async_remote_copy(
        src_ref=sums.at[others], dst_ref=sums.at[others],
        send_sem=sum_sem.at[0], recv_sem=sum_sem.at[1],
        device_id={"chain": lax.rem(me + 1, chain)}, device_id_type=MESH,
    )

    source_cell = lax.broadcasted_iota(jnp.int32, (BLOCK, BLOCK), 0)
    target_cell = lax.broadcasted_iota(jnp.int32, (BLOCK, BLOCK), 1)
    before_cell = jnp.where(source_cell < target_cell, 1.0, 0.0)

    def own_sums():
        total = jnp.zeros((pencils, BLOCK), jnp.float32)
        for var in range(VARS):
            pick = jnp.where(target_cell == var, 1.0, 0.0)
            both = jnp.concatenate([before_cell, pick], axis=1).astype(jnp.bfloat16)
            summed = exact_dot(moments[MOMENTS * var], both)
            base[var] = summed[:, :BLOCK]
            total = total + summed[:, BLOCK:]
        sums[me] = jnp.where(
            lax.broadcasted_iota(jnp.int32, (8, BLOCK), 0) == VARS,
            jnp.sum(total, axis=0, keepdims=True), jnp.transpose(total)[:8],
        )

    def send_sums():
        for copy in sum_copies:
            copy.start()

    lane = lax.broadcasted_iota(jnp.int32, (TILE, BLOCK), 1)
    spot = lane & 15

    def pack(group):
        halves = {}
        edge = None
        for tile in range(TILES):
            rows = pl.ds(group * GROUP + tile * TILE, TILE)
            flag = flags[rows, :]
            keep_linear, keep_full = flag <= 1, flag == 0
            rolled = []
            for row in range(ROWS):
                value = moments[row, rows, :]
                order = row % MOMENTS
                if order > 0:
                    value = jnp.where(keep_linear if order == 1 else keep_full, value, 0.0)
                    moments[row, rows, :] = value
                rolled.append(pltpu.roll(value, turn_of(row), 1) if turn_of(row) else value)
            for side, (held, target) in enumerate(((AFTER, to_left), (BEFORE, to_right))):
                for chunk in range(FULL + 1):
                    value = None
                    for start, row in held[chunk]:
                        part = moments[row, rows, :] if row == WRAPPED and side == 0 else rolled[row]
                        value = part if value is None else jnp.where(lane >= start, part, value)
                    if chunk < FULL:
                        target[group, TILES * chunk + tile] = value
                    else:
                        halves[side, tile] = value
            for index in range(EDGES):
                value = None
                for row in range(8 * index, min(8 * index + 8, ROWS)):
                    here = (lane >> 4) == edge_lane(row) // 16
                    value = rolled[row] if value is None else jnp.where(here, rolled[row], value)
                at = EDGES * tile + index
                value = pltpu.roll(value, at, 1) if at else value
                edge = value if edge is None else jnp.where(spot >= at, value, edge)
        for side, target in enumerate((to_left, to_right)):
            target[group, SENT - 1] = jnp.where(
                lane < HALF, halves[side, 0], pltpu.roll(halves[side, 1], HALF, 1)
            )
        own_edges[group] = edge

    edge_copy = pltpu.make_async_remote_copy(
        src_ref=edges_out, dst_ref=edges_in,
        send_sem=edge_sem.at[0], recv_sem=edge_sem.at[1],
        device_id={"chain": lax.rem(me + chain - 1, chain)}, device_id_type=MESH,
    )

    def send_edges():
        for index in range(groups // 2):
            edges_out[index] = jnp.where(
                spot < EDGE_STEP, own_edges[2 * index], pltpu.roll(own_edges[2 * index + 1], EDGE_STEP, 1)
            )

        @pl.when(has_left)
        def _():
            edge_copy.start()

    def receive_edges():
        @pl.when(has_right)
        def _():
            edge_copy.wait_recv()

        for group in range(groups):
            value = edges_in[group // 2]
            for at in range(EDGE_STEP):
                back = EDGE_STEP * (group % 2) + at
                edges[group, at] = pltpu.roll(value, BLOCK - back, 1) if back else value

    right_relays, left_relays = relays

    def to_relay(group, source, send_sem, through):
        return pltpu.make_async_remote_copy(
            src_ref=source.at[group], dst_ref=relay.at[group],
            send_sem=send_sem.at[0], recv_sem=relay_recv.at[group // 2],
            device_id={"chain": jnp.int32(through)}, device_id_type=MESH,
        )

    def onward(group, landing, recv_sem, target):
        return pltpu.make_async_remote_copy(
            src_ref=relay.at[group], dst_ref=landing.at[group],
            send_sem=relay_send.at[0], recv_sem=recv_sem.at[group],
            device_id={"chain": jnp.int32(target)}, device_id_type=MESH,
        )

    def send(group, direct, wanted, among, routes, source, send_sem):
        group = jnp.int32(group)
        relayed = functools.reduce(jnp.logical_or, [group == index for index in among])
        for start, (through, _) in routes.items():
            wanted = wanted & ((me != start) | jnp.logical_not(relayed))

            @pl.when((me == start) & relayed)
            def _():
                to_relay(group, source, send_sem, through).start()

        if direct is rightward:
            for start in routes:
                wanted = wanted & ((me != start) | (group < LATE))

        @pl.when(wanted)
        def _():
            direct(group).start()

    def send_late():
        for start in right_relays:

            @pl.when(me == start)
            def _():
                for group in range(groups):
                    if group >= LATE and group not in RELAYED_RIGHT:
                        rightward(group).start()

    def send_both(group):
        send(group, leftward, has_left, RELAYED_LEFT, left_relays, to_left, left_send)
        send(group, rightward, has_right, RELAYED_RIGHT, right_relays, to_right, right_send)

    def pack_next(group, carry):
        pack(group)
        return carry

    def send_next(group, carry):
        send_both(group)
        return carry

    pack(0)
    soon = (lax.rem(me, 2) == 1) | (me == 0)

    @pl.when(soon)
    def _():
        for copy in rest:
            copy.wait()
        own_sums()
        pack(1)

    pl.semaphore_wait(barrier, jnp.where(leads, chain - 1 + cross - 1, chain - 1))
    send_both(0)

    @pl.when(leads)
    def _():
        for step in range(1, cross):
            peer = lax.rem(plane + step, cross)
            pl.semaphore_signal(ready_sem, inc=1, device_id={"cross": peer}, device_id_type=MESH)

    @pl.when(jnp.logical_not(soon))
    def _():
        for copy in rest:
            copy.wait()
        own_sums()

    send_sums()

    @pl.when(jnp.logical_not(soon))
    def _():
        pack(1)

    for group in range(1, 2):
        send_both(group)
    for group in range(2, groups):
        pack(group)
    send_edges()
    for group in range(2, groups):
        send_both(group)

    part_copies = [
        pltpu.make_async_remote_copy(
            src_ref=parts.at[plane], dst_ref=parts.at[plane],
            send_sem=part_sem.at[0], recv_sem=part_sem.at[1],
            device_id={"cross": lax.rem(plane + step, cross)}, device_id_type=MESH,
        )
        for step in range(1, cross)
    ]

    elsewhere = pl.ds(0, cross - 1)
    all_parts = pltpu.make_async_remote_copy(
        src_ref=parts.at[elsewhere], dst_ref=parts.at[elsewhere],
        send_sem=part_sem.at[0], recv_sem=part_sem.at[1],
        device_id={"cross": lax.rem(plane + 1, cross)}, device_id_type=MESH,
    )

    def open_planes():
        @pl.when(leads)
        def _():
            pl.semaphore_wait(ready_sem, cross - 1)
            for peer in range(1, chain):
                pl.semaphore_signal(open_sem, inc=1, device_id={"chain": jnp.int32(peer)}, device_id_type=MESH)

    def send_parts():
        @pl.when(jnp.logical_not(leads))
        def _():
            pl.semaphore_wait(open_sem, 1)

        for copy in part_copies:
            copy.start()

    def pass_on(index, sides=(0, 1)):
        for side, (among, routes, source, send_sem, landing, recv_sem) in enumerate((
            (RELAYED_RIGHT, right_relays, to_right, right_send, from_left, right_recv),
            (RELAYED_LEFT, left_relays, to_left, left_send, from_right, left_recv),
        )):
            if side not in sides:
                continue
            for through, target in routes.values():
                if index >= len(among):
                    continue
                group = among[index]

                @pl.when(me == through)
                def _():
                    to_relay(group, source, send_sem, through).wait_recv()
                    onward(group, landing, recv_sem, target).start()

    shift_row = shifts[...]

    def reduce_chain():
        starts[...] = jnp.zeros_like(starts)
        all_sums.wait_recv()
        before = jnp.zeros((8, pencils), jnp.float32)
        whole = jnp.zeros((1, BLOCK), jnp.float32)
        for index in range(chain):
            before = before + jnp.where(index < me, sums[index], 0.0)
            whole = whole + sums[index, VARS : VARS + 1]
        parts[plane] = whole
        starts[0:8, :] = before
        starts[8:16, :] = before + jnp.where(shift_row >= 0, sums[me], 0.0)

    def spread_starts():
        turned = jnp.transpose(starts[...])
        for var in range(VARS):
            base[var] = base[var] + turned[:, var : var + 1]
            beyond[var] = jnp.broadcast_to(turned[:, 8 + var : 9 + var], (pencils, BLOCK))

    open_planes()
    pass_on(0)
    pass_on(1)
    reduce_chain()
    for index in range(2, len(RELAYED_RIGHT)):
        pass_on(index, (0,))
    send_parts()
    send_late()

    @pl.when(me == 0)
    def _():
        from_left[...] = jnp.zeros_like(from_left)

    @pl.when(me == chain - 1)
    def _():
        from_right[...] = jnp.zeros_like(from_right)
        edges_in[...] = jnp.zeros_like(edges_in)

    f = fraction[...]
    first = interval_integrals(-1.0 + 0.0 * f, 1.0 - 2.0 * f, 2.0 * f)
    second = interval_integrals(1.0 - 2.0 * f, 1.0 + 0.0 * f, 2.0 * f - 2.0)
    raw[...] = jnp.zeros_like(raw)
    columns = partial_weights(f) + first + second + [shift_row.astype(jnp.float32)]
    for index, value in enumerate(columns):
        raw[index : index + 1, :] = value
    turned = jnp.transpose(raw[...])
    for index in range(COEFS):
        coef[index] = jnp.broadcast_to(turned[:, index : index + 1], (pencils, BLOCK))
    shift_of[...] = jnp.broadcast_to(turned[:, COEFS : COEFS + 1], (pencils, BLOCK)).astype(jnp.int32)

    up_to_edge = jnp.where(source_cell < BLOCK // 2, before_cell, 1.0 - before_cell)
    triangle[...] = up_to_edge.astype(jnp.bfloat16)
    for index in range(2, len(RELAYED_LEFT)):
        pass_on(index, (1,))
    spread_starts()
    receive_edges()


    held = moments, from_left, from_right, edges, coef, shift_of, base, beyond, triangle

    def receive(group):
        @pl.when(has_right)
        def _():
            leftward(group).wait_recv()

        @pl.when(has_left)
        def _():
            rightward(group).wait_recv()

    def turn_to(step):
        group = jnp.int32(step)
        for order, routes in ((ORDER_RIGHT, right_relays), (ORDER_LEFT, left_relays)):
            for _, target in routes.values():
                for index, other in enumerate(order):
                    group = jnp.where((me == target) & (step == index), other, group)
        return group

    def remap(step, carry):
        group = turn_to(step)
        receive(group)
        finish_group(group, held, remapped, mass, 0)
        return carry

    lax.fori_loop(0, groups - 1, remap, 0)

    all_parts.wait_recv()
    grand = parts[0]
    for index in range(1, cross):
        grand = grand + parts[index]
    mean = grand / float(pencils * cross)
    for var in range(VARS):
        mean_of[var : var + 1, :] = jnp.broadcast_to(mean[:, var : var + 1], (1, BLOCK))
    done = pl.ds(0, pencils - GROUP)
    for var in range(VARS):
        mass[var, done, :] = mass[var, done, :] / mean_of[var : var + 1, :]

    all_sums.wait_send()
    all_parts.wait_send()

    for among, routes, landing, recv_sem in (
        (RELAYED_RIGHT, right_relays, from_left, right_recv), (RELAYED_LEFT, left_relays, from_right, left_recv)
    ):
        for through, target in routes.values():

            @pl.when(me == through)
            def _():
                passed = pl.ds(0, len(among))
                pltpu.make_async_remote_copy(
                    src_ref=relay.at[passed], dst_ref=landing.at[passed],
                    send_sem=relay_send.at[0], recv_sem=recv_sem.at[0],
                    device_id={"chain": jnp.int32(target)}, device_id_type=MESH,
                ).wait_send()

    @pl.when(has_left)
    def _():
        edge_copy.wait_send()
        pltpu.make_async_remote_copy(
            src_ref=to_left, dst_ref=from_right,
            send_sem=left_send.at[0], recv_sem=left_recv.at[0],
            device_id={"chain": lax.rem(me + chain - 1, chain)}, device_id_type=MESH,
        ).wait_send()

    @pl.when(has_right)
    def _():
        pltpu.make_async_remote_copy(
            src_ref=to_right, dst_ref=from_left,
            send_sem=right_send.at[0], recv_sem=right_recv.at[0],
            device_id={"chain": lax.rem(me + 1, chain)}, device_id_type=MESH,
        ).wait_send()

    receive(groups - 1)


def deliver(
    remapped, mass, moments, from_left, from_right, edges, coef, shift_of, base, beyond, triangle, mean_of,
    remapped_out, mass_out,
    last_remapped, last_mass, sem,
):
    done = remapped.shape[1] - GROUP
    early, late = pl.ds(0, done), pl.ds(done, GROUP)
    held = moments, from_left, from_right, edges, coef, shift_of, base, beyond, triangle
    copies = [
        pltpu.make_async_copy(source, target, sem.at[index])
        for index, (source, target) in enumerate((
            (remapped.at[:, early, :], remapped_out.at[:, early, :]),
            (mass.at[:, early, :], mass_out.at[:, early, :]),
            (last_remapped, remapped_out.at[:, late, :]),
            (last_mass, mass_out.at[:, late, :]),
        ))
    ]
    for copy in copies[:2]:
        copy.start()
    finish_group(done // GROUP, held, last_remapped, last_mass, done)
    for var in range(VARS):
        last_mass[var] = last_mass[var] / mean_of[var : var + 1, :]
    for copy in copies[2:]:
        copy.start()
    for copy in copies:
        copy.wait()


def solution(mesh):
    chain, cross = mesh.shape["chain"], mesh.shape["cross"]
    relays = corner_relays(mesh)

    def shards(moments, flags, shifts, fraction):
        row_count, pencils, cells = moments.shape
        assert row_count == ROWS and cells == BLOCK and pencils == BLOCK
        groups = pencils // GROUP
        dma = pltpu.SemaphoreType.DMA
        float_of = functools.partial(jax.ShapeDtypeStruct, dtype=jnp.float32)
        halo = (groups, SENT, TILE, BLOCK)
        block = pltpu.VMEM(halo, jnp.float32)
        results = float_of(moments.shape), float_of((VARS, pencils, cells))
        handed = results + (
            float_of(moments.shape), float_of(halo), float_of(halo), float_of((groups, EDGE_STEP, TILE, BLOCK)),
            float_of((COEFS, pencils, BLOCK)), jax.ShapeDtypeStruct((pencils, BLOCK), jnp.int32),
            float_of((VARS, pencils, BLOCK)), float_of((VARS, pencils, BLOCK)),
            jax.ShapeDtypeStruct((BLOCK, BLOCK), jnp.bfloat16), float_of((8, BLOCK)),
        )
        in_vmem = pl.BlockSpec(memory_space=pltpu.VMEM)
        in_hbm = pl.BlockSpec(memory_space=pltpu.HBM)
        ready = pl.pallas_call(
            functools.partial(kernel, chain, cross, relays),
            out_shape=handed,
            in_specs=[in_hbm] * 4,
            out_specs=(in_vmem,) * len(handed),
            scratch_shapes=[
                pltpu.VMEM(flags.shape, jnp.int32),
                pltpu.VMEM((1, pencils), jnp.int32),
                pltpu.VMEM((1, pencils), jnp.float32),
                block, block, block,
                pltpu.VMEM((groups, TILE, BLOCK), jnp.float32),
                pltpu.VMEM((groups // 2, TILE, BLOCK), jnp.float32),
                pltpu.VMEM((groups // 2, TILE, BLOCK), jnp.float32),
                pltpu.VMEM((chain, 8, pencils), jnp.float32),
                pltpu.VMEM((cross, 1, BLOCK), jnp.float32),
                pltpu.VMEM((BLOCK, pencils), jnp.float32),
                pltpu.VMEM((BLOCK, pencils), jnp.float32),
                dma((1,)), dma((groups,)), dma((1,)), dma((groups,)),
                dma((1,)), dma((groups // 2,)), dma((2,)), dma((2,)),
                pltpu.SemaphoreType.REGULAR, pltpu.SemaphoreType.REGULAR, dma((2,)), dma((5,)),
            ],
            compiler_params=pltpu.CompilerParams(
                collective_id=0, has_side_effects=True, vmem_limit_bytes=24 << 20
            ),
        )(*(
            pltpu.with_memory_space_constraint(value, pltpu.HBM)
            for value in (moments, flags, shifts.T, fraction.reshape(1, pencils))
        ))
        return pl.pallas_call(
            deliver,
            out_shape=results,
            in_specs=[in_vmem] * len(handed),
            out_specs=(in_hbm,) * 2,
            scratch_shapes=[
                pltpu.VMEM((ROWS, GROUP, BLOCK), jnp.float32),
                pltpu.VMEM((VARS, GROUP, BLOCK), jnp.float32),
                dma((4,)),
            ],
            compiler_params=pltpu.CompilerParams(vmem_limit_bytes=16 << 20),
        )(*ready)

    in_specs = (P(None, "cross", "chain"), P("cross", "chain"), P("cross", "chain"), P("cross"))
    out_specs = (P(None, "cross", "chain"), P(None, "cross", "chain"))
    return jax.shard_map(shards, mesh=mesh, in_specs=in_specs, out_specs=out_specs, check_vma=False)
```

```python
import functools

import jax
import numpy as np
import jax.numpy as jnp
from jax import lax
from jax.experimental import pallas as pl
from jax.experimental.pallas import tpu as pltpu
from jax.sharding import PartitionSpec as P

VARS = 5
MOMENTS = 4
BLOCK = 128
SHIFT_MAX = 48
ROWS = VARS * MOMENTS
SPAN = ROWS * SHIFT_MAX
FULL, HALF = SPAN // BLOCK, BLOCK // 2
TILE = 8
TILES = 2
GROUP = TILES * TILE
SENT = TILES * FULL + 1
EDGES = -(-ROWS // 8)
EDGE_STEP = TILES * EDGES
LATE = 2
ORDER_RIGHT, ORDER_LEFT = (0, 1, 3, 5, 6, 2, 4), (0, 2, 4, 6, 1, 3, 5)
RELAYED_RIGHT, RELAYED_LEFT = (1, 3, 5, 6), (1, 3, 5)
PAIRS = tuple((k, m) for k in range(1, MOMENTS) for m in range(k, MOMENTS))
COEFS = MOMENTS + 2 * len(PAIRS)
MESH = pl.DeviceIdType.MESH
HIGHEST = lax.Precision.HIGHEST

gauss_nodes = (-0.8611363115940526, -0.3399810435848563, 0.3399810435848563, 0.8611363115940526)
gauss_weights = (0.3478548451374538, 0.6521451548625461, 0.6521451548625461, 0.3478548451374538)


AFTER_FIRST, AFTER_LENGTH = SHIFT_MAX, SHIFT_MAX + 1
BEFORE_FIRST, BEFORE_LENGTH = 0, SHIFT_MAX


def place(row, first):
    chunk, lane = divmod((first + SHIFT_MAX * row) % SPAN, BLOCK)
    return chunk, lane, lane + SHIFT_MAX > BLOCK


def segments(first):
    held = [[] for _ in range(FULL + 1)]
    for row in range(ROWS):
        chunk, lane, splits = place(row, first)
        held[chunk].append((lane, row))
        if splits:
            held[chunk + 1].append((0, row))
    return [sorted(chunk) for chunk in held]


AFTER, BEFORE = segments(AFTER_FIRST), segments(BEFORE_FIRST)
WRAPPED = ROWS - 1


def turn_of(row):
    return (SHIFT_MAX * (row + 1)) % BLOCK


def edge_lane(row):
    return (turn_of(row) + SHIFT_MAX) % BLOCK


def legendre_values(point):
    return [
        jnp.ones_like(point),
        point,
        0.5 * (3.0 * point * point - 1.0),
        0.5 * (5.0 * point * point * point - 3.0 * point),
    ]


def interval_integrals(low_end, high_end, offset):
    half = 0.5 * (high_end - low_end)
    middle = 0.5 * (high_end + low_end)
    entries = [jnp.zeros_like(low_end) for _ in PAIRS]
    for node, weight in zip(gauss_nodes, gauss_weights):
        point = middle + half * node
        target = legendre_values(point)
        source = legendre_values(point + offset)
        scaled = [weight * half * value for value in target]
        for index, (k, m) in enumerate(PAIRS):
            entries[index] = entries[index] + scaled[k] * source[m]
    return entries


def partial_weights(fraction):
    shifted = 2.0 * fraction - 1.0
    square = shifted * shifted
    return [
        fraction,
        fraction * fraction - fraction,
        0.25 * (square * shifted - shifted),
        0.5 * (0.5 * (1.25 * square * square - 1.5 * square) + 0.125),
    ]


def corner_relays(mesh):
    ring = np.moveaxis(mesh.devices, mesh.axis_names.index("chain"), 0).reshape(mesh.shape["chain"], -1)[:, 0]
    if any(getattr(device, "coords", None) is None for device in ring):
        return {}, {}
    spots = [tuple(device.coords) for device in ring]
    rightward, leftward = {}, {}
    if len({spot[0] for spot in spots}) == 2 and len({spot[1] for spot in spots}) == 2:
        for index in range(len(spots) - 1):
            low, high = spots[index], spots[index + 1]
            if low[0] != high[0] and low[1] != high[1]:
                for found, source, target, pick in (
                    (rightward, index, index + 1, max), (leftward, index + 1, index, max)
                ):
                    corner = (spots[source][0], spots[target][1])
                    at = [i for i, spot in enumerate(spots) if spot[:2] == corner]
                    if at:
                        found[source] = (pick(at), target)
    return rightward, leftward


def exact_dot(value, ones):
    high = value.astype(jnp.bfloat16)
    rest = value - high.astype(jnp.float32)
    middle = rest.astype(jnp.bfloat16)
    low = (rest - middle.astype(jnp.float32)).astype(jnp.bfloat16)
    return sum(jnp.dot(part, ones, preferred_element_type=jnp.float32) for part in (low, middle, high))


def finish_group(group, held, remapped, mass, skipped):
    moments, from_left, from_right, edges, coef, shift_of, base, beyond, triangle = held
    lane = lax.broadcasted_iota(jnp.int32, (TILE, BLOCK), 1)
    halos, places_of = [], []
    for tile in range(GROUP // TILE):
        rows = pl.ds(pl.multiple_of(group * GROUP + tile * TILE, TILE), TILE)
        inner = pl.ds(tile * TILE, TILE)
        shift = shift_of[rows, :]
        ahead = shift >= 0
        put = pl.ds(pl.multiple_of(group * GROUP + tile * TILE - skipped, TILE), TILE)
        places_of.append((rows, put, shift, ahead))

        folded = {}
        for name, ref in (("right", from_right), ("left", from_left)):
            value = ref[group, SENT - 1]
            folded[name] = pltpu.roll(value, HALF, 1) if tile else value

        def fetch(name, ref, row, first):
            chunk, start, splits = place(row, first)
            values = [
                ref[group, TILES * index + tile] if index < FULL else folded[name]
                for index in ((chunk, chunk + 1) if splits else (chunk,))
            ]
            return jnp.where(lane >= start, *values) if splits else values[0]

        def halo_row(row):
            right = fetch("right", from_right, row, AFTER_FIRST)
            left = fetch("left", from_left, row, BEFORE_FIRST)
            edge = edges[group, EDGES * tile + row // 8]
            wrapped = row == WRAPPED
            value = left if wrapped else jnp.where(ahead, right, left)
            value = jnp.where(ahead & (lane == edge_lane(row)), edge, value)
            value = pltpu.roll(value, (BLOCK - turn_of(row)) % BLOCK, 1) if turn_of(row) else value
            return jnp.where(ahead & (lane < SHIFT_MAX), right, value) if wrapped else value

        halos.append([halo_row(row) for row in range(ROWS)])

    signed = []
    for (_, _, _, ahead), halo in zip(places_of, halos):
        for var in range(VARS):
            value = halo[MOMENTS * var]
            signed.append(jnp.where(
                ahead,
                jnp.where(lane < AFTER_LENGTH, value, 0.0),
                jnp.where(lane >= BLOCK - BEFORE_LENGTH, -value, 0.0),
            ))
    crossed = exact_dot(jnp.concatenate(signed, axis=0), triangle[...])

    for tile, ((rows, put, shift, ahead), halo) in enumerate(zip(places_of, halos)):
        turn = shift & (BLOCK - 1)
        outside = jnp.where(ahead, lane - turn, turn - 1 - lane) < 0
        outside_next = jnp.where(ahead, lane - turn - 1, turn - lane) < 0
        at = (lane + turn) & (BLOCK - 1)
        weight = [coef[m, rows, :] for m in range(MOMENTS)]
        inside, across = {}, {}
        for index, (k, m) in enumerate(PAIRS):
            inside[k, m] = coef[MOMENTS + index, rows, :]
            across[k, m] = coef[MOMENTS + len(PAIRS) + index, rows, :]

        def settle(value):
            return jnp.take_along_axis(value, at, axis=1, mode="promise_in_bounds")

        for var in range(VARS):
            here, after = [], []
            for order in range(MOMENTS):
                own = moments[MOMENTS * var + order, rows, :]
                other = halo[MOMENTS * var + order]
                here.append(jnp.where(outside, other, own))
                after.append(pltpu.roll(jnp.where(outside_next, other, own), BLOCK - 1, 1))
            filled = weight[0] * here[0]
            filled_after = weight[0] * after[0]
            for m in range(1, MOMENTS):
                filled = filled + weight[m] * here[m]
                filled_after = filled_after + weight[m] * after[m]
            rise = after[0] - here[0]
            remapped[MOMENTS * var, put, :] = settle(here[0] + (filled_after - filled))
            for k in range(1, MOMENTS):
                value = inside[k, k] * here[k] + across[k, k] * after[k]
                for m in range(1, MOMENTS):
                    if m == k:
                        continue
                    pair = (min(k, m), max(k, m))
                    term = inside[pair] * here[m] + across[pair] * after[m]
                    value = value - term if k > m and (k + m) % 2 else value + term
                edge = (2.0 if k % 2 == 0 else -2.0) * (weight[k] * rise)
                remapped[MOMENTS * var + k, put, :] = settle((k + 0.5) * (value + edge))
            index = (tile * VARS + var) * TILE
            start = jnp.where(
                outside, crossed[index : index + TILE] + beyond[var, rows, :], base[var, rows, :]
            )
            mass[var, put, :] = settle(start + filled)


def kernel(
    chain, cross, relays,
    moments_in, flags_in, shifts_in, fraction_in,
    remapped, mass, moments, from_left, from_right, edges, coef, shift_of, base, beyond, triangle, mean_of,
    flags, shifts, fraction,
    to_left, to_right, relay, own_edges, edges_out, edges_in,
    sums, parts, raw, starts,
    left_send, left_recv, right_send, right_recv, relay_send, relay_recv,
    sum_sem, part_sem, ready_sem, open_sem, edge_sem, input_sem,
):
    pencils = moments.shape[1]
    groups = pencils // GROUP
    me = lax.axis_index("chain")
    plane = lax.axis_index("cross")

    first_rows, later_rows = pl.ds(0, GROUP), pl.ds(GROUP, pencils - GROUP)
    inputs = [
        pltpu.make_async_copy(source, target, input_sem.at[index])
        for index, (source, target) in enumerate((
            (flags_in, flags),
            (moments_in.at[:, first_rows, :], moments.at[:, first_rows, :]),
            (moments_in.at[:, later_rows, :], moments.at[:, later_rows, :]),
            (shifts_in, shifts),
            (fraction_in, fraction),
        ))
    ]
    urgent, rest = inputs[:2], inputs[2:]
    for copy in urgent:
        copy.start()

    barrier = pltpu.get_barrier_semaphore()
    for step in range(1, chain):
        peer = lax.rem(me + step, chain)
        pl.semaphore_signal(barrier, inc=1, device_id={"chain": peer}, device_id_type=MESH)
    leads = me == 0

    @pl.when(leads)
    def _():
        for step in range(1, cross):
            peer = lax.rem(plane + step, cross)
            pl.semaphore_signal(barrier, inc=1, device_id={"cross": peer}, device_id_type=MESH)

    for copy in rest:
        copy.start()
    for copy in urgent:
        copy.wait()

    def leftward(group):
        return pltpu.make_async_remote_copy(
            src_ref=to_left.at[group], dst_ref=from_right.at[group],
            send_sem=left_send.at[0], recv_sem=left_recv.at[group],
            device_id={"chain": lax.rem(me + chain - 1, chain)}, device_id_type=MESH,
        )

    def rightward(group):
        return pltpu.make_async_remote_copy(
            src_ref=to_right.at[group], dst_ref=from_left.at[group],
            send_sem=right_send.at[0], recv_sem=right_recv.at[group],
            device_id={"chain": lax.rem(me + 1, chain)}, device_id_type=MESH,
        )

    has_left, has_right = me > 0, me < chain - 1

    sum_copies = [
        pltpu.make_async_remote_copy(
            src_ref=sums.at[me], dst_ref=sums.at[me],
            send_sem=sum_sem.at[0], recv_sem=sum_sem.at[1],
            device_id={"chain": lax.rem(me + step, chain)}, device_id_type=MESH,
        )
        for step in range(1, chain)
    ]
    others = pl.ds(0, chain - 1)
    all_sums = pltpu.make_async_remote_copy(
        src_ref=sums.at[others], dst_ref=sums.at[others],
        send_sem=sum_sem.at[0], recv_sem=sum_sem.at[1],
        device_id={"chain": lax.rem(me + 1, chain)}, device_id_type=MESH,
    )

    source_cell = lax.broadcasted_iota(jnp.int32, (BLOCK, BLOCK), 0)
    target_cell = lax.broadcasted_iota(jnp.int32, (BLOCK, BLOCK), 1)
    before_cell = jnp.where(source_cell < target_cell, 1.0, 0.0)

    def own_sums():
        total = jnp.zeros((pencils, BLOCK), jnp.float32)
        for var in range(VARS):
            pick = jnp.where(target_cell == var, 1.0, 0.0)
            both = jnp.concatenate([before_cell, pick], axis=1).astype(jnp.bfloat16)
            summed = exact_dot(moments[MOMENTS * var], both)
            base[var] = summed[:, :BLOCK]
            total = total + summed[:, BLOCK:]
        sums[me] = jnp.where(
            lax.broadcasted_iota(jnp.int32, (8, BLOCK), 0) == VARS,
            jnp.sum(total, axis=0, keepdims=True), jnp.transpose(total)[:8],
        )

    def send_sums():
        for copy in sum_copies:
            copy.start()

    lane = lax.broadcasted_iota(jnp.int32, (TILE, BLOCK), 1)
    spot = lane & 15

    def pack(group):
        halves = {}
        edge = None
        for tile in range(TILES):
            rows = pl.ds(group * GROUP + tile * TILE, TILE)
            flag = flags[rows, :]
            keep_linear, keep_full = flag <= 1, flag == 0
            rolled = []
            for row in range(ROWS):
                value = moments[row, rows, :]
                order = row % MOMENTS
                if order > 0:
                    value = jnp.where(keep_linear if order == 1 else keep_full, value, 0.0)
                    moments[row, rows, :] = value
                rolled.append(pltpu.roll(value, turn_of(row), 1) if turn_of(row) else value)
            for side, (held, target) in enumerate(((AFTER, to_left), (BEFORE, to_right))):
                for chunk in range(FULL + 1):
                    value = None
                    for start, row in held[chunk]:
                        part = moments[row, rows, :] if row == WRAPPED and side == 0 else rolled[row]
                        value = part if value is None else jnp.where(lane >= start, part, value)
                    if chunk < FULL:
                        target[group, TILES * chunk + tile] = value
                    else:
                        halves[side, tile] = value
            for index in range(EDGES):
                value = None
                for row in range(8 * index, min(8 * index + 8, ROWS)):
                    here = (lane >> 4) == edge_lane(row) // 16
                    value = rolled[row] if value is None else jnp.where(here, rolled[row], value)
                at = EDGES * tile + index
                value = pltpu.roll(value, at, 1) if at else value
                edge = value if edge is None else jnp.where(spot >= at, value, edge)
        for side, target in enumerate((to_left, to_right)):
            target[group, SENT - 1] = jnp.where(
                lane < HALF, halves[side, 0], pltpu.roll(halves[side, 1], HALF, 1)
            )
        own_edges[group] = edge

    edge_copy = pltpu.make_async_remote_copy(
        src_ref=edges_out, dst_ref=edges_in,
        send_sem=edge_sem.at[0], recv_sem=edge_sem.at[1],
        device_id={"chain": lax.rem(me + chain - 1, chain)}, device_id_type=MESH,
    )

    def send_edges():
        for index in range(groups // 2):
            edges_out[index] = jnp.where(
                spot < EDGE_STEP, own_edges[2 * index], pltpu.roll(own_edges[2 * index + 1], EDGE_STEP, 1)
            )

        @pl.when(has_left)
        def _():
            edge_copy.start()

    def receive_edges():
        @pl.when(has_right)
        def _():
            edge_copy.wait_recv()

        for group in range(groups):
            value = edges_in[group // 2]
            for at in range(EDGE_STEP):
                back = EDGE_STEP * (group % 2) + at
                edges[group, at] = pltpu.roll(value, BLOCK - back, 1) if back else value

    right_relays, left_relays = relays

    def to_relay(group, source, send_sem, through):
        return pltpu.make_async_remote_copy(
            src_ref=source.at[group], dst_ref=relay.at[group],
            send_sem=send_sem.at[0], recv_sem=relay_recv.at[group // 2],
            device_id={"chain": jnp.int32(through)}, device_id_type=MESH,
        )

    def onward(group, landing, recv_sem, target):
        return pltpu.make_async_remote_copy(
            src_ref=relay.at[group], dst_ref=landing.at[group],
            send_sem=relay_send.at[0], recv_sem=recv_sem.at[group],
            device_id={"chain": jnp.int32(target)}, device_id_type=MESH,
        )

    def send(group, direct, wanted, among, routes, source, send_sem):
        group = jnp.int32(group)
        relayed = functools.reduce(jnp.logical_or, [group == index for index in among])
        for start, (through, _) in routes.items():
            wanted = wanted & ((me != start) | jnp.logical_not(relayed))

            @pl.when((me == start) & relayed)
            def _():
                to_relay(group, source, send_sem, through).start()

        if direct is rightward:
            for start in routes:
                wanted = wanted & ((me != start) | (group < LATE))

        @pl.when(wanted)
        def _():
            direct(group).start()

    def send_late():
        for start in right_relays:

            @pl.when(me == start)
            def _():
                for group in range(groups):
                    if group >= LATE and group not in RELAYED_RIGHT:
                        rightward(group).start()

    def send_both(group):
        send(group, leftward, has_left, RELAYED_LEFT, left_relays, to_left, left_send)
        send(group, rightward, has_right, RELAYED_RIGHT, right_relays, to_right, right_send)

    def pack_next(group, carry):
        pack(group)
        return carry

    def send_next(group, carry):
        send_both(group)
        return carry

    pack(0)
    soon = (lax.rem(me, 2) == 1) | (me == 0)

    @pl.when(soon)
    def _():
        for copy in rest:
            copy.wait()
        own_sums()
        pack(1)

    pl.semaphore_wait(barrier, jnp.where(leads, chain - 1 + cross - 1, chain - 1))
    send_both(0)

    @pl.when(leads)
    def _():
        for step in range(1, cross):
            peer = lax.rem(plane + step, cross)
            pl.semaphore_signal(ready_sem, inc=1, device_id={"cross": peer}, device_id_type=MESH)

    @pl.when(jnp.logical_not(soon))
    def _():
        for copy in rest:
            copy.wait()
        own_sums()

    send_sums()

    @pl.when(jnp.logical_not(soon))
    def _():
        pack(1)

    for group in range(1, 2):
        send_both(group)
    for group in range(2, groups):
        pack(group)
    send_edges()
    for group in range(2, groups):
        send_both(group)

    part_copies = [
        pltpu.make_async_remote_copy(
            src_ref=parts.at[plane], dst_ref=parts.at[plane],
            send_sem=part_sem.at[0], recv_sem=part_sem.at[1],
            device_id={"cross": lax.rem(plane + step, cross)}, device_id_type=MESH,
        )
        for step in range(1, cross)
    ]

    elsewhere = pl.ds(0, cross - 1)
    all_parts = pltpu.make_async_remote_copy(
        src_ref=parts.at[elsewhere], dst_ref=parts.at[elsewhere],
        send_sem=part_sem.at[0], recv_sem=part_sem.at[1],
        device_id={"cross": lax.rem(plane + 1, cross)}, device_id_type=MESH,
    )

    def open_planes():
        @pl.when(leads)
        def _():
            pl.semaphore_wait(ready_sem, cross - 1)
            for peer in range(1, chain):
                pl.semaphore_signal(open_sem, inc=1, device_id={"chain": jnp.int32(peer)}, device_id_type=MESH)

    def send_parts():
        @pl.when(jnp.logical_not(leads))
        def _():
            pl.semaphore_wait(open_sem, 1)

        for copy in part_copies:
            copy.start()

    def pass_on(index, sides=(0, 1)):
        for side, (among, routes, source, send_sem, landing, recv_sem) in enumerate((
            (RELAYED_RIGHT, right_relays, to_right, right_send, from_left, right_recv),
            (RELAYED_LEFT, left_relays, to_left, left_send, from_right, left_recv),
        )):
            if side not in sides:
                continue
            for through, target in routes.values():
                if index >= len(among):
                    continue
                group = among[index]

                @pl.when(me == through)
                def _():
                    to_relay(group, source, send_sem, through).wait_recv()
                    onward(group, landing, recv_sem, target).start()

    shift_row = shifts[...]

    def reduce_chain():
        starts[...] = jnp.zeros_like(starts)
        all_sums.wait_recv()
        before = jnp.zeros((8, pencils), jnp.float32)
        whole = jnp.zeros((1, BLOCK), jnp.float32)
        for index in range(chain):
            before = before + jnp.where(index < me, sums[index], 0.0)
            whole = whole + sums[index, VARS : VARS + 1]
        parts[plane] = whole
        starts[0:8, :] = before
        starts[8:16, :] = before + jnp.where(shift_row >= 0, sums[me], 0.0)

    def spread_starts():
        turned = jnp.transpose(starts[...])
        for var in range(VARS):
            base[var] = base[var] + turned[:, var : var + 1]
            beyond[var] = jnp.broadcast_to(turned[:, 8 + var : 9 + var], (pencils, BLOCK))

    pass_on(0)
    open_planes()
    pass_on(1)
    reduce_chain()
    for index in range(2, len(RELAYED_RIGHT)):
        pass_on(index, (0,))
    send_parts()
    send_late()

    @pl.when(me == 0)
    def _():
        from_left[...] = jnp.zeros_like(from_left)

    @pl.when(me == chain - 1)
    def _():
        from_right[...] = jnp.zeros_like(from_right)
        edges_in[...] = jnp.zeros_like(edges_in)

    f = fraction[...]
    first = interval_integrals(-1.0 + 0.0 * f, 1.0 - 2.0 * f, 2.0 * f)
    second = interval_integrals(1.0 - 2.0 * f, 1.0 + 0.0 * f, 2.0 * f - 2.0)
    raw[...] = jnp.zeros_like(raw)
    columns = partial_weights(f) + first + second + [shift_row.astype(jnp.float32)]
    for index, value in enumerate(columns):
        raw[index : index + 1, :] = value
    turned = jnp.transpose(raw[...])
    for index in range(COEFS):
        coef[index] = jnp.broadcast_to(turned[:, index : index + 1], (pencils, BLOCK))
    shift_of[...] = jnp.broadcast_to(turned[:, COEFS : COEFS + 1], (pencils, BLOCK)).astype(jnp.int32)

    up_to_edge = jnp.where(source_cell < BLOCK // 2, before_cell, 1.0 - before_cell)
    triangle[...] = up_to_edge.astype(jnp.bfloat16)
    for index in range(2, len(RELAYED_LEFT)):
        pass_on(index, (1,))
    spread_starts()
    receive_edges()


    held = moments, from_left, from_right, edges, coef, shift_of, base, beyond, triangle

    def receive(group):
        @pl.when(has_right)
        def _():
            leftward(group).wait_recv()

        @pl.when(has_left)
        def _():
            rightward(group).wait_recv()

    def turn_to(step):
        group = jnp.int32(step)
        for order, routes in ((ORDER_RIGHT, right_relays), (ORDER_LEFT, left_relays)):
            for _, target in routes.values():
                for index, other in enumerate(order):
                    group = jnp.where((me == target) & (step == index), other, group)
        return group

    def remap(step, carry):
        group = turn_to(step)
        receive(group)
        finish_group(group, held, remapped, mass, 0)
        return carry

    lax.fori_loop(0, groups - 1, remap, 0)

    all_parts.wait_recv()
    grand = parts[0]
    for index in range(1, cross):
        grand = grand + parts[index]
    mean = grand / float(pencils * cross)
    for var in range(VARS):
        mean_of[var : var + 1, :] = jnp.broadcast_to(mean[:, var : var + 1], (1, BLOCK))
    done = pl.ds(0, pencils - GROUP)
    for var in range(VARS):
        mass[var, done, :] = mass[var, done, :] / mean_of[var : var + 1, :]

    all_sums.wait_send()
    all_parts.wait_send()

    for among, routes, landing, recv_sem in (
        (RELAYED_RIGHT, right_relays, from_left, right_recv), (RELAYED_LEFT, left_relays, from_right, left_recv)
    ):
        for through, target in routes.values():

            @pl.when(me == through)
            def _():
                passed = pl.ds(0, len(among))
                pltpu.make_async_remote_copy(
                    src_ref=relay.at[passed], dst_ref=landing.at[passed],
                    send_sem=relay_send.at[0], recv_sem=recv_sem.at[0],
                    device_id={"chain": jnp.int32(target)}, device_id_type=MESH,
                ).wait_send()

    @pl.when(has_left)
    def _():
        edge_copy.wait_send()
        pltpu.make_async_remote_copy(
            src_ref=to_left, dst_ref=from_right,
            send_sem=left_send.at[0], recv_sem=left_recv.at[0],
            device_id={"chain": lax.rem(me + chain - 1, chain)}, device_id_type=MESH,
        ).wait_send()

    @pl.when(has_right)
    def _():
        pltpu.make_async_remote_copy(
            src_ref=to_right, dst_ref=from_left,
            send_sem=right_send.at[0], recv_sem=right_recv.at[0],
            device_id={"chain": lax.rem(me + 1, chain)}, device_id_type=MESH,
        ).wait_send()

    receive(groups - 1)


def deliver(
    remapped, mass, moments, from_left, from_right, edges, coef, shift_of, base, beyond, triangle, mean_of,
    remapped_out, mass_out,
    last_remapped, last_mass, sem,
):
    done = remapped.shape[1] - GROUP
    early, late = pl.ds(0, done), pl.ds(done, GROUP)
    held = moments, from_left, from_right, edges, coef, shift_of, base, beyond, triangle
    copies = [
        pltpu.make_async_copy(source, target, sem.at[index % 2])
        for index, (source, target) in enumerate((
            (remapped.at[:, early, :], remapped_out.at[:, early, :]),
            (mass.at[:, early, :], mass_out.at[:, early, :]),
            (last_remapped, remapped_out.at[:, late, :]),
            (last_mass, mass_out.at[:, late, :]),
        ))
    ]
    for copy in copies[:2]:
        copy.start()
    finish_group(done // GROUP, held, last_remapped, last_mass, done)
    for var in range(VARS):
        last_mass[var] = last_mass[var] / mean_of[var : var + 1, :]
    for copy in copies[2:]:
        copy.start()
    pltpu.make_async_copy(remapped, remapped_out, sem.at[0]).wait()
    pltpu.make_async_copy(mass, mass_out, sem.at[1]).wait()


def solution(mesh):
    chain, cross = mesh.shape["chain"], mesh.shape["cross"]
    relays = corner_relays(mesh)

    def shards(moments, flags, shifts, fraction):
        row_count, pencils, cells = moments.shape
        assert row_count == ROWS and cells == BLOCK and pencils == BLOCK
        groups = pencils // GROUP
        dma = pltpu.SemaphoreType.DMA
        float_of = functools.partial(jax.ShapeDtypeStruct, dtype=jnp.float32)
        halo = (groups, SENT, TILE, BLOCK)
        block = pltpu.VMEM(halo, jnp.float32)
        results = float_of(moments.shape), float_of((VARS, pencils, cells))
        handed = results + (
            float_of(moments.shape), float_of(halo), float_of(halo), float_of((groups, EDGE_STEP, TILE, BLOCK)),
            float_of((COEFS, pencils, BLOCK)), jax.ShapeDtypeStruct((pencils, BLOCK), jnp.int32),
            float_of((VARS, pencils, BLOCK)), float_of((VARS, pencils, BLOCK)),
            jax.ShapeDtypeStruct((BLOCK, BLOCK), jnp.bfloat16), float_of((8, BLOCK)),
        )
        in_vmem = pl.BlockSpec(memory_space=pltpu.VMEM)
        in_hbm = pl.BlockSpec(memory_space=pltpu.HBM)
        ready = pl.pallas_call(
            functools.partial(kernel, chain, cross, relays),
            out_shape=handed,
            in_specs=[in_hbm] * 4,
            out_specs=(in_vmem,) * len(handed),
            scratch_shapes=[
                pltpu.VMEM(flags.shape, jnp.int32),
                pltpu.VMEM((1, pencils), jnp.int32),
                pltpu.VMEM((1, pencils), jnp.float32),
                block, block, block,
                pltpu.VMEM((groups, TILE, BLOCK), jnp.float32),
                pltpu.VMEM((groups // 2, TILE, BLOCK), jnp.float32),
                pltpu.VMEM((groups // 2, TILE, BLOCK), jnp.float32),
                pltpu.VMEM((chain, 8, pencils), jnp.float32),
                pltpu.VMEM((cross, 1, BLOCK), jnp.float32),
                pltpu.VMEM((BLOCK, pencils), jnp.float32),
                pltpu.VMEM((BLOCK, pencils), jnp.float32),
                dma((1,)), dma((groups,)), dma((1,)), dma((groups,)),
                dma((1,)), dma((groups // 2,)), dma((2,)), dma((2,)),
                pltpu.SemaphoreType.REGULAR, pltpu.SemaphoreType.REGULAR, dma((2,)), dma((5,)),
            ],
            compiler_params=pltpu.CompilerParams(
                collective_id=0, has_side_effects=True, vmem_limit_bytes=24 << 20
            ),
        )(*(
            pltpu.with_memory_space_constraint(value, pltpu.HBM)
            for value in (moments, flags, shifts.T, fraction.reshape(1, pencils))
        ))
        return pl.pallas_call(
            deliver,
            out_shape=results,
            in_specs=[in_vmem] * len(handed),
            out_specs=(in_hbm,) * 2,
            scratch_shapes=[
                pltpu.VMEM((ROWS, GROUP, BLOCK), jnp.float32),
                pltpu.VMEM((VARS, GROUP, BLOCK), jnp.float32),
                dma((2,)),
            ],
            compiler_params=pltpu.CompilerParams(vmem_limit_bytes=16 << 20),
        )(*ready)

    in_specs = (P(None, "cross", "chain"), P("cross", "chain"), P("cross", "chain"), P("cross"))
    out_specs = (P(None, "cross", "chain"), P(None, "cross", "chain"))
    return jax.shard_map(shards, mesh=mesh, in_specs=in_specs, out_specs=out_specs, check_vma=False)
```

```python
import functools

import jax
import numpy as np
import jax.numpy as jnp
from jax import lax
from jax.experimental import pallas as pl
from jax.experimental.pallas import tpu as pltpu
from jax.sharding import PartitionSpec as P

VARS = 5
MOMENTS = 4
BLOCK = 128
SHIFT_MAX = 48
ROWS = VARS * MOMENTS
SPAN = ROWS * SHIFT_MAX
FULL, HALF = SPAN // BLOCK, BLOCK // 2
TILE = 8
TILES = 2
GROUP = TILES * TILE
SENT = TILES * FULL + 1
EDGES = -(-ROWS // 8)
EDGE_STEP = TILES * EDGES
LATE = 2
ORDER_RIGHT, ORDER_LEFT = (0, 1, 3, 5, 6, 2, 4), (0, 2, 4, 6, 1, 3, 5)
RELAYED_RIGHT, RELAYED_LEFT = (1, 3, 5, 6), (1, 3, 5)
PAIRS = tuple((k, m) for k in range(1, MOMENTS) for m in range(k, MOMENTS))
COEFS = MOMENTS + 2 * len(PAIRS)
MESH = pl.DeviceIdType.MESH
HIGHEST = lax.Precision.HIGHEST

gauss_nodes = (-0.8611363115940526, -0.3399810435848563, 0.3399810435848563, 0.8611363115940526)
gauss_weights = (0.3478548451374538, 0.6521451548625461, 0.6521451548625461, 0.3478548451374538)


AFTER_FIRST, AFTER_LENGTH = SHIFT_MAX, SHIFT_MAX + 1
BEFORE_FIRST, BEFORE_LENGTH = 0, SHIFT_MAX


def place(row, first):
    chunk, lane = divmod((first + SHIFT_MAX * row) % SPAN, BLOCK)
    return chunk, lane, lane + SHIFT_MAX > BLOCK


def segments(first):
    held = [[] for _ in range(FULL + 1)]
    for row in range(ROWS):
        chunk, lane, splits = place(row, first)
        held[chunk].append((lane, row))
        if splits:
            held[chunk + 1].append((0, row))
    return [sorted(chunk) for chunk in held]


AFTER, BEFORE = segments(AFTER_FIRST), segments(BEFORE_FIRST)
WRAPPED = ROWS - 1


def turn_of(row):
    return (SHIFT_MAX * (row + 1)) % BLOCK


def edge_lane(row):
    return (turn_of(row) + SHIFT_MAX) % BLOCK


def legendre_values(point):
    return [
        jnp.ones_like(point),
        point,
        0.5 * (3.0 * point * point - 1.0),
        0.5 * (5.0 * point * point * point - 3.0 * point),
    ]


def interval_integrals(low_end, high_end, offset):
    half = 0.5 * (high_end - low_end)
    middle = 0.5 * (high_end + low_end)
    entries = [jnp.zeros_like(low_end) for _ in PAIRS]
    for node, weight in zip(gauss_nodes, gauss_weights):
        point = middle + half * node
        target = legendre_values(point)
        source = legendre_values(point + offset)
        scaled = [weight * half * value for value in target]
        for index, (k, m) in enumerate(PAIRS):
            entries[index] = entries[index] + scaled[k] * source[m]
    return entries


def partial_weights(fraction):
    shifted = 2.0 * fraction - 1.0
    square = shifted * shifted
    return [
        fraction,
        fraction * fraction - fraction,
        0.25 * (square * shifted - shifted),
        0.5 * (0.5 * (1.25 * square * square - 1.5 * square) + 0.125),
    ]


def corner_relays(mesh):
    ring = np.moveaxis(mesh.devices, mesh.axis_names.index("chain"), 0).reshape(mesh.shape["chain"], -1)[:, 0]
    if any(getattr(device, "coords", None) is None for device in ring):
        return {}, {}
    spots = [tuple(device.coords) for device in ring]
    rightward, leftward = {}, {}
    if len({spot[0] for spot in spots}) == 2 and len({spot[1] for spot in spots}) == 2:
        for index in range(len(spots) - 1):
            low, high = spots[index], spots[index + 1]
            if low[0] != high[0] and low[1] != high[1]:
                for found, source, target, pick in (
                    (rightward, index, index + 1, max), (leftward, index + 1, index, max)
                ):
                    corner = (spots[source][0], spots[target][1])
                    at = [i for i, spot in enumerate(spots) if spot[:2] == corner]
                    if at:
                        found[source] = (pick(at), target)
    return rightward, leftward


def exact_dot(value, ones):
    high = value.astype(jnp.bfloat16)
    rest = value - high.astype(jnp.float32)
    middle = rest.astype(jnp.bfloat16)
    low = (rest - middle.astype(jnp.float32)).astype(jnp.bfloat16)
    return sum(jnp.dot(part, ones, preferred_element_type=jnp.float32) for part in (low, middle, high))


def finish_group(group, held, remapped, mass, skipped):
    moments, from_left, from_right, edges, coef, shift_of, base, beyond, triangle = held
    lane = lax.broadcasted_iota(jnp.int32, (TILE, BLOCK), 1)
    halos, places_of = [], []
    for tile in range(GROUP // TILE):
        rows = pl.ds(pl.multiple_of(group * GROUP + tile * TILE, TILE), TILE)
        inner = pl.ds(tile * TILE, TILE)
        shift = shift_of[rows, :]
        ahead = shift >= 0
        put = pl.ds(pl.multiple_of(group * GROUP + tile * TILE - skipped, TILE), TILE)
        places_of.append((rows, put, shift, ahead))

        folded = {}
        for name, ref in (("right", from_right), ("left", from_left)):
            value = ref[group, SENT - 1]
            folded[name] = pltpu.roll(value, HALF, 1) if tile else value

        def fetch(name, ref, row, first):
            chunk, start, splits = place(row, first)
            values = [
                ref[group, TILES * index + tile] if index < FULL else folded[name]
                for index in ((chunk, chunk + 1) if splits else (chunk,))
            ]
            return jnp.where(lane >= start, *values) if splits else values[0]

        def halo_row(row):
            right = fetch("right", from_right, row, AFTER_FIRST)
            left = fetch("left", from_left, row, BEFORE_FIRST)
            edge = edges[group, EDGES * tile + row // 8]
            wrapped = row == WRAPPED
            value = left if wrapped else jnp.where(ahead, right, left)
            value = jnp.where(ahead & (lane == edge_lane(row)), edge, value)
            value = pltpu.roll(value, (BLOCK - turn_of(row)) % BLOCK, 1) if turn_of(row) else value
            return jnp.where(ahead & (lane < SHIFT_MAX), right, value) if wrapped else value

        halos.append([halo_row(row) for row in range(ROWS)])

    signed = []
    for (_, _, _, ahead), halo in zip(places_of, halos):
        for var in range(VARS):
            value = halo[MOMENTS * var]
            signed.append(jnp.where(
                ahead,
                jnp.where(lane < AFTER_LENGTH, value, 0.0),
                jnp.where(lane >= BLOCK - BEFORE_LENGTH, -value, 0.0),
            ))
    crossed = exact_dot(jnp.concatenate(signed, axis=0), triangle[...])

    for tile, ((rows, put, shift, ahead), halo) in enumerate(zip(places_of, halos)):
        turn = shift & (BLOCK - 1)
        outside = jnp.where(ahead, lane - turn, turn - 1 - lane) < 0
        outside_next = jnp.where(ahead, lane - turn - 1, turn - lane) < 0
        at = (lane + turn) & (BLOCK - 1)
        weight = [coef[m, rows, :] for m in range(MOMENTS)]
        inside, across = {}, {}
        for index, (k, m) in enumerate(PAIRS):
            inside[k, m] = coef[MOMENTS + index, rows, :]
            across[k, m] = coef[MOMENTS + len(PAIRS) + index, rows, :]

        def settle(value):
            return jnp.take_along_axis(value, at, axis=1, mode="promise_in_bounds")

        for var in range(VARS):
            here, after = [], []
            for order in range(MOMENTS):
                own = moments[MOMENTS * var + order, rows, :]
                other = halo[MOMENTS * var + order]
                here.append(jnp.where(outside, other, own))
                after.append(pltpu.roll(jnp.where(outside_next, other, own), BLOCK - 1, 1))
            filled = weight[0] * here[0]
            filled_after = weight[0] * after[0]
            for m in range(1, MOMENTS):
                filled = filled + weight[m] * here[m]
                filled_after = filled_after + weight[m] * after[m]
            rise = after[0] - here[0]
            remapped[MOMENTS * var, put, :] = settle(here[0] + (filled_after - filled))
            for k in range(1, MOMENTS):
                value = inside[k, k] * here[k] + across[k, k] * after[k]
                for m in range(1, MOMENTS):
                    if m == k:
                        continue
                    pair = (min(k, m), max(k, m))
                    term = inside[pair] * here[m] + across[pair] * after[m]
                    value = value - term if k > m and (k + m) % 2 else value + term
                edge = (2.0 if k % 2 == 0 else -2.0) * (weight[k] * rise)
                remapped[MOMENTS * var + k, put, :] = settle((k + 0.5) * (value + edge))
            index = (tile * VARS + var) * TILE
            start = jnp.where(
                outside, crossed[index : index + TILE] + beyond[var, rows, :], base[var, rows, :]
            )
            mass[var, put, :] = settle(start + filled)


def kernel(
    chain, cross, relays,
    moments_in, flags_in, shifts_in, fraction_in,
    remapped, mass, moments, from_left, from_right, edges, coef, shift_of, base, beyond, triangle, mean_of,
    flags, shifts, fraction,
    to_left, to_right, relay, own_edges, edges_out, edges_in,
    sums, parts, raw, starts,
    left_send, left_recv, right_send, right_recv, relay_send, relay_recv,
    sum_sem, part_sem, ready_sem, open_sem, edge_sem, input_sem,
):
    pencils = moments.shape[1]
    groups = pencils // GROUP
    me = lax.axis_index("chain")
    plane = lax.axis_index("cross")

    first_rows, later_rows = pl.ds(0, GROUP), pl.ds(GROUP, pencils - GROUP)
    inputs = [
        pltpu.make_async_copy(source, target, input_sem.at[index])
        for index, (source, target) in enumerate((
            (flags_in, flags),
            (moments_in.at[:, first_rows, :], moments.at[:, first_rows, :]),
            (moments_in.at[:, later_rows, :], moments.at[:, later_rows, :]),
            (shifts_in, shifts),
            (fraction_in, fraction),
        ))
    ]
    urgent, rest = inputs[:2], inputs[2:]
    for copy in urgent:
        copy.start()

    barrier = pltpu.get_barrier_semaphore()
    for step in range(1, chain):
        peer = lax.rem(me + step, chain)
        pl.semaphore_signal(barrier, inc=1, device_id={"chain": peer}, device_id_type=MESH)
    leads = me == 0

    @pl.when(leads)
    def _():
        for step in range(1, cross):
            peer = lax.rem(plane + step, cross)
            pl.semaphore_signal(barrier, inc=1, device_id={"cross": peer}, device_id_type=MESH)

    for copy in rest:
        copy.start()
    for copy in urgent:
        copy.wait()

    def leftward(group):
        return pltpu.make_async_remote_copy(
            src_ref=to_left.at[group], dst_ref=from_right.at[group],
            send_sem=left_send.at[0], recv_sem=left_recv.at[group],
            device_id={"chain": lax.rem(me + chain - 1, chain)}, device_id_type=MESH,
        )

    def rightward(group):
        return pltpu.make_async_remote_copy(
            src_ref=to_right.at[group], dst_ref=from_left.at[group],
            send_sem=right_send.at[0], recv_sem=right_recv.at[group],
            device_id={"chain": lax.rem(me + 1, chain)}, device_id_type=MESH,
        )

    has_left, has_right = me > 0, me < chain - 1

    sum_copies = [
        pltpu.make_async_remote_copy(
            src_ref=sums.at[me], dst_ref=sums.at[me],
            send_sem=sum_sem.at[0], recv_sem=sum_sem.at[1],
            device_id={"chain": lax.rem(me + step, chain)}, device_id_type=MESH,
        )
        for step in range(1, chain)
    ]
    others = pl.ds(0, chain - 1)
    all_sums = pltpu.make_async_remote_copy(
        src_ref=sums.at[others], dst_ref=sums.at[others],
        send_sem=sum_sem.at[0], recv_sem=sum_sem.at[1],
        device_id={"chain": lax.rem(me + 1, chain)}, device_id_type=MESH,
    )

    source_cell = lax.broadcasted_iota(jnp.int32, (BLOCK, BLOCK), 0)
    target_cell = lax.broadcasted_iota(jnp.int32, (BLOCK, BLOCK), 1)
    before_cell = jnp.where(source_cell < target_cell, 1.0, 0.0)

    def own_sums():
        total = jnp.zeros((pencils, BLOCK), jnp.float32)
        for var in range(VARS):
            pick = jnp.where(target_cell == var, 1.0, 0.0)
            both = jnp.concatenate([before_cell, pick], axis=1).astype(jnp.bfloat16)
            summed = exact_dot(moments[MOMENTS * var], both)
            base[var] = summed[:, :BLOCK]
            total = total + summed[:, BLOCK:]
        sums[me] = jnp.where(
            lax.broadcasted_iota(jnp.int32, (8, BLOCK), 0) == VARS,
            jnp.sum(total, axis=0, keepdims=True), jnp.transpose(total)[:8],
        )

    def send_sums():
        for copy in sum_copies:
            copy.start()

    lane = lax.broadcasted_iota(jnp.int32, (TILE, BLOCK), 1)
    spot = lane & 15

    def pack(group):
        halves = {}
        edge = None
        for tile in range(TILES):
            rows = pl.ds(group * GROUP + tile * TILE, TILE)
            flag = flags[rows, :]
            keep_linear, keep_full = flag <= 1, flag == 0
            rolled = []
            for row in range(ROWS):
                value = moments[row, rows, :]
                order = row % MOMENTS
                if order > 0:
                    value = jnp.where(keep_linear if order == 1 else keep_full, value, 0.0)
                    moments[row, rows, :] = value
                rolled.append(pltpu.roll(value, turn_of(row), 1) if turn_of(row) else value)
            for side, (held, target) in enumerate(((AFTER, to_left), (BEFORE, to_right))):
                for chunk in range(FULL + 1):
                    value = None
                    for start, row in held[chunk]:
                        part = moments[row, rows, :] if row == WRAPPED and side == 0 else rolled[row]
                        value = part if value is None else jnp.where(lane >= start, part, value)
                    if chunk < FULL:
                        target[group, TILES * chunk + tile] = value
                    else:
                        halves[side, tile] = value
            for index in range(EDGES):
                value = None
                for row in range(8 * index, min(8 * index + 8, ROWS)):
                    here = (lane >> 4) == edge_lane(row) // 16
                    value = rolled[row] if value is None else jnp.where(here, rolled[row], value)
                at = EDGES * tile + index
                value = pltpu.roll(value, at, 1) if at else value
                edge = value if edge is None else jnp.where(spot >= at, value, edge)
        for side, target in enumerate((to_left, to_right)):
            target[group, SENT - 1] = jnp.where(
                lane < HALF, halves[side, 0], pltpu.roll(halves[side, 1], HALF, 1)
            )
        own_edges[group] = edge

    edge_copy = pltpu.make_async_remote_copy(
        src_ref=edges_out, dst_ref=edges_in,
        send_sem=edge_sem.at[0], recv_sem=edge_sem.at[1],
        device_id={"chain": lax.rem(me + chain - 1, chain)}, device_id_type=MESH,
    )

    def send_edges():
        for index in range(groups // 2):
            edges_out[index] = jnp.where(
                spot < EDGE_STEP, own_edges[2 * index], pltpu.roll(own_edges[2 * index + 1], EDGE_STEP, 1)
            )

        @pl.when(has_left)
        def _():
            edge_copy.start()

    def receive_edges():
        @pl.when(has_right)
        def _():
            edge_copy.wait_recv()

        for group in range(groups):
            value = edges_in[group // 2]
            for at in range(EDGE_STEP):
                back = EDGE_STEP * (group % 2) + at
                edges[group, at] = pltpu.roll(value, BLOCK - back, 1) if back else value

    right_relays, left_relays = relays

    def to_relay(group, source, send_sem, through):
        return pltpu.make_async_remote_copy(
            src_ref=source.at[group], dst_ref=relay.at[group],
            send_sem=send_sem.at[0], recv_sem=relay_recv.at[group // 2],
            device_id={"chain": jnp.int32(through)}, device_id_type=MESH,
        )

    def onward(group, landing, recv_sem, target):
        return pltpu.make_async_remote_copy(
            src_ref=relay.at[group], dst_ref=landing.at[group],
            send_sem=relay_send.at[0], recv_sem=recv_sem.at[group],
            device_id={"chain": jnp.int32(target)}, device_id_type=MESH,
        )

    def send(group, direct, wanted, among, routes, source, send_sem):
        group = jnp.int32(group)
        relayed = functools.reduce(jnp.logical_or, [group == index for index in among])
        for start, (through, _) in routes.items():
            wanted = wanted & ((me != start) | jnp.logical_not(relayed))

            @pl.when((me == start) & relayed)
            def _():
                to_relay(group, source, send_sem, through).start()

        if direct is rightward:
            for start in routes:
                wanted = wanted & ((me != start) | (group < LATE))

        @pl.when(wanted)
        def _():
            direct(group).start()

    def send_late():
        for start in right_relays:

            @pl.when(me == start)
            def _():
                for group in range(groups):
                    if group >= LATE and group not in RELAYED_RIGHT:
                        rightward(group).start()

    def send_both(group):
        send(group, leftward, has_left, RELAYED_LEFT, left_relays, to_left, left_send)
        send(group, rightward, has_right, RELAYED_RIGHT, right_relays, to_right, right_send)

    def pack_next(group, carry):
        pack(group)
        return carry

    def send_next(group, carry):
        send_both(group)
        return carry

    pack(0)
    soon = me != chain - 2

    @pl.when(soon)
    def _():
        for copy in rest:
            copy.wait()
        own_sums()
        pack(1)

    pl.semaphore_wait(barrier, jnp.where(leads, chain - 1 + cross - 1, chain - 1))
    send_both(0)

    @pl.when(leads)
    def _():
        for step in range(1, cross):
            peer = lax.rem(plane + step, cross)
            pl.semaphore_signal(ready_sem, inc=1, device_id={"cross": peer}, device_id_type=MESH)

    @pl.when(jnp.logical_not(soon))
    def _():
        for copy in rest:
            copy.wait()
        own_sums()

    send_sums()

    @pl.when(jnp.logical_not(soon))
    def _():
        pack(1)

    for group in range(1, 2):
        send_both(group)
    for group in range(2, groups):
        pack(group)
    send_edges()
    for group in range(2, groups):
        send_both(group)

    part_copies = [
        pltpu.make_async_remote_copy(
            src_ref=parts.at[plane], dst_ref=parts.at[plane],
            send_sem=part_sem.at[0], recv_sem=part_sem.at[1],
            device_id={"cross": lax.rem(plane + step, cross)}, device_id_type=MESH,
        )
        for step in range(1, cross)
    ]

    elsewhere = pl.ds(0, cross - 1)
    all_parts = pltpu.make_async_remote_copy(
        src_ref=parts.at[elsewhere], dst_ref=parts.at[elsewhere],
        send_sem=part_sem.at[0], recv_sem=part_sem.at[1],
        device_id={"cross": lax.rem(plane + 1, cross)}, device_id_type=MESH,
    )

    def open_planes():
        @pl.when(leads)
        def _():
            pl.semaphore_wait(ready_sem, cross - 1)
            for peer in range(1, chain):
                pl.semaphore_signal(open_sem, inc=1, device_id={"chain": jnp.int32(peer)}, device_id_type=MESH)

    def send_parts():
        @pl.when(jnp.logical_not(leads))
        def _():
            pl.semaphore_wait(open_sem, 1)

        for copy in part_copies:
            copy.start()

    def pass_on(index, sides=(0, 1)):
        for side, (among, routes, source, send_sem, landing, recv_sem) in enumerate((
            (RELAYED_RIGHT, right_relays, to_right, right_send, from_left, right_recv),
            (RELAYED_LEFT, left_relays, to_left, left_send, from_right, left_recv),
        )):
            if side not in sides:
                continue
            for through, target in routes.values():
                if index >= len(among):
                    continue
                group = among[index]

                @pl.when(me == through)
                def _():
                    to_relay(group, source, send_sem, through).wait_recv()
                    onward(group, landing, recv_sem, target).start()

    shift_row = shifts[...]

    def reduce_chain():
        starts[...] = jnp.zeros_like(starts)
        all_sums.wait_recv()
        before = jnp.zeros((8, pencils), jnp.float32)
        whole = jnp.zeros((1, BLOCK), jnp.float32)
        for index in range(chain):
            before = before + jnp.where(index < me, sums[index], 0.0)
            whole = whole + sums[index, VARS : VARS + 1]
        parts[plane] = whole
        starts[0:8, :] = before
        starts[8:16, :] = before + jnp.where(shift_row >= 0, sums[me], 0.0)

    def spread_starts():
        turned = jnp.transpose(starts[...])
        for var in range(VARS):
            base[var] = base[var] + turned[:, var : var + 1]
            beyond[var] = jnp.broadcast_to(turned[:, 8 + var : 9 + var], (pencils, BLOCK))

    pass_on(0)
    open_planes()
    pass_on(1)
    reduce_chain()
    for index in range(2, len(RELAYED_RIGHT)):
        pass_on(index, (0,))
    send_parts()
    send_late()

    @pl.when(me == 0)
    def _():
        from_left[...] = jnp.zeros_like(from_left)

    @pl.when(me == chain - 1)
    def _():
        from_right[...] = jnp.zeros_like(from_right)
        edges_in[...] = jnp.zeros_like(edges_in)

    f = fraction[...]
    first = interval_integrals(-1.0 + 0.0 * f, 1.0 - 2.0 * f, 2.0 * f)
    second = interval_integrals(1.0 - 2.0 * f, 1.0 + 0.0 * f, 2.0 * f - 2.0)
    raw[...] = jnp.zeros_like(raw)
    columns = partial_weights(f) + first + second + [shift_row.astype(jnp.float32)]
    for index, value in enumerate(columns):
        raw[index : index + 1, :] = value
    turned = jnp.transpose(raw[...])
    for index in range(COEFS):
        coef[index] = jnp.broadcast_to(turned[:, index : index + 1], (pencils, BLOCK))
    shift_of[...] = jnp.broadcast_to(turned[:, COEFS : COEFS + 1], (pencils, BLOCK)).astype(jnp.int32)

    up_to_edge = jnp.where(source_cell < BLOCK // 2, before_cell, 1.0 - before_cell)
    triangle[...] = up_to_edge.astype(jnp.bfloat16)
    for index in range(2, len(RELAYED_LEFT)):
        pass_on(index, (1,))
    spread_starts()
    receive_edges()


    held = moments, from_left, from_right, edges, coef, shift_of, base, beyond, triangle

    def receive(group):
        @pl.when(has_right)
        def _():
            leftward(group).wait_recv()

        @pl.when(has_left)
        def _():
            rightward(group).wait_recv()

    def turn_to(step):
        group = jnp.int32(step)
        for order, routes in ((ORDER_RIGHT, right_relays), (ORDER_LEFT, left_relays)):
            for _, target in routes.values():
                for index, other in enumerate(order):
                    group = jnp.where((me == target) & (step == index), other, group)
        return group

    def remap(step, carry):
        group = turn_to(step)
        receive(group)
        finish_group(group, held, remapped, mass, 0)
        return carry

    lax.fori_loop(0, groups - 1, remap, 0)

    all_parts.wait_recv()
    grand = parts[0]
    for index in range(1, cross):
        grand = grand + parts[index]
    mean = grand / float(pencils * cross)
    for var in range(VARS):
        mean_of[var : var + 1, :] = jnp.broadcast_to(mean[:, var : var + 1], (1, BLOCK))
    done = pl.ds(0, pencils - GROUP)
    for var in range(VARS):
        mass[var, done, :] = mass[var, done, :] / mean_of[var : var + 1, :]

    all_sums.wait_send()
    all_parts.wait_send()

    for among, routes, landing, recv_sem in (
        (RELAYED_RIGHT, right_relays, from_left, right_recv), (RELAYED_LEFT, left_relays, from_right, left_recv)
    ):
        for through, target in routes.values():

            @pl.when(me == through)
            def _():
                passed = pl.ds(0, len(among))
                pltpu.make_async_remote_copy(
                    src_ref=relay.at[passed], dst_ref=landing.at[passed],
                    send_sem=relay_send.at[0], recv_sem=recv_sem.at[0],
                    device_id={"chain": jnp.int32(target)}, device_id_type=MESH,
                ).wait_send()

    @pl.when(has_left)
    def _():
        edge_copy.wait_send()
        pltpu.make_async_remote_copy(
            src_ref=to_left, dst_ref=from_right,
            send_sem=left_send.at[0], recv_sem=left_recv.at[0],
            device_id={"chain": lax.rem(me + chain - 1, chain)}, device_id_type=MESH,
        ).wait_send()

    @pl.when(has_right)
    def _():
        pltpu.make_async_remote_copy(
            src_ref=to_right, dst_ref=from_left,
            send_sem=right_send.at[0], recv_sem=right_recv.at[0],
            device_id={"chain": lax.rem(me + 1, chain)}, device_id_type=MESH,
        ).wait_send()

    receive(groups - 1)


def deliver(
    remapped, mass, moments, from_left, from_right, edges, coef, shift_of, base, beyond, triangle, mean_of,
    remapped_out, mass_out,
    last_remapped, last_mass, sem,
):
    done = remapped.shape[1] - GROUP
    early, late = pl.ds(0, done), pl.ds(done, GROUP)
    held = moments, from_left, from_right, edges, coef, shift_of, base, beyond, triangle
    copies = [
        pltpu.make_async_copy(source, target, sem.at[index % 2])
        for index, (source, target) in enumerate((
            (remapped.at[:, early, :], remapped_out.at[:, early, :]),
            (mass.at[:, early, :], mass_out.at[:, early, :]),
            (last_remapped, remapped_out.at[:, late, :]),
            (last_mass, mass_out.at[:, late, :]),
        ))
    ]
    for copy in copies[:2]:
        copy.start()
    finish_group(done // GROUP, held, last_remapped, last_mass, done)
    for var in range(VARS):
        last_mass[var] = last_mass[var] / mean_of[var : var + 1, :]
    for copy in copies[2:]:
        copy.start()
    pltpu.make_async_copy(remapped, remapped_out, sem.at[0]).wait()
    pltpu.make_async_copy(mass, mass_out, sem.at[1]).wait()


def solution(mesh):
    chain, cross = mesh.shape["chain"], mesh.shape["cross"]
    relays = corner_relays(mesh)

    def shards(moments, flags, shifts, fraction):
        row_count, pencils, cells = moments.shape
        assert row_count == ROWS and cells == BLOCK and pencils == BLOCK
        groups = pencils // GROUP
        dma = pltpu.SemaphoreType.DMA
        float_of = functools.partial(jax.ShapeDtypeStruct, dtype=jnp.float32)
        halo = (groups, SENT, TILE, BLOCK)
        block = pltpu.VMEM(halo, jnp.float32)
        results = float_of(moments.shape), float_of((VARS, pencils, cells))
        handed = results + (
            float_of(moments.shape), float_of(halo), float_of(halo), float_of((groups, EDGE_STEP, TILE, BLOCK)),
            float_of((COEFS, pencils, BLOCK)), jax.ShapeDtypeStruct((pencils, BLOCK), jnp.int32),
            float_of((VARS, pencils, BLOCK)), float_of((VARS, pencils, BLOCK)),
            jax.ShapeDtypeStruct((BLOCK, BLOCK), jnp.bfloat16), float_of((8, BLOCK)),
        )
        in_vmem = pl.BlockSpec(memory_space=pltpu.VMEM)
        in_hbm = pl.BlockSpec(memory_space=pltpu.HBM)
        ready = pl.pallas_call(
            functools.partial(kernel, chain, cross, relays),
            out_shape=handed,
            in_specs=[in_hbm] * 4,
            out_specs=(in_vmem,) * len(handed),
            scratch_shapes=[
                pltpu.VMEM(flags.shape, jnp.int32),
                pltpu.VMEM((1, pencils), jnp.int32),
                pltpu.VMEM((1, pencils), jnp.float32),
                block, block, block,
                pltpu.VMEM((groups, TILE, BLOCK), jnp.float32),
                pltpu.VMEM((groups // 2, TILE, BLOCK), jnp.float32),
                pltpu.VMEM((groups // 2, TILE, BLOCK), jnp.float32),
                pltpu.VMEM((chain, 8, pencils), jnp.float32),
                pltpu.VMEM((cross, 1, BLOCK), jnp.float32),
                pltpu.VMEM((BLOCK, pencils), jnp.float32),
                pltpu.VMEM((BLOCK, pencils), jnp.float32),
                dma((1,)), dma((groups,)), dma((1,)), dma((groups,)),
                dma((1,)), dma((groups // 2,)), dma((2,)), dma((2,)),
                pltpu.SemaphoreType.REGULAR, pltpu.SemaphoreType.REGULAR, dma((2,)), dma((5,)),
            ],
            compiler_params=pltpu.CompilerParams(
                collective_id=0, has_side_effects=True, vmem_limit_bytes=24 << 20
            ),
        )(*(
            pltpu.with_memory_space_constraint(value, pltpu.HBM)
            for value in (moments, flags, shifts.T, fraction.reshape(1, pencils))
        ))
        return pl.pallas_call(
            deliver,
            out_shape=results,
            in_specs=[in_vmem] * len(handed),
            out_specs=(in_hbm,) * 2,
            scratch_shapes=[
                pltpu.VMEM((ROWS, GROUP, BLOCK), jnp.float32),
                pltpu.VMEM((VARS, GROUP, BLOCK), jnp.float32),
                dma((2,)),
            ],
            compiler_params=pltpu.CompilerParams(vmem_limit_bytes=16 << 20),
        )(*ready)

    in_specs = (P(None, "cross", "chain"), P("cross", "chain"), P("cross", "chain"), P("cross"))
    out_specs = (P(None, "cross", "chain"), P(None, "cross", "chain"))
    return jax.shard_map(shards, mesh=mesh, in_specs=in_specs, out_specs=out_specs, check_vma=False)
```

```python
import functools

import jax
import numpy as np
import jax.numpy as jnp
from jax import lax
from jax.experimental import pallas as pl
from jax.experimental.pallas import tpu as pltpu
from jax.sharding import PartitionSpec as P

VARS = 5
MOMENTS = 4
BLOCK = 128
SHIFT_MAX = 48
ROWS = VARS * MOMENTS
SPAN = ROWS * SHIFT_MAX
FULL, HALF = SPAN // BLOCK, BLOCK // 2
TILE = 8
TILES = 2
GROUP = TILES * TILE
SENT = TILES * FULL + 1
EDGES = -(-ROWS // 8)
EDGE_STEP = TILES * EDGES
LATE = 2
ORDER_RIGHT, ORDER_LEFT = (0, 1, 3, 5, 6, 2, 4), (0, 2, 4, 6, 1, 3, 5)
RELAYED_RIGHT, RELAYED_LEFT = (1, 3, 5, 6), (1, 3, 5)
PAIRS = tuple((k, m) for k in range(1, MOMENTS) for m in range(k, MOMENTS))
COEFS = MOMENTS + 2 * len(PAIRS)
MESH = pl.DeviceIdType.MESH
HIGHEST = lax.Precision.HIGHEST

gauss_nodes = (-0.8611363115940526, -0.3399810435848563, 0.3399810435848563, 0.8611363115940526)
gauss_weights = (0.3478548451374538, 0.6521451548625461, 0.6521451548625461, 0.3478548451374538)


AFTER_FIRST, AFTER_LENGTH = SHIFT_MAX, SHIFT_MAX + 1
BEFORE_FIRST, BEFORE_LENGTH = 0, SHIFT_MAX


def place(row, first):
    chunk, lane = divmod((first + SHIFT_MAX * row) % SPAN, BLOCK)
    return chunk, lane, lane + SHIFT_MAX > BLOCK


def segments(first):
    held = [[] for _ in range(FULL + 1)]
    for row in range(ROWS):
        chunk, lane, splits = place(row, first)
        held[chunk].append((lane, row))
        if splits:
            held[chunk + 1].append((0, row))
    return [sorted(chunk) for chunk in held]


AFTER, BEFORE = segments(AFTER_FIRST), segments(BEFORE_FIRST)
WRAPPED = ROWS - 1


def turn_of(row):
    return (SHIFT_MAX * (row + 1)) % BLOCK


def edge_lane(row):
    return (turn_of(row) + SHIFT_MAX) % BLOCK


def legendre_values(point):
    return [
        jnp.ones_like(point),
        point,
        0.5 * (3.0 * point * point - 1.0),
        0.5 * (5.0 * point * point * point - 3.0 * point),
    ]


def interval_integrals(low_end, high_end, offset):
    half = 0.5 * (high_end - low_end)
    middle = 0.5 * (high_end + low_end)
    entries = [jnp.zeros_like(low_end) for _ in PAIRS]
    for node, weight in zip(gauss_nodes, gauss_weights):
        point = middle + half * node
        target = legendre_values(point)
        source = legendre_values(point + offset)
        scaled = [weight * half * value for value in target]
        for index, (k, m) in enumerate(PAIRS):
            entries[index] = entries[index] + scaled[k] * source[m]
    return entries


def partial_weights(fraction):
    shifted = 2.0 * fraction - 1.0
    square = shifted * shifted
    return [
        fraction,
        fraction * fraction - fraction,
        0.25 * (square * shifted - shifted),
        0.5 * (0.5 * (1.25 * square * square - 1.5 * square) + 0.125),
    ]


def corner_relays(mesh):
    ring = np.moveaxis(mesh.devices, mesh.axis_names.index("chain"), 0).reshape(mesh.shape["chain"], -1)[:, 0]
    if any(getattr(device, "coords", None) is None for device in ring):
        return {}, {}
    spots = [tuple(device.coords) for device in ring]
    rightward, leftward = {}, {}
    if len({spot[0] for spot in spots}) == 2 and len({spot[1] for spot in spots}) == 2:
        for index in range(len(spots) - 1):
            low, high = spots[index], spots[index + 1]
            if low[0] != high[0] and low[1] != high[1]:
                for found, source, target, pick in (
                    (rightward, index, index + 1, max), (leftward, index + 1, index, max)
                ):
                    corner = (spots[source][0], spots[target][1])
                    at = [i for i, spot in enumerate(spots) if spot[:2] == corner]
                    if at:
                        found[source] = (pick(at), target)
    return rightward, leftward


def exact_dot(value, ones):
    high = value.astype(jnp.bfloat16)
    rest = value - high.astype(jnp.float32)
    middle = rest.astype(jnp.bfloat16)
    low = (rest - middle.astype(jnp.float32)).astype(jnp.bfloat16)
    return sum(jnp.dot(part, ones, preferred_element_type=jnp.float32) for part in (low, middle, high))


def finish_group(group, held, remapped, mass, skipped):
    moments, from_left, from_right, edges, coef, shift_of, base, beyond, triangle = held
    lane = lax.broadcasted_iota(jnp.int32, (TILE, BLOCK), 1)
    halos, places_of = [], []
    for tile in range(GROUP // TILE):
        rows = pl.ds(pl.multiple_of(group * GROUP + tile * TILE, TILE), TILE)
        inner = pl.ds(tile * TILE, TILE)
        shift = shift_of[rows, :]
        ahead = shift >= 0
        put = pl.ds(pl.multiple_of(group * GROUP + tile * TILE - skipped, TILE), TILE)
        places_of.append((rows, put, shift, ahead))

        folded = {}
        for name, ref in (("right", from_right), ("left", from_left)):
            value = ref[group, SENT - 1]
            folded[name] = pltpu.roll(value, HALF, 1) if tile else value

        def fetch(name, ref, row, first):
            chunk, start, splits = place(row, first)
            values = [
                ref[group, TILES * index + tile] if index < FULL else folded[name]
                for index in ((chunk, chunk + 1) if splits else (chunk,))
            ]
            return jnp.where(lane >= start, *values) if splits else values[0]

        def halo_row(row):
            right = fetch("right", from_right, row, AFTER_FIRST)
            left = fetch("left", from_left, row, BEFORE_FIRST)
            edge = edges[group, EDGES * tile + row // 8]
            wrapped = row == WRAPPED
            value = left if wrapped else jnp.where(ahead, right, left)
            value = jnp.where(ahead & (lane == edge_lane(row)), edge, value)
            value = pltpu.roll(value, (BLOCK - turn_of(row)) % BLOCK, 1) if turn_of(row) else value
            return jnp.where(ahead & (lane < SHIFT_MAX), right, value) if wrapped else value

        halos.append([halo_row(row) for row in range(ROWS)])

    signed = []
    for (_, _, _, ahead), halo in zip(places_of, halos):
        for var in range(VARS):
            value = halo[MOMENTS * var]
            signed.append(jnp.where(
                ahead,
                jnp.where(lane < AFTER_LENGTH, value, 0.0),
                jnp.where(lane >= BLOCK - BEFORE_LENGTH, -value, 0.0),
            ))
    crossed = exact_dot(jnp.concatenate(signed, axis=0), triangle[...])

    for tile, ((rows, put, shift, ahead), halo) in enumerate(zip(places_of, halos)):
        turn = shift & (BLOCK - 1)
        outside = jnp.where(ahead, lane - turn, turn - 1 - lane) < 0
        outside_next = jnp.where(ahead, lane - turn - 1, turn - lane) < 0
        at = (lane + turn) & (BLOCK - 1)
        weight = [coef[m, rows, :] for m in range(MOMENTS)]
        inside, across = {}, {}
        for index, (k, m) in enumerate(PAIRS):
            inside[k, m] = coef[MOMENTS + index, rows, :]
            across[k, m] = coef[MOMENTS + len(PAIRS) + index, rows, :]

        def settle(value):
            return jnp.take_along_axis(value, at, axis=1, mode="promise_in_bounds")

        for var in range(VARS):
            here, after = [], []
            for order in range(MOMENTS):
                own = moments[MOMENTS * var + order, rows, :]
                other = halo[MOMENTS * var + order]
                here.append(jnp.where(outside, other, own))
                after.append(pltpu.roll(jnp.where(outside_next, other, own), BLOCK - 1, 1))
            filled = weight[0] * here[0]
            filled_after = weight[0] * after[0]
            for m in range(1, MOMENTS):
                filled = filled + weight[m] * here[m]
                filled_after = filled_after + weight[m] * after[m]
            rise = after[0] - here[0]
            remapped[MOMENTS * var, put, :] = settle(here[0] + (filled_after - filled))
            for k in range(1, MOMENTS):
                value = inside[k, k] * here[k] + across[k, k] * after[k]
                for m in range(1, MOMENTS):
                    if m == k:
                        continue
                    pair = (min(k, m), max(k, m))
                    term = inside[pair] * here[m] + across[pair] * after[m]
                    value = value - term if k > m and (k + m) % 2 else value + term
                edge = (2.0 if k % 2 == 0 else -2.0) * (weight[k] * rise)
                remapped[MOMENTS * var + k, put, :] = settle((k + 0.5) * (value + edge))
            index = (tile * VARS + var) * TILE
            start = jnp.where(
                outside, crossed[index : index + TILE] + beyond[var, rows, :], base[var, rows, :]
            )
            mass[var, put, :] = settle(start + filled)


def kernel(
    chain, cross, relays,
    moments_in, flags_in, shifts_in, fraction_in,
    remapped, mass, moments, from_left, from_right, edges, coef, shift_of, base, beyond, triangle, mean_of,
    flags, shifts, fraction,
    to_left, to_right, relay, own_edges, edges_out, edges_in,
    sums, parts, raw, starts,
    left_send, left_recv, right_send, right_recv, relay_send, relay_recv,
    sum_sem, part_sem, ready_sem, open_sem, edge_sem, input_sem,
):
    pencils = moments.shape[1]
    groups = pencils // GROUP
    me = lax.axis_index("chain")
    plane = lax.axis_index("cross")

    first_rows, later_rows = pl.ds(0, GROUP), pl.ds(GROUP, pencils - GROUP)
    inputs = [
        pltpu.make_async_copy(source, target, input_sem.at[index])
        for index, (source, target) in enumerate((
            (flags_in, flags),
            (moments_in.at[:, first_rows, :], moments.at[:, first_rows, :]),
            (moments_in.at[:, later_rows, :], moments.at[:, later_rows, :]),
            (shifts_in, shifts),
            (fraction_in, fraction),
        ))
    ]
    urgent, rest = inputs[:2], inputs[2:]
    for copy in urgent:
        copy.start()

    barrier = pltpu.get_barrier_semaphore()
    for step in range(1, chain):
        peer = lax.rem(me + step, chain)
        pl.semaphore_signal(barrier, inc=1, device_id={"chain": peer}, device_id_type=MESH)
    leads = me == 0

    @pl.when(leads)
    def _():
        for step in range(1, cross):
            peer = lax.rem(plane + step, cross)
            pl.semaphore_signal(barrier, inc=1, device_id={"cross": peer}, device_id_type=MESH)

    for copy in rest:
        copy.start()
    for copy in urgent:
        copy.wait()

    def leftward(group):
        return pltpu.make_async_remote_copy(
            src_ref=to_left.at[group], dst_ref=from_right.at[group],
            send_sem=left_send.at[0], recv_sem=left_recv.at[group],
            device_id={"chain": lax.rem(me + chain - 1, chain)}, device_id_type=MESH,
        )

    def rightward(group):
        return pltpu.make_async_remote_copy(
            src_ref=to_right.at[group], dst_ref=from_left.at[group],
            send_sem=right_send.at[0], recv_sem=right_recv.at[group],
            device_id={"chain": lax.rem(me + 1, chain)}, device_id_type=MESH,
        )

    has_left, has_right = me > 0, me < chain - 1

    sum_copies = [
        pltpu.make_async_remote_copy(
            src_ref=sums.at[me], dst_ref=sums.at[me],
            send_sem=sum_sem.at[0], recv_sem=sum_sem.at[1],
            device_id={"chain": lax.rem(me + step, chain)}, device_id_type=MESH,
        )
        for step in range(1, chain)
    ]
    others = pl.ds(0, chain - 1)
    all_sums = pltpu.make_async_remote_copy(
        src_ref=sums.at[others], dst_ref=sums.at[others],
        send_sem=sum_sem.at[0], recv_sem=sum_sem.at[1],
        device_id={"chain": lax.rem(me + 1, chain)}, device_id_type=MESH,
    )

    source_cell = lax.broadcasted_iota(jnp.int32, (BLOCK, BLOCK), 0)
    target_cell = lax.broadcasted_iota(jnp.int32, (BLOCK, BLOCK), 1)
    before_cell = jnp.where(source_cell < target_cell, 1.0, 0.0)

    def own_sums():
        total = jnp.zeros((pencils, BLOCK), jnp.float32)
        for var in range(VARS):
            pick = jnp.where(target_cell == var, 1.0, 0.0)
            both = jnp.concatenate([before_cell, pick], axis=1).astype(jnp.bfloat16)
            summed = exact_dot(moments[MOMENTS * var], both)
            base[var] = summed[:, :BLOCK]
            total = total + summed[:, BLOCK:]
        sums[me] = jnp.where(
            lax.broadcasted_iota(jnp.int32, (8, BLOCK), 0) == VARS,
            jnp.sum(total, axis=0, keepdims=True), jnp.transpose(total)[:8],
        )

    def send_sums():
        for copy in sum_copies:
            copy.start()

    lane = lax.broadcasted_iota(jnp.int32, (TILE, BLOCK), 1)
    spot = lane & 15

    def pack(group):
        halves = {}
        edge = None
        for tile in range(TILES):
            rows = pl.ds(group * GROUP + tile * TILE, TILE)
            flag = flags[rows, :]
            keep_linear, keep_full = flag <= 1, flag == 0
            rolled = []
            for row in range(ROWS):
                value = moments[row, rows, :]
                order = row % MOMENTS
                if order > 0:
                    value = jnp.where(keep_linear if order == 1 else keep_full, value, 0.0)
                    moments[row, rows, :] = value
                rolled.append(pltpu.roll(value, turn_of(row), 1) if turn_of(row) else value)
            for side, (held, target) in enumerate(((AFTER, to_left), (BEFORE, to_right))):
                for chunk in range(FULL + 1):
                    value = None
                    for start, row in held[chunk]:
                        part = moments[row, rows, :] if row == WRAPPED and side == 0 else rolled[row]
                        value = part if value is None else jnp.where(lane >= start, part, value)
                    if chunk < FULL:
                        target[group, TILES * chunk + tile] = value
                    else:
                        halves[side, tile] = value
            for index in range(EDGES):
                value = None
                for row in range(8 * index, min(8 * index + 8, ROWS)):
                    here = (lane >> 4) == edge_lane(row) // 16
                    value = rolled[row] if value is None else jnp.where(here, rolled[row], value)
                at = EDGES * tile + index
                value = pltpu.roll(value, at, 1) if at else value
                edge = value if edge is None else jnp.where(spot >= at, value, edge)
        for side, target in enumerate((to_left, to_right)):
            target[group, SENT - 1] = jnp.where(
                lane < HALF, halves[side, 0], pltpu.roll(halves[side, 1], HALF, 1)
            )
        own_edges[group] = edge

    edge_copy = pltpu.make_async_remote_copy(
        src_ref=edges_out, dst_ref=edges_in,
        send_sem=edge_sem.at[0], recv_sem=edge_sem.at[1],
        device_id={"chain": lax.rem(me + chain - 1, chain)}, device_id_type=MESH,
    )

    def send_edges():
        for index in range(groups // 2):
            edges_out[index] = jnp.where(
                spot < EDGE_STEP, own_edges[2 * index], pltpu.roll(own_edges[2 * index + 1], EDGE_STEP, 1)
            )

        @pl.when(has_left)
        def _():
            edge_copy.start()

    def receive_edges():
        @pl.when(has_right)
        def _():
            edge_copy.wait_recv()

        for group in range(groups):
            value = edges_in[group // 2]
            for at in range(EDGE_STEP):
                back = EDGE_STEP * (group % 2) + at
                edges[group, at] = pltpu.roll(value, BLOCK - back, 1) if back else value

    right_relays, left_relays = relays

    def to_relay(group, source, send_sem, through):
        return pltpu.make_async_remote_copy(
            src_ref=source.at[group], dst_ref=relay.at[group],
            send_sem=send_sem.at[0], recv_sem=relay_recv.at[group // 2],
            device_id={"chain": jnp.int32(through)}, device_id_type=MESH,
        )

    def onward(group, landing, recv_sem, target):
        return pltpu.make_async_remote_copy(
            src_ref=relay.at[group], dst_ref=landing.at[group],
            send_sem=relay_send.at[0], recv_sem=recv_sem.at[group],
            device_id={"chain": jnp.int32(target)}, device_id_type=MESH,
        )

    def send(group, direct, wanted, among, routes, source, send_sem):
        group = jnp.int32(group)
        relayed = functools.reduce(jnp.logical_or, [group == index for index in among])
        for start, (through, _) in routes.items():
            wanted = wanted & ((me != start) | jnp.logical_not(relayed))

            @pl.when((me == start) & relayed)
            def _():
                to_relay(group, source, send_sem, through).start()

        if direct is rightward:
            for start in routes:
                wanted = wanted & ((me != start) | (group < LATE))

        @pl.when(wanted)
        def _():
            direct(group).start()

    def send_late():
        for start in right_relays:

            @pl.when(me == start)
            def _():
                for group in range(groups):
                    if group >= LATE and group not in RELAYED_RIGHT:
                        rightward(group).start()

    def send_both(group):
        send(group, leftward, has_left, RELAYED_LEFT, left_relays, to_left, left_send)
        send(group, rightward, has_right, RELAYED_RIGHT, right_relays, to_right, right_send)

    def pack_next(group, carry):
        pack(group)
        return carry

    def send_next(group, carry):
        send_both(group)
        return carry

    pack(0)
    soon = (lax.rem(me, 2) == 1) | (me == 0)

    @pl.when(soon)
    def _():
        for copy in rest:
            copy.wait()
        own_sums()
        pack(1)

    pl.semaphore_wait(barrier, jnp.where(leads, chain - 1 + cross - 1, chain - 1))
    send_both(0)

    @pl.when(leads)
    def _():
        for step in range(1, cross):
            peer = lax.rem(plane + step, cross)
            pl.semaphore_signal(ready_sem, inc=1, device_id={"cross": peer}, device_id_type=MESH)

    @pl.when(jnp.logical_not(soon))
    def _():
        for copy in rest:
            copy.wait()
        own_sums()

    send_sums()

    @pl.when(jnp.logical_not(soon))
    def _():
        pack(1)

    for group in range(1, 2):
        send_both(group)
    for group in range(2, groups):
        pack(group)
    send_edges()
    for group in range(2, groups):
        send_both(group)

    part_copies = [
        pltpu.make_async_remote_copy(
            src_ref=parts.at[plane], dst_ref=parts.at[plane],
            send_sem=part_sem.at[0], recv_sem=part_sem.at[1],
            device_id={"cross": lax.rem(plane + step, cross)}, device_id_type=MESH,
        )
        for step in range(1, cross)
    ]

    elsewhere = pl.ds(0, cross - 1)
    all_parts = pltpu.make_async_remote_copy(
        src_ref=parts.at[elsewhere], dst_ref=parts.at[elsewhere],
        send_sem=part_sem.at[0], recv_sem=part_sem.at[1],
        device_id={"cross": lax.rem(plane + 1, cross)}, device_id_type=MESH,
    )

    def open_planes():
        @pl.when(leads)
        def _():
            pl.semaphore_wait(ready_sem, cross - 1)
            for peer in range(1, chain):
                pl.semaphore_signal(open_sem, inc=1, device_id={"chain": jnp.int32(peer)}, device_id_type=MESH)

    def send_parts():
        @pl.when(jnp.logical_not(leads))
        def _():
            pl.semaphore_wait(open_sem, 1)

        for copy in part_copies:
            copy.start()

    def pass_on(index, sides=(0, 1)):
        for side, (among, routes, source, send_sem, landing, recv_sem) in enumerate((
            (RELAYED_RIGHT, right_relays, to_right, right_send, from_left, right_recv),
            (RELAYED_LEFT, left_relays, to_left, left_send, from_right, left_recv),
        )):
            if side not in sides:
                continue
            for through, target in routes.values():
                if index >= len(among):
                    continue
                group = among[index]

                @pl.when(me == through)
                def _():
                    to_relay(group, source, send_sem, through).wait_recv()
                    onward(group, landing, recv_sem, target).start()

    shift_row = shifts[...]

    def reduce_chain():
        starts[...] = jnp.zeros_like(starts)
        all_sums.wait_recv()
        before = jnp.zeros((8, pencils), jnp.float32)
        whole = jnp.zeros((1, BLOCK), jnp.float32)
        for index in range(chain):
            before = before + jnp.where(index < me, sums[index], 0.0)
            whole = whole + sums[index, VARS : VARS + 1]
        parts[plane] = whole
        starts[0:8, :] = before
        starts[8:16, :] = before + jnp.where(shift_row >= 0, sums[me], 0.0)

    def spread_starts():
        turned = jnp.transpose(starts[...])
        for var in range(VARS):
            base[var] = base[var] + turned[:, var : var + 1]
            beyond[var] = jnp.broadcast_to(turned[:, 8 + var : 9 + var], (pencils, BLOCK))

    open_planes()
    pass_on(0)
    pass_on(1)
    reduce_chain()
    for index in range(2, len(RELAYED_RIGHT)):
        pass_on(index, (0,))
    send_parts()
    send_late()

    @pl.when(me == 0)
    def _():
        from_left[...] = jnp.zeros_like(from_left)

    @pl.when(me == chain - 1)
    def _():
        from_right[...] = jnp.zeros_like(from_right)
        edges_in[...] = jnp.zeros_like(edges_in)

    f = fraction[...]
    first = interval_integrals(-1.0 + 0.0 * f, 1.0 - 2.0 * f, 2.0 * f)
    second = interval_integrals(1.0 - 2.0 * f, 1.0 + 0.0 * f, 2.0 * f - 2.0)
    raw[...] = jnp.zeros_like(raw)
    columns = partial_weights(f) + first + second + [shift_row.astype(jnp.float32)]
    for index, value in enumerate(columns):
        raw[index : index + 1, :] = value
    turned = jnp.transpose(raw[...])
    for index in range(COEFS):
        coef[index] = jnp.broadcast_to(turned[:, index : index + 1], (pencils, BLOCK))
    shift_of[...] = jnp.broadcast_to(turned[:, COEFS : COEFS + 1], (pencils, BLOCK)).astype(jnp.int32)

    up_to_edge = jnp.where(source_cell < BLOCK // 2, before_cell, 1.0 - before_cell)
    triangle[...] = up_to_edge.astype(jnp.bfloat16)
    for index in range(2, len(RELAYED_LEFT)):
        pass_on(index, (1,))
    spread_starts()
    receive_edges()


    held = moments, from_left, from_right, edges, coef, shift_of, base, beyond, triangle

    def receive(group):
        @pl.when(has_right)
        def _():
            leftward(group).wait_recv()

        @pl.when(has_left)
        def _():
            rightward(group).wait_recv()

    def turn_to(step):
        group = jnp.int32(step)
        for order, routes in ((ORDER_RIGHT, right_relays), (ORDER_LEFT, left_relays)):
            for _, target in routes.values():
                for index, other in enumerate(order):
                    group = jnp.where((me == target) & (step == index), other, group)
        return group

    def remap(step, carry):
        group = turn_to(step)
        receive(group)
        finish_group(group, held, remapped, mass, 0)
        return carry

    lax.fori_loop(0, groups - 1, remap, 0)

    all_parts.wait_recv()
    grand = parts[0]
    for index in range(1, cross):
        grand = grand + parts[index]
    mean = grand / float(pencils * cross)
    for var in range(VARS):
        mean_of[var : var + 1, :] = jnp.broadcast_to(mean[:, var : var + 1], (1, BLOCK))
    done = pl.ds(0, pencils - GROUP)
    for var in range(VARS):
        mass[var, done, :] = mass[var, done, :] / mean_of[var : var + 1, :]

    all_sums.wait_send()
    all_parts.wait_send()

    for among, routes, landing, recv_sem in (
        (RELAYED_RIGHT, right_relays, from_left, right_recv), (RELAYED_LEFT, left_relays, from_right, left_recv)
    ):
        for through, target in routes.values():

            @pl.when(me == through)
            def _():
                passed = pl.ds(0, len(among))
                pltpu.make_async_remote_copy(
                    src_ref=relay.at[passed], dst_ref=landing.at[passed],
                    send_sem=relay_send.at[0], recv_sem=recv_sem.at[0],
                    device_id={"chain": jnp.int32(target)}, device_id_type=MESH,
                ).wait_send()

    @pl.when(has_left)
    def _():
        edge_copy.wait_send()
        pltpu.make_async_remote_copy(
            src_ref=to_left, dst_ref=from_right,
            send_sem=left_send.at[0], recv_sem=left_recv.at[0],
            device_id={"chain": lax.rem(me + chain - 1, chain)}, device_id_type=MESH,
        ).wait_send()

    @pl.when(has_right)
    def _():
        pltpu.make_async_remote_copy(
            src_ref=to_right, dst_ref=from_left,
            send_sem=right_send.at[0], recv_sem=right_recv.at[0],
            device_id={"chain": lax.rem(me + 1, chain)}, device_id_type=MESH,
        ).wait_send()

    receive(groups - 1)


def deliver(
    remapped, mass, moments, from_left, from_right, edges, coef, shift_of, base, beyond, triangle, mean_of,
    remapped_out, mass_out,
    last_remapped, last_mass, sem,
):
    done = remapped.shape[1] - GROUP
    early, late = pl.ds(0, done), pl.ds(done, GROUP)
    held = moments, from_left, from_right, edges, coef, shift_of, base, beyond, triangle
    copies = [
        pltpu.make_async_copy(source, target, sem.at[index % 2])
        for index, (source, target) in enumerate((
            (remapped.at[:, early, :], remapped_out.at[:, early, :]),
            (mass.at[:, early, :], mass_out.at[:, early, :]),
            (last_remapped, remapped_out.at[:, late, :]),
            (last_mass, mass_out.at[:, late, :]),
        ))
    ]
    for copy in copies[:2]:
        copy.start()
    finish_group(done // GROUP, held, last_remapped, last_mass, done)
    for var in range(VARS):
        last_mass[var] = last_mass[var] / mean_of[var : var + 1, :]
    for copy in copies[2:]:
        copy.start()
    pltpu.make_async_copy(remapped, remapped_out, sem.at[0]).wait()
    pltpu.make_async_copy(mass, mass_out, sem.at[1]).wait()


def solution(mesh):
    chain, cross = mesh.shape["chain"], mesh.shape["cross"]
    relays = corner_relays(mesh)

    def shards(moments, flags, shifts, fraction):
        row_count, pencils, cells = moments.shape
        assert row_count == ROWS and cells == BLOCK and pencils == BLOCK
        groups = pencils // GROUP
        dma = pltpu.SemaphoreType.DMA
        float_of = functools.partial(jax.ShapeDtypeStruct, dtype=jnp.float32)
        halo = (groups, SENT, TILE, BLOCK)
        block = pltpu.VMEM(halo, jnp.float32)
        results = float_of(moments.shape), float_of((VARS, pencils, cells))
        handed = results + (
            float_of(moments.shape), float_of(halo), float_of(halo), float_of((groups, EDGE_STEP, TILE, BLOCK)),
            float_of((COEFS, pencils, BLOCK)), jax.ShapeDtypeStruct((pencils, BLOCK), jnp.int32),
            float_of((VARS, pencils, BLOCK)), float_of((VARS, pencils, BLOCK)),
            jax.ShapeDtypeStruct((BLOCK, BLOCK), jnp.bfloat16), float_of((8, BLOCK)),
        )
        in_vmem = pl.BlockSpec(memory_space=pltpu.VMEM)
        in_hbm = pl.BlockSpec(memory_space=pltpu.HBM)
        ready = pl.pallas_call(
            functools.partial(kernel, chain, cross, relays),
            out_shape=handed,
            in_specs=[in_hbm] * 4,
            out_specs=(in_vmem,) * len(handed),
            scratch_shapes=[
                pltpu.VMEM(flags.shape, jnp.int32),
                pltpu.VMEM((1, pencils), jnp.int32),
                pltpu.VMEM((1, pencils), jnp.float32),
                block, block, block,
                pltpu.VMEM((groups, TILE, BLOCK), jnp.float32),
                pltpu.VMEM((groups // 2, TILE, BLOCK), jnp.float32),
                pltpu.VMEM((groups // 2, TILE, BLOCK), jnp.float32),
                pltpu.VMEM((chain, 8, pencils), jnp.float32),
                pltpu.VMEM((cross, 1, BLOCK), jnp.float32),
                pltpu.VMEM((BLOCK, pencils), jnp.float32),
                pltpu.VMEM((BLOCK, pencils), jnp.float32),
                dma((1,)), dma((groups,)), dma((1,)), dma((groups,)),
                dma((1,)), dma((groups // 2,)), dma((2,)), dma((2,)),
                pltpu.SemaphoreType.REGULAR, pltpu.SemaphoreType.REGULAR, dma((2,)), dma((5,)),
            ],
            compiler_params=pltpu.CompilerParams(
                collective_id=0, has_side_effects=True, vmem_limit_bytes=24 << 20
            ),
        )(*(
            pltpu.with_memory_space_constraint(value, pltpu.HBM)
            for value in (moments, flags, shifts.T, fraction.reshape(1, pencils))
        ))
        return pl.pallas_call(
            deliver,
            out_shape=results,
            in_specs=[in_vmem] * len(handed),
            out_specs=(in_hbm,) * 2,
            scratch_shapes=[
                pltpu.VMEM((ROWS, GROUP, BLOCK), jnp.float32),
                pltpu.VMEM((VARS, GROUP, BLOCK), jnp.float32),
                dma((2,)),
            ],
            compiler_params=pltpu.CompilerParams(vmem_limit_bytes=16 << 20),
        )(*ready)

    in_specs = (P(None, "cross", "chain"), P("cross", "chain"), P("cross", "chain"), P("cross"))
    out_specs = (P(None, "cross", "chain"), P(None, "cross", "chain"))
    return jax.shard_map(shards, mesh=mesh, in_specs=in_specs, out_specs=out_specs, check_vma=False)
```
